256 devices in a mesh: spec: 16 (over z_lo, x, core), photo: 16 (over y, z_hi).
Axes of the slice: x: 4, y: 4, z: 8 (z_hi: 4, z_lo: 2; z = z_hi * 2 + z_lo), core: 2. Of those that a mesh axis runs over, the one named last changes fastest.
Arguments:
- spec_feat: bfloat16 [131072, 64], P(('spec', 'photo')), may hold values from -2.5 to 2.5
- photo_feat: bfloat16 [16, 16384, 64], P('spec', 'photo'), may hold values from -2.5 to 2.5
- spec_mass: bfloat16 [131072], P(('spec', 'photo')), may hold values from 0.25 to 4
- photo_mass: bfloat16 [16, 16384], P('spec', 'photo'), may hold values from 0.25 to 4
- tile_index: int32 [16, 16, 96], P('spec', 'photo'), may hold values from 0 to 2047, as said below
- tile_count: int32 [16, 16], P('spec', 'photo'), may hold values from 4 to 96, as said below
Outputs:
- grad_spec: float32 [131072, 64], P(('spec', 'photo'))
- grad_photo: float32 [16, 16384, 64], P('spec', 'photo')
The draws below stay inside these ranges and needn't reach their ends.
Inputs may be any that keep to these rules, and one draw needn't show every extreme that they name: `tile_index`: the first tile_count[s, p] entries of each list are distinct; over all lists, every tile row of every spectroscopic block and every tile column of every photometric block lies in some live tile. Entries past the count are ignored. `tile_count`: some pair of blocks has exactly 96 live tiles.
All inputs are finite; a program needn't handle non-finite values.
Results may differ from the reference program's by a relative error of at most 0.002.
Values may be sent and summed in bfloat16 or wider, within the bound.
No kernel may reach another device: no remote copies, remote signals or barrier semaphores. Data moves between devices by JAX's collectives and lax.ppermute only.
A program may use at most 64 MiB of HBM per device.

```python
import math
import jax
import jax.numpy as jnp
from jax import lax

F = 64
TILE = 256
SWEEPS = 2
TR = 32
TC = 64
TMAX = 96
SPEC_BLOCKS = 16
PHOTO_BLOCKS = 16
PHOTO_ROWS = 16384
NSPEC = 131072
NPHOTO = 262144
BASE = 4


def tile_pattern(key):
    total = TR * TC
    spec_ids = jnp.arange(SPEC_BLOCKS, dtype=jnp.int32)[:, None, None]
    photo_ids = jnp.arange(PHOTO_BLOCKS, dtype=jnp.int32)[None, :, None]
    offsets = jnp.arange(BASE, dtype=jnp.int32)[None, None, :]
    base_cells = (photo_ids * BASE + offsets) % TR * TC + (spec_ids * BASE + offsets) % TC
    positions = jnp.arange(total, dtype=jnp.int32)
    spread = max(1, 2 ** 30 // total)
    scores = jax.random.randint(jax.random.fold_in(key, 11), (SPEC_BLOCKS, PHOTO_BLOCKS, total), 0, spread, dtype=jnp.int32) * total + positions
    spec_grid = jnp.broadcast_to(spec_ids, base_cells.shape)
    photo_grid = jnp.broadcast_to(photo_ids, base_cells.shape)
    scores = scores.at[spec_grid, photo_grid, base_cells].set(base_cells - total)
    order = jnp.argsort(scores, axis=2, stable=True)
    return order[:, :, :TMAX].astype(jnp.int32)


def draw_tile_index(key, part):
    return tile_pattern(key)


def draw_tile_count(key, part):
    pairs = SPEC_BLOCKS * PHOTO_BLOCKS
    span = TMAX - BASE
    picks = jax.random.randint(jax.random.fold_in(key, 23), (pairs,), 0, span + 1, dtype=jnp.int32)
    counts = BASE + picks * picks // max(span, 1)
    busiest = jax.random.randint(jax.random.fold_in(key, 29), (), 0, pairs, dtype=jnp.int32)
    offset = jax.random.randint(jax.random.fold_in(key, 31), (), 1, pairs, dtype=jnp.int32)
    counts = counts.at[(busiest + offset) % pairs].set(BASE)
    counts = counts.at[busiest].set(TMAX)
    return counts.reshape(SPEC_BLOCKS, PHOTO_BLOCKS).astype(jnp.int32)


def shard_levels(stream_key, extent, shards, low, largest):
    level, own = 1.0, jax.random.fold_in(stream_key, 6)
    for dim, blocks in shards:
        heights = jnp.exp(jax.random.uniform(jax.random.fold_in(own, dim), (blocks,), jnp.float32, low / len(shards), largest / len(shards)))
        level = level * jnp.repeat(heights, extent[dim] // blocks).reshape([-1 if axis == dim else 1 for axis in range(len(extent))])
    return level


def centred(own_key, shape, width, limit, cuts=(), kind=jnp.bfloat16):
    level = shard_levels(own_key, shape, cuts, -0.22, 0.18) if cuts else 1.0
    array = jax.random.normal(own_key, shape, jnp.float32) * width * level
    return jnp.minimum(jnp.maximum(array, -limit), limit).astype(kind)


def setup_inputs(seed: int = 0) -> dict:
    arg_keys = jax.random.split(jax.random.key(seed), 7)
    return {
        "spec_feat": centred(arg_keys[0], (NSPEC, F), 1.0, 2.5, ((0, 256),)),
        "photo_feat": centred(arg_keys[1], (SPEC_BLOCKS, NPHOTO // SPEC_BLOCKS, F), 1.0, 2.5, ((0, 16), (1, 16))),
        "spec_mass": jnp.clip(jnp.exp(math.log(4.0) - 2.7725887 * jax.random.uniform(arg_keys[2], (NSPEC,), jnp.float32) ** shard_levels(arg_keys[2], (NSPEC,), ((0, 256),), -0.2, 0.2)), 0.25, 4.0).astype(jnp.bfloat16),
        "photo_mass": jnp.clip(jnp.exp(math.log(4.0) - 2.7725887 * jax.random.uniform(arg_keys[3], (SPEC_BLOCKS, NPHOTO // SPEC_BLOCKS), jnp.float32) ** shard_levels(arg_keys[3], (SPEC_BLOCKS, NPHOTO // SPEC_BLOCKS), ((0, 16), (1, 16)), -0.2, 0.2)), 0.25, 4.0).astype(jnp.bfloat16),
        "tile_index": draw_tile_index(jax.random.fold_in(arg_keys[6], 71), 0),
        "tile_count": draw_tile_count(jax.random.fold_in(arg_keys[6], 71), 0),
    }


TEMPER = 16.0


def device_tiles(spec_blocks, photo_blocks, spec_squares, photo_squares, tile_index, tile_count, flat):
    spec_id = flat // PHOTO_BLOCKS
    photo_id = flat % PHOTO_BLOCKS
    slots = tile_index[spec_id, photo_id]
    live = jnp.arange(TMAX, dtype=jnp.int32) < tile_count[spec_id, photo_id]
    rows = slots // TC
    columns = slots % TC
    spec_tiles = spec_blocks[spec_id][rows]
    photo_tiles = photo_blocks[photo_id][columns]
    cross = jnp.einsum("gif,gjf->gij", spec_tiles.astype(jnp.float32), photo_tiles.astype(jnp.float32), precision=lax.Precision.HIGHEST)
    dist = spec_squares[spec_id][rows][:, :, None] + photo_squares[photo_id][columns][:, None, :] - 2.0 * cross
    kernel = jnp.where(live[:, None, None], jnp.exp(-dist / TEMPER), jnp.float32(0.0))
    return spec_id, photo_id, rows, columns, spec_tiles, photo_tiles, kernel


def kernel_sums(blocks, row_scale, column_scale):
    def step(carry, flat):
        row_acc, column_acc = carry
        spec_id, photo_id, rows, columns, spec_tiles, photo_tiles, kernel = device_tiles(*blocks, flat)
        row_part = jnp.sum(kernel * column_scale[photo_id][columns][:, None, :], axis=2)
        column_part = jnp.sum(row_scale[spec_id][rows][:, :, None] * kernel, axis=1)
        row_acc = row_acc.at[spec_id, rows].add(row_part)
        column_acc = column_acc.at[photo_id, columns].add(column_part)
        return (row_acc, column_acc), None

    start = (jnp.zeros((SPEC_BLOCKS, TR, TILE), jnp.float32), jnp.zeros((PHOTO_BLOCKS, TC, TILE), jnp.float32))
    result, _ = lax.scan(step, start, jnp.arange(SPEC_BLOCKS * PHOTO_BLOCKS, dtype=jnp.int32))
    return result


def reference(spec_feat, photo_feat, spec_mass, photo_mass, tile_index, tile_count):
    share = PHOTO_ROWS // SPEC_BLOCKS
    spec_blocks = spec_feat.reshape(SPEC_BLOCKS, TR, TILE, F)
    photo_blocks = photo_feat.reshape(SPEC_BLOCKS, PHOTO_BLOCKS, share, F).transpose(1, 0, 2, 3).reshape(PHOTO_BLOCKS, TC, TILE, F)
    spec_weights = spec_mass.astype(jnp.float32).reshape(SPEC_BLOCKS, TR, TILE)
    photo_weights = photo_mass.astype(jnp.float32).reshape(SPEC_BLOCKS, PHOTO_BLOCKS, share).transpose(1, 0, 2).reshape(PHOTO_BLOCKS, TC, TILE)
    spec_squares = jnp.sum(jnp.square(spec_blocks.astype(jnp.float32)), axis=3)
    photo_squares = jnp.sum(jnp.square(photo_blocks.astype(jnp.float32)), axis=3)
    blocks = (spec_blocks, photo_blocks, spec_squares, photo_squares, tile_index, tile_count)
    row_scale = jnp.ones((SPEC_BLOCKS, TR, TILE), jnp.float32)
    column_scale = jnp.ones((PHOTO_BLOCKS, TC, TILE), jnp.float32)
    column_total = column_scale
    for sweep in range(SWEEPS):
        row_total, _ = kernel_sums(blocks, row_scale, column_scale)
        row_scale = spec_weights / row_total
        _, column_total = kernel_sums(blocks, row_scale, column_scale)
        column_scale = photo_weights / column_total
    marginal = column_scale * column_total

    def grad_step(carry, flat):
        row_sum, spec_acc, photo_acc = carry
        spec_id, photo_id, rows, columns, spec_tiles, photo_tiles, kernel = device_tiles(*blocks, flat)
        plan = row_scale[spec_id][rows][:, :, None] * kernel * column_scale[photo_id][columns][:, None, :]
        plan_low = plan.astype(jnp.bfloat16).astype(jnp.float32)
        row_sum = row_sum.at[spec_id, rows].add(jnp.sum(plan, axis=2))
        toward = jnp.einsum("gij,gjf->gif", plan_low, photo_tiles.astype(jnp.float32), precision=lax.Precision.HIGHEST)
        back = jnp.einsum("gij,gif->gjf", plan_low, spec_tiles.astype(jnp.float32), precision=lax.Precision.HIGHEST)
        spec_acc = spec_acc.at[spec_id, rows].add(toward)
        photo_acc = photo_acc.at[photo_id, columns].add(back)
        return (row_sum, spec_acc, photo_acc), None

    start = (jnp.zeros((SPEC_BLOCKS, TR, TILE), jnp.float32), jnp.zeros((SPEC_BLOCKS, TR, TILE, F), jnp.float32), jnp.zeros((PHOTO_BLOCKS, TC, TILE, F), jnp.float32))
    (row_sum, spec_acc, photo_acc), _ = lax.scan(grad_step, start, jnp.arange(SPEC_BLOCKS * PHOTO_BLOCKS, dtype=jnp.int32))
    grad_spec = 2.0 * (row_sum[..., None] * spec_blocks.astype(jnp.float32) - spec_acc)
    grad_photo = 2.0 * (marginal[..., None] * photo_blocks.astype(jnp.float32) - photo_acc)
    grad_photo = grad_photo.reshape(PHOTO_BLOCKS, SPEC_BLOCKS, share, F).transpose(1, 0, 2, 3).reshape(SPEC_BLOCKS, PHOTO_BLOCKS * share, F)
    return grad_spec.reshape(NSPEC, F), grad_photo
```

```python
import math

import jax
import jax.numpy as jnp
from jax import lax
from jax.experimental import pallas as pl
from jax.experimental.pallas import tpu as pltpu
from jax.sharding import PartitionSpec as P

TILE = 256
TR = 32
TC = 64
F = 64
TMAX = 96
SB = 512
PB = 1024
EXT = 72
WROWS = 80
SLOTS = 16
GROUP = 4
TURNS = TMAX // GROUP
SCALE = 0.125 * math.log2(math.e)
f32 = jnp.float32
bf16 = jnp.bfloat16


def photo_perm(fy, fz):
    return [(y * 4 + z, fy(y) * 4 + fz(z)) for y in range(4) for z in range(4)]


def spec_perm(fl, fx, fc):
    return [
        (l * 8 + x * 2 + c, fl(l) * 8 + fx(x) * 2 + fc(c))
        for l in range(2)
        for x in range(4)
        for c in range(2)
    ]


def same(i):
    return i


def flip(i):
    return i ^ 1


def mirror(i):
    return 3 - i


def shift(k):
    return lambda i: (i + k) % 4


def shift_y(a, k):
    return lax.ppermute(a, "photo", photo_perm(shift(k), same))


def shift_z(a, k):
    return lax.ppermute(a, "photo", photo_perm(same, shift(k)))


def shift_x(a, k):
    return lax.ppermute(a, "spec", spec_perm(same, shift(k), same))


def swap_core(a):
    return lax.ppermute(a, "spec", spec_perm(same, same, flip))


def swap_low(a):
    return lax.ppermute(a, "spec", spec_perm(flip, same, same))


def sum_photo(a):
    a = a + lax.ppermute(a, "photo", photo_perm(flip, same))
    a = a + lax.ppermute(a, "photo", photo_perm(mirror, same))
    a = a + lax.ppermute(a, "photo", photo_perm(same, flip))
    return (a, lax.ppermute(a, "photo", photo_perm(same, mirror)))


def sum_spec(a):
    a = a + swap_core(a)
    a = a + swap_low(a)
    a = a + lax.ppermute(a, "spec", spec_perm(same, flip, same))
    return (a, lax.ppermute(a, "spec", spec_perm(same, mirror, same)))


def spec_slot(q, photo_id):
    return (((photo_id >> 2) - (q >> 2)) & 3) * 4 + ((photo_id - q) & 3)


def photo_slot(q, spec_id):
    low = ((spec_id >> 3) - (q >> 3)) & 1
    across = ((spec_id >> 1) - (q >> 1)) & 3
    core = (spec_id - q) & 1
    return core * 8 + across * 2 + low


def entry_of(index_ref, t, last):
    entry = index_ref[jnp.minimum(t, last)]
    return ((entry >> 6) & 31, entry & 63)


def contract_last(a, b):
    return lax.dot_general(a, b, (((1,), (1,)), ((), ())), preferred_element_type=f32)


def high_low_rows(value):
    high = value.astype(bf16).astype(f32)
    sub = lax.broadcasted_iota(jnp.int32, value.shape, 0)
    return jnp.where(sub == 0, high, jnp.where(sub == 1, value - high, 0.0)).astype(bf16)


def high_low(value):
    return high_low_rows(jnp.broadcast_to(value, (16, value.shape[1])))


def turns_of(count_ref):
    return (count_ref[0] + GROUP - 1) // GROUP


def over_tiles(index_ref, count_ref, before, step, after):
    last = count_ref[0] - 1

    def turn(i, carry):
        before(i)
        for k in range(GROUP):
            row, column = entry_of(index_ref, i * GROUP + k, last)
            step(i, k, row, column)
        after(i)
        return carry

    lax.fori_loop(0, turns_of(count_ref), turn, 0)


def start_tiles(count_ref, g_hbm, g_ref, sems):
    def turn(i, carry):
        pltpu.make_async_copy(g_hbm.at[i], g_ref.at[i], sems.at[i]).start()
        return carry

    lax.fori_loop(0, turns_of(count_ref), turn, 0)


def wait_tiles(g_hbm, g_ref, sems):
    return lambda i: pltpu.make_async_copy(g_hbm.at[i], g_ref.at[i], sems.at[i]).wait()


def nothing(i):
    pass


def store_pairs(acc_ref, out_ref):
    for i in range(out_ref.shape[0]):
        both = acc_ref[i]
        out_ref[i : i + 1, :] = both[0:1, :] + both[1:2, :]


def piece_copies(xs, ys, xt_ref, yt_ref, sems):
    copies = [pltpu.make_async_copy(xs[k], xt_ref.at[pl.ds(4 * k, 4)], sems.at[k]) for k in range(4)]
    return copies + [
        pltpu.make_async_copy(ys[k], yt_ref.at[pl.ds(2 * k, 2)], sems.at[4 + k]) for k in range(8)
    ]


def first_kernel(index_ref, count_ref, pos_ref, *refs):
    xs, ys = (refs[0:4], refs[4:12])
    out_ref, m_ref, n_ref, g_hbm = refs[12:16]
    xt_ref, yt_ref, xr_ref, w_ref, acc_ref, g_ref, sems, g_sems = refs[16:]
    copies = piece_copies(xs, ys, xt_ref, yt_ref, sems)
    for copy in copies:
        copy.start()
    acc_ref[...] = jnp.zeros_like(acc_ref)
    for copy in copies:
        copy.wait()

    def turn_slot(s, carry):
        for h in range(2):
            x = xt_ref[s, 0:F, h * TILE : (h + 1) * TILE].astype(f32)
            xr_ref[2 * s + h] = jnp.transpose(x).astype(bf16)
        return carry

    lax.fori_loop(0, SLOTS, turn_slot, 0)

    def weigh(q, carry):
        slot = photo_slot(q, pos_ref[1])
        for k in range(4):
            y = yt_ref[slot, 0:F, k * TILE : (k + 1) * TILE].astype(f32)
            norm = jnp.sum(y * y, axis=0, keepdims=True)
            w_ref[4 * q + k] = high_low(jnp.exp(norm * -0.0625))
        return carry

    lax.fori_loop(0, SLOTS, weigh, 0)
    for row in range(TR):
        slot = spec_slot(row >> 1, pos_ref[0])
        lanes = slice((row & 1) * TILE, (row & 1) * TILE + TILE)
        m_ref[row : row + 1, :] = xt_ref[slot, F:EXT, lanes].astype(f32)[0:1, :]
    for column in range(TC):
        slot = photo_slot(column >> 2, pos_ref[1])
        lanes = slice((column & 3) * TILE, (column & 3) * TILE + TILE)
        n_ref[column : column + 1, :] = yt_ref[slot, F:EXT, lanes].astype(f32)[0:1, :]

    def step(i, k, row, column):
        row_local = spec_slot(row >> 1, pos_ref[0]) * 2 + (row & 1)
        slot = photo_slot(column >> 2, pos_ref[1])
        lane = pl.multiple_of((column & 3) * TILE, TILE)
        y = yt_ref[slot, 0:F, pl.ds(lane, TILE)]
        cross = jnp.dot(xr_ref[row_local], y, preferred_element_type=f32)
        g = jnp.exp2(cross * SCALE)
        g = jnp.where(i * GROUP + k < count_ref[0], g, 0.0).astype(bf16)
        g_ref[i, k] = g
        acc_ref[row] += contract_last(w_ref[column], g)

    def send(i):
        pltpu.make_async_copy(g_ref.at[i], g_hbm.at[i], g_sems.at[i]).start()

    over_tiles(index_ref, count_ref, nothing, step, send)
    store_pairs(acc_ref, out_ref)

    def sent(i, carry):
        pltpu.make_async_copy(g_ref.at[i], g_hbm.at[i], g_sems.at[i]).wait()
        return carry

    lax.fori_loop(0, turns_of(count_ref), sent, 0)


def column_kernel(index_ref, count_ref, ra_ref, rb_ref, m_ref, g_hbm, out_ref, w_ref, acc_ref, g_ref, sems):
    start_tiles(count_ref, g_hbm, g_ref, sems)
    acc_ref[...] = jnp.zeros_like(acc_ref)
    u = m_ref[...] / (ra_ref[...] + rb_ref[...])
    for row in range(TR):
        w_ref[row] = high_low(u[row : row + 1, :])

    def step(i, k, row, column):
        acc_ref[column] += jnp.dot(w_ref[row], g_ref[i, k], preferred_element_type=f32)

    over_tiles(index_ref, count_ref, wait_tiles(g_hbm, g_ref, sems), step, nothing)
    store_pairs(acc_ref, out_ref)


def row_kernel(index_ref, count_ref, ca_ref, cb_ref, n_ref, g_hbm, out_ref, w_ref, acc_ref, g_ref, sems):
    start_tiles(count_ref, g_hbm, g_ref, sems)
    acc_ref[...] = jnp.zeros_like(acc_ref)
    v = n_ref[...] / (ca_ref[...] + cb_ref[...])
    for column in range(TC):
        w_ref[column] = high_low(v[column : column + 1, :])

    def step(i, k, row, column):
        acc_ref[row] += contract_last(w_ref[column], g_ref[i, k])

    over_tiles(index_ref, count_ref, wait_tiles(g_hbm, g_ref, sems), step, nothing)
    store_pairs(acc_ref, out_ref)


def grad_kernel(index_ref, count_ref, pos_ref, ra_ref, rb_ref, ca_ref, cb_ref, m_ref, n_ref, g_hbm, *refs):
    xs, ys = (refs[0:4], refs[4:12])
    spec_outs, photo_outs, share_ref = (refs[12:16], refs[16:18], refs[18])
    xt_ref, yt_ref, u_ref, v_ref, wy_ref, vx_ref, spec_acc, photo_acc = refs[19:27]
    spec_ref, photo_ref, g_ref, sems, g_sems, out_sems = refs[27:]
    copies = piece_copies(xs, ys, xt_ref, yt_ref, sems)
    for copy in copies:
        copy.start()
    start_tiles(count_ref, g_hbm, g_ref, g_sems)
    u_all = m_ref[...] / (ra_ref[...] + rb_ref[...])
    total = ca_ref[...] + cb_ref[...]
    v_all = n_ref[...] / total
    both_all = v_all * total
    for row in range(TR):
        local = spec_slot(row >> 1, pos_ref[0]) * 2 + (row & 1)
        u_ref[local] = jnp.broadcast_to(u_all[row : row + 1, :], (8, TILE))
    for column in range(TC):
        local = photo_slot(column >> 2, pos_ref[1]) * 4 + (column & 3)
        v_ref[local] = jnp.broadcast_to(v_all[column : column + 1, :], (8, TILE))

        @pl.when(local < 4)
        def _():
            share_ref[local] = jnp.broadcast_to(both_all[column : column + 1, :], (8, TILE))

    spec_acc[...] = jnp.zeros_like(spec_acc)
    photo_acc[...] = jnp.zeros_like(photo_acc)
    for copy in copies:
        copy.wait()

    def ready_y(s, carry):
        for k in range(4):
            y = yt_ref[s, 0:F, k * TILE : (k + 1) * TILE].astype(f32)
            v = v_ref[4 * s + k][0:1, :]
            wy_ref[4 * s + k, 0:F, :] = (y * v).astype(bf16)
            wy_ref[4 * s + k, F:WROWS, :] = high_low(v)
        return carry

    def ready_x(s, carry):
        for k in range(2):
            x = xt_ref[s, 0:F, k * TILE : (k + 1) * TILE].astype(f32)
            vx_ref[2 * s + k] = (x * u_ref[2 * s + k][0:1, :]).astype(bf16)
        return carry

    lax.fori_loop(0, SLOTS, ready_y, 0)
    lax.fori_loop(0, SLOTS, ready_x, 0)

    def step(i, k, row, column):
        row_local = spec_slot(row >> 1, pos_ref[0]) * 2 + (row & 1)
        column_local = photo_slot(column >> 2, pos_ref[1]) * 4 + (column & 3)
        g = g_ref[i, k]
        spec_acc[row_local] += contract_last(wy_ref[column_local], g)
        photo_acc[column_local] += jnp.dot(vx_ref[row_local], g, preferred_element_type=f32)

    over_tiles(index_ref, count_ref, wait_tiles(g_hbm, g_ref, g_sems), step, nothing)

    def store_y(s, carry):
        for k in range(4):
            v = v_ref[4 * s + k][0:1, :]
            photo_ref[s, :, k * TILE : (k + 1) * TILE] = (photo_acc[4 * s + k] * v).astype(bf16)
        return carry

    def store_x(s, carry):
        for k in range(2):
            lanes = slice(k * TILE, (k + 1) * TILE)
            u = u_ref[2 * s + k][0:1, :]
            both = spec_acc[2 * s + k]
            spec_ref[s, 0:F, lanes] = (both[0:F, :] * u).astype(bf16)
            total = jnp.broadcast_to((both[F : F + 1, :] + both[F + 1 : F + 2, :]) * u, (8, TILE))
            spec_ref[s, F:EXT, lanes] = high_low_rows(total)
        return carry

    sends = []
    for h in (1, 0):
        lax.fori_loop(8 * h, 8 * h + 8, store_y, 0)
        sends.append(pltpu.make_async_copy(photo_ref.at[pl.ds(8 * h, 8)], photo_outs[h], out_sems.at[4 + h]))
        sends[-1].start()
    for h in range(4):
        lax.fori_loop(4 * h, 4 * h + 4, store_x, 0)
        sends.append(pltpu.make_async_copy(spec_ref.at[pl.ds(4 * h, 4)], spec_outs[h], out_sems.at[h]))
        sends[-1].start()
    for send in sends:
        send.wait()


def relay_kernel(a_ref, b_ref, c_ref, d_ref, own_ref, *send_refs):
    for k in range(4):
        parts = [ref[k].astype(f32) for ref in (a_ref, b_ref, c_ref, d_ref)]
        part = parts[0] + parts[1] + parts[2] + parts[3]
        if k == 0:
            own_ref[...] = part
            continue
        send_refs[k - 1][0:F, :] = part[0:F, :].astype(bf16)
        total = jnp.broadcast_to(part[F : F + 1, :] + part[F + 1 : F + 2, :], (8, SB))
        send_refs[k - 1][F:EXT, :] = high_low_rows(total)


SMEM = pl.BlockSpec(memory_space=pltpu.SMEM)
VMEM = pl.BlockSpec(memory_space=pltpu.VMEM)
ANY = pl.BlockSpec(memory_space=pl.ANY)


def call(kernel, name, in_specs, outs, scratch, *args):
    return pl.pallas_call(
        kernel,
        name=name,
        in_specs=in_specs,
        out_specs=[spec for spec, _, _ in outs],
        out_shape=[jax.ShapeDtypeStruct(s, d) for _, s, d in outs],
        scratch_shapes=scratch,
    )(*args)


def in_vmem(arrays):
    return [pltpu.with_memory_space_constraint(a, pltpu.VMEM) for a in arrays]


def per_device(spec_feat, photo_feat, spec_mass, photo_mass, tile_index, tile_count):
    photo_id = lax.axis_index("photo")
    spec_id = lax.axis_index("spec")
    meta = (
        tile_index.reshape(TMAX),
        tile_count.reshape(1),
        jnp.stack([photo_id, spec_id]).astype(jnp.int32),
    )
    x_own = spec_feat.T
    y_own = photo_feat[0].T
    x_pad = jnp.zeros((EXT - F - 1, SB), bf16)
    y_pad = jnp.zeros((EXT - F - 1, PB), bf16)
    x0 = jnp.concatenate([x_own, spec_mass.reshape(1, SB), x_pad])[None]
    y0 = jnp.concatenate([y_own, photo_mass.reshape(1, PB), y_pad])[None]

    y0 = jnp.concatenate([y0, swap_low(y0)])
    x0 = jnp.concatenate([x0] + [shift_z(x0, k) for k in (1, 2, 3)])
    ys = [y0] + [shift_x(y0, k) for k in (1, 2, 3)]
    xs = [x0] + [shift_y(x0, k) for k in (1, 2, 3)]
    ys = ys + [swap_core(y) for y in ys]

    tiles = pltpu.VMEM((TURNS, GROUP, TILE, TILE), bf16)
    tile_sems = pltpu.SemaphoreType.DMA((TURNS,))
    row_acc = [pltpu.VMEM((TC, 16, TILE), bf16), pltpu.VMEM((TR, 16, TILE), f32)]
    column_acc = [pltpu.VMEM((TR, 16, TILE), bf16), pltpu.VMEM((TC, 16, TILE), f32)]
    blocks = [pltpu.VMEM((SLOTS, EXT, SB), bf16), pltpu.VMEM((SLOTS, EXT, PB), bf16)]
    piece_sems = pltpu.SemaphoreType.DMA((12,))
    r, m, n, g = call(
        first_kernel, "rows0", [SMEM] * 3 + [ANY] * 12,
        [
            (VMEM, (TR, TILE), f32), (VMEM, (TR, TILE), f32), (VMEM, (TC, TILE), f32),
            (ANY, (TURNS, GROUP, TILE, TILE), bf16),
        ],
        blocks + [pltpu.VMEM((TR, TILE, F), bf16)] + row_acc + [tiles, piece_sems, tile_sems],
        *meta, *xs, *ys,
    )
    lists = meta[0:2]

    def columns(name, ra, rb):
        return call(
            column_kernel, name, [SMEM] * 2 + [VMEM] * 3 + [ANY], [(VMEM, (TC, TILE), f32)],
            column_acc + [tiles, tile_sems], *lists, ra, rb, m, g,
        )[0]

    ra, rb = in_vmem(sum_photo(r))
    ca, cb = in_vmem(sum_spec(columns("columns0", ra, rb)))
    (r,) = call(
        row_kernel, "rows1", [SMEM] * 2 + [VMEM] * 3 + [ANY], [(VMEM, (TR, TILE), f32)],
        row_acc + [tiles, tile_sems], *lists, ca, cb, n, g,
    )
    ra, rb = in_vmem(sum_photo(r))
    ca, cb = in_vmem(sum_spec(columns("columns1", ra, rb)))
    *parts, share = call(
        grad_kernel, "grads", [SMEM] * 3 + [VMEM] * 6 + [ANY] * 13,
        [(ANY, (4, EXT, SB), bf16)] * 4 + [(ANY, (8, F, PB), bf16)] * 2 + [(VMEM, (4, 8, TILE), f32)],
        blocks
        + [
            pltpu.VMEM((TR, 8, TILE), f32),
            pltpu.VMEM((TC, 8, TILE), f32),
            pltpu.VMEM((TC, WROWS, TILE), bf16),
            pltpu.VMEM((TR, F, TILE), bf16),
            pltpu.VMEM((TR, WROWS, TILE), f32),
            pltpu.VMEM((TC, F, TILE), f32),
            pltpu.VMEM((SLOTS, EXT, SB), bf16),
            pltpu.VMEM((SLOTS, F, PB), bf16),
            tiles, piece_sems, tile_sems,
            pltpu.SemaphoreType.DMA((6,)),
        ],
        *meta, ra, rb, ca, cb, m, n, g, *xs, *ys,
    )
    share = share[:, 0, :].reshape(1, PB)

    spec_parts, photo_parts = (parts[0:4], parts[4:6])
    far = swap_core(photo_parts[1])
    y_parts = [shift_y(spec_parts[k], -k) for k in (1, 2, 3)]
    photo_sums = [
        photo_parts[0][2 * k : 2 * k + 2].astype(f32) + far[2 * k : 2 * k + 2].astype(f32) for k in range(4)
    ]
    x_parts = [shift_x(photo_sums[k].astype(bf16), -k) for k in (1, 2, 3)]
    y_parts, x_parts = lax.optimization_barrier((y_parts, x_parts))
    spec_sum, *z_parts = call(
        relay_kernel, "relay", [VMEM] * 4,
        [(VMEM, (EXT, SB), f32)] + [(VMEM, (EXT, SB), bf16)] * 3, [],
        spec_parts[0], *in_vmem(y_parts),
    )
    z_parts = [shift_z(part, -k) for k, part in zip((1, 2, 3), z_parts)]
    photo_sum = photo_sums[0]
    for part in x_parts:
        photo_sum = photo_sum + part.astype(f32)
    for part in z_parts:
        spec_sum = spec_sum + part.astype(f32)
    photo_sum = photo_sum[0] + swap_low(photo_sum[1].astype(bf16)).astype(f32)
    row_marginal = spec_sum[F : F + 1] + spec_sum[F + 1 : F + 2]
    grad_spec = 2.0 * (row_marginal * x_own.astype(f32) - spec_sum[0:F])
    grad_photo = 2.0 * (share * y_own.astype(f32) - photo_sum)
    return (grad_spec.T, grad_photo.T[None])


def solution(mesh):
    return jax.shard_map(
        per_device,
        mesh=mesh,
        in_specs=(
            P(("spec", "photo"), None),
            P("spec", "photo", None),
            P(("spec", "photo")),
            P("spec", "photo"),
            P("spec", "photo", None),
            P("spec", "photo"),
        ),
        out_specs=(P(("spec", "photo"), None), P("spec", "photo", None)),
        check_vma=False,
    )
```

```python
import math

import jax
import jax.numpy as jnp
from jax import lax
from jax.experimental import pallas as pl
from jax.experimental.pallas import tpu as pltpu
from jax.sharding import PartitionSpec as P


TILE = 256
TR = 32
TC = 64
F = 64
TMAX = 96
SB = 512
PB = 1024
EXT = 72
WROWS = 80
SLOTS = 16
GROUP = 8
TURNS = TMAX // GROUP
SCALE = 0.125 * math.log2(math.e)
f32 = jnp.float32
bf16 = jnp.bfloat16


def photo_perm(fy, fz):
    return [(y * 4 + z, fy(y) * 4 + fz(z)) for y in range(4) for z in range(4)]


def spec_perm(fl, fx, fc):
    return [
        (l * 8 + x * 2 + c, fl(l) * 8 + fx(x) * 2 + fc(c))
        for l in range(2)
        for x in range(4)
        for c in range(2)
    ]


def same(i):
    return i


def flip(i):
    return i ^ 1


def mirror(i):
    return 3 - i


def shift(k):
    return lambda i: (i + k) % 4


def shift_y(a, k):
    return lax.ppermute(a, "photo", photo_perm(shift(k), same))


def shift_z(a, k):
    return lax.ppermute(a, "photo", photo_perm(same, shift(k)))


def shift_x(a, k):
    return lax.ppermute(a, "spec", spec_perm(same, shift(k), same))


def swap_core(a):
    return lax.ppermute(a, "spec", spec_perm(same, same, flip))


def swap_low(a):
    return lax.ppermute(a, "spec", spec_perm(flip, same, same))


def sum_photo(a):
    parts = [lax.ppermute(a, "photo", photo_perm(fy, fz)) for fy, fz in ((flip, same), (same, flip), (flip, flip))]
    a = (a + parts[0]) + (parts[1] + parts[2])
    a = a + lax.ppermute(a, "photo", photo_perm(mirror, same))
    return (a, lax.ppermute(a, "photo", photo_perm(same, mirror)))


def sum_spec(a):
    a = a + swap_core(a)
    parts = [
        lax.ppermute(a, "spec", spec_perm(fl, fx, same)) for fl, fx in ((flip, same), (same, flip), (flip, flip))
    ]
    a = (a + parts[0]) + (parts[1] + parts[2])
    return (a, lax.ppermute(a, "spec", spec_perm(same, mirror, same)))


def spec_slot(q, photo_id):
    return (((photo_id >> 2) - (q >> 2)) & 3) * 4 + ((photo_id - q) & 3)


def photo_slot(q, spec_id):
    low = ((spec_id >> 3) - (q >> 3)) & 1
    across = ((spec_id >> 1) - (q >> 1)) & 3
    core = (spec_id - q) & 1
    return core * 8 + across * 2 + low


def entry_of(index_ref, t, last):
    entry = index_ref[jnp.minimum(t, last)]
    return ((entry >> 6) & 31, entry & 63)


def live(value, t, count_ref):
    return value * (t < count_ref[0]).astype(value.dtype)


def contract_last(a, b):
    return lax.dot_general(a, b, (((1,), (1,)), ((), ())), preferred_element_type=f32)


def high_low_rows(value):
    high = value.astype(bf16).astype(f32)
    sub = lax.broadcasted_iota(jnp.int32, value.shape, 0)
    return jnp.where(sub == 0, high, jnp.where(sub == 1, value - high, 0.0)).astype(bf16)


def high_low(value):
    return high_low_rows(jnp.broadcast_to(value, (16, value.shape[1])))


def turns_of(count_ref):
    return (count_ref[0] + GROUP - 1) // GROUP


def over_tiles(index_ref, count_ref, before, step, after):
    last = count_ref[0] - 1

    def turn(i, carry):
        before(i)
        for k in range(GROUP):
            row, column = entry_of(index_ref, i * GROUP + k, last)
            step(i, k, i * GROUP + k, row, column)
        after(i)
        return carry

    lax.fori_loop(0, turns_of(count_ref), turn, 0)


def start_tiles(count_ref, g_hbm, g_ref, sems):
    def turn(i, carry):
        pltpu.make_async_copy(g_hbm.at[i], g_ref.at[i], sems.at[i]).start()
        return carry

    lax.fori_loop(0, turns_of(count_ref), turn, 0)


def wait_tiles(g_hbm, g_ref, sems):
    return lambda i: pltpu.make_async_copy(g_hbm.at[i], g_ref.at[i], sems.at[i]).wait()


def nothing(i):
    pass


def store_pairs(acc_ref, out_ref):
    for i in range(out_ref.shape[0]):
        both = acc_ref[i]
        out_ref[i : i + 1, :] = both[0:1, :] + both[1:2, :]


def piece_copies(xs, ys, xt_ref, yt_ref, sems):
    copies = [pltpu.make_async_copy(xs[k], xt_ref.at[pl.ds(4 * k, 4)], sems.at[k]) for k in range(4)]
    return copies + [
        pltpu.make_async_copy(ys[k], yt_ref.at[pl.ds(2 * k, 2)], sems.at[4 + k]) for k in range(8)
    ]


def first_kernel(index_ref, count_ref, pos_ref, *refs):
    xs, ys = (refs[0:4], refs[4:12])
    out_ref, m_ref, n_ref, g_hbm = refs[12:16]
    xt_ref, yt_ref, xr_ref, w_ref, acc_ref, g_ref, sems, g_sems = refs[16:]
    copies = piece_copies(xs, ys, xt_ref, yt_ref, sems)
    for copy in copies:
        copy.start()
    acc_ref[...] = jnp.zeros_like(acc_ref)
    for copy in copies:
        copy.wait()

    def turn_slot(s, carry):
        for h in range(2):
            x = xt_ref[s, 0:F, h * TILE : (h + 1) * TILE].astype(f32)
            xr_ref[2 * s + h] = jnp.transpose(x).astype(bf16)
        return carry

    lax.fori_loop(0, SLOTS, turn_slot, 0)

    def weigh(q, carry):
        slot = photo_slot(q, pos_ref[1])
        for k in range(4):
            y = yt_ref[slot, 0:F, k * TILE : (k + 1) * TILE].astype(f32)
            norm = jnp.sum(y * y, axis=0, keepdims=True)
            w_ref[4 * q + k] = high_low(jnp.exp(norm * -0.0625))
        return carry

    lax.fori_loop(0, SLOTS, weigh, 0)
    for q in range(SLOTS):
        mass = xt_ref[spec_slot(q, pos_ref[0]), F:EXT, :].astype(f32)
        for k in range(2):
            m_ref[2 * q + k : 2 * q + k + 1, :] = mass[0:1, k * TILE : (k + 1) * TILE]
    for q in range(SLOTS):
        mass = yt_ref[photo_slot(q, pos_ref[1]), F:EXT, :].astype(f32)
        for k in range(4):
            n_ref[4 * q + k : 4 * q + k + 1, :] = mass[0:1, k * TILE : (k + 1) * TILE]

    def step(i, k, t, row, column):
        row_local = spec_slot(row >> 1, pos_ref[0]) * 2 + (row & 1)
        slot = photo_slot(column >> 2, pos_ref[1])
        lane = pl.multiple_of((column & 3) * TILE, TILE)
        y = yt_ref[slot, 0:F, pl.ds(lane, TILE)]
        cross = jnp.dot(xr_ref[row_local], y, preferred_element_type=f32)
        g = jnp.exp2(cross * SCALE).astype(bf16)
        g_ref[i, k] = g
        acc_ref[row] += contract_last(live(w_ref[column], t, count_ref), g)

    def send(i):
        pltpu.make_async_copy(g_ref.at[i], g_hbm.at[i], g_sems.at[i]).start()

    over_tiles(index_ref, count_ref, nothing, step, send)
    store_pairs(acc_ref, out_ref)

    def sent(i, carry):
        pltpu.make_async_copy(g_ref.at[i], g_hbm.at[i], g_sems.at[i]).wait()
        return carry

    lax.fori_loop(0, turns_of(count_ref), sent, 0)


def column_kernel(index_ref, count_ref, ra_ref, rb_ref, m_ref, g_hbm, out_ref, w_ref, acc_ref, g_ref, sems):
    start_tiles(count_ref, g_hbm, g_ref, sems)
    acc_ref[...] = jnp.zeros_like(acc_ref)
    u = m_ref[...] / (ra_ref[...] + rb_ref[...])
    for row in range(TR):
        w_ref[row] = high_low(u[row : row + 1, :])

    def step(i, k, t, row, column):
        acc_ref[column] += jnp.dot(live(w_ref[row], t, count_ref), g_ref[i, k], preferred_element_type=f32)

    over_tiles(index_ref, count_ref, wait_tiles(g_hbm, g_ref, sems), step, nothing)
    store_pairs(acc_ref, out_ref)


def row_kernel(index_ref, count_ref, ca_ref, cb_ref, n_ref, g_hbm, out_ref, w_ref, acc_ref, g_ref, sems):
    start_tiles(count_ref, g_hbm, g_ref, sems)
    acc_ref[...] = jnp.zeros_like(acc_ref)
    v = n_ref[...] / (ca_ref[...] + cb_ref[...])
    for column in range(TC):
        w_ref[column] = high_low(v[column : column + 1, :])

    def step(i, k, t, row, column):
        acc_ref[row] += contract_last(live(w_ref[column], t, count_ref), g_ref[i, k])

    over_tiles(index_ref, count_ref, wait_tiles(g_hbm, g_ref, sems), step, nothing)
    store_pairs(acc_ref, out_ref)


def grad_kernel(index_ref, count_ref, pos_ref, ra_ref, rb_ref, ca_ref, cb_ref, m_ref, n_ref, g_hbm, *refs):
    xs, ys = (refs[0:4], refs[4:12])
    spec_outs, photo_outs, share_ref = (refs[12:16], refs[16:18], refs[18])
    xt_ref, yt_ref, u_ref, v_ref, wy_ref, vx_ref, spec_acc, photo_acc = refs[19:27]
    spec_ref, photo_ref, g_ref, sems, g_sems, out_sems = refs[27:]
    copies = piece_copies(xs, ys, xt_ref, yt_ref, sems)
    for copy in copies:
        copy.start()
    start_tiles(count_ref, g_hbm, g_ref, g_sems)
    u_all = m_ref[...] / (ra_ref[...] + rb_ref[...])
    total = ca_ref[...] + cb_ref[...]
    v_all = n_ref[...] / total
    both_all = v_all * total
    for q in range(SLOTS):
        slot = spec_slot(q, pos_ref[0])
        for k in range(2):
            row = 2 * q + k
            u_ref[2 * slot + k] = jnp.broadcast_to(u_all[row : row + 1, :], (8, TILE))
    for q in range(SLOTS):
        slot = photo_slot(q, pos_ref[1])
        for k in range(4):
            column = 4 * q + k
            v_ref[4 * slot + k] = jnp.broadcast_to(v_all[column : column + 1, :], (8, TILE))

        @pl.when(slot == 0)
        def _():
            for k in range(4):
                share_ref[k] = jnp.broadcast_to(both_all[4 * q + k : 4 * q + k + 1, :], (8, TILE))

    spec_acc[...] = jnp.zeros_like(spec_acc)
    photo_acc[...] = jnp.zeros_like(photo_acc)
    for copy in copies:
        copy.wait()

    def ready_y(s, carry):
        for k in range(4):
            y = yt_ref[s, 0:F, k * TILE : (k + 1) * TILE].astype(f32)
            v = v_ref[4 * s + k][0:1, :]
            wy_ref[4 * s + k, 0:F, :] = (y * v).astype(bf16)
            wy_ref[4 * s + k, F:WROWS, :] = high_low(v)
        return carry

    def ready_x(s, carry):
        for k in range(2):
            x = xt_ref[s, 0:F, k * TILE : (k + 1) * TILE].astype(f32)
            vx_ref[2 * s + k] = (x * u_ref[2 * s + k][0:1, :]).astype(bf16)
        return carry

    lax.fori_loop(0, SLOTS, ready_y, 0)
    lax.fori_loop(0, SLOTS, ready_x, 0)

    def step(i, k, t, row, column):
        row_local = spec_slot(row >> 1, pos_ref[0]) * 2 + (row & 1)
        column_local = photo_slot(column >> 2, pos_ref[1]) * 4 + (column & 3)
        g = g_ref[i, k]
        spec_acc[row_local] += contract_last(live(wy_ref[column_local], t, count_ref), g)
        photo_acc[column_local] += jnp.dot(live(vx_ref[row_local], t, count_ref), g, preferred_element_type=f32)

    over_tiles(index_ref, count_ref, wait_tiles(g_hbm, g_ref, g_sems), step, nothing)

    def store_y(s, carry):
        for k in range(4):
            v = v_ref[4 * s + k][0:1, :]
            photo_ref[s, :, k * TILE : (k + 1) * TILE] = (photo_acc[4 * s + k] * v).astype(bf16)
        return carry

    def store_x(s, carry):
        for k in range(2):
            lanes = slice(k * TILE, (k + 1) * TILE)
            u = u_ref[2 * s + k][0:1, :]
            both = spec_acc[2 * s + k]
            spec_ref[s, 0:F, lanes] = (both[0:F, :] * u).astype(bf16)
            total = jnp.broadcast_to((both[F : F + 1, :] + both[F + 1 : F + 2, :]) * u, (8, TILE))
            spec_ref[s, F:EXT, lanes] = high_low_rows(total)
        return carry

    sends = []
    for h in (1, 0):
        lax.fori_loop(8 * h, 8 * h + 8, store_y, 0)
        sends.append(pltpu.make_async_copy(photo_ref.at[pl.ds(8 * h, 8)], photo_outs[h], out_sems.at[4 + h]))
        sends[-1].start()
    for h in range(4):
        lax.fori_loop(4 * h, 4 * h + 4, store_x, 0)
        sends.append(pltpu.make_async_copy(spec_ref.at[pl.ds(4 * h, 4)], spec_outs[h], out_sems.at[h]))
        sends[-1].start()
    for send in sends:
        send.wait()


def relay_kernel(a_ref, b_ref, c_ref, d_ref, own_ref, *send_refs):
    for k in range(4):
        parts = [ref[k].astype(f32) for ref in (a_ref, b_ref, c_ref, d_ref)]
        part = parts[0] + parts[1] + parts[2] + parts[3]
        if k == 0:
            own_ref[...] = part
            continue
        send_refs[k - 1][0:F, :] = part[0:F, :].astype(bf16)
        total = jnp.broadcast_to(part[F : F + 1, :] + part[F + 1 : F + 2, :], (8, SB))
        send_refs[k - 1][F:EXT, :] = high_low_rows(total)


SMEM = pl.BlockSpec(memory_space=pltpu.SMEM)
VMEM = pl.BlockSpec(memory_space=pltpu.VMEM)
ANY = pl.BlockSpec(memory_space=pl.ANY)


def call(kernel, in_specs, outs, scratch, *args):
    return pl.pallas_call(
        kernel,
        in_specs=in_specs,
        out_specs=[spec for spec, _, _ in outs],
        out_shape=[jax.ShapeDtypeStruct(s, d) for _, s, d in outs],
        scratch_shapes=scratch,
    )(*args)


def in_vmem(arrays):
    return [pltpu.with_memory_space_constraint(a, pltpu.VMEM) for a in arrays]


def per_device(spec_feat, photo_feat, spec_mass, photo_mass, tile_index, tile_count):
    photo_id = lax.axis_index("photo")
    spec_id = lax.axis_index("spec")
    meta = (
        tile_index.reshape(TMAX),
        tile_count.reshape(1),
        jnp.stack([photo_id, spec_id]).astype(jnp.int32),
    )
    x_own = spec_feat.T
    y_own = photo_feat[0].T
    x_pad = jnp.zeros((EXT - F - 1, SB), bf16)
    y_pad = jnp.zeros((EXT - F - 1, PB), bf16)
    x0 = jnp.concatenate([x_own, spec_mass.reshape(1, SB), x_pad])[None]
    y0 = jnp.concatenate([y_own, photo_mass.reshape(1, PB), y_pad])[None]

    x_parts = [shift_z(x0, k) for k in (1, 2, 3)]
    y_low = swap_low(y0)
    y0 = jnp.concatenate([y0, y_low])
    x0 = jnp.concatenate([x0] + x_parts)
    ys = [y0] + [shift_x(y0, k) for k in (1, 2, 3)]
    xs = [x0] + [shift_y(x0, k) for k in (1, 2, 3)]
    ys = ys + [swap_core(y) for y in ys]

    tiles = pltpu.VMEM((TURNS, GROUP, TILE, TILE), bf16)
    tile_sems = pltpu.SemaphoreType.DMA((TURNS,))
    row_acc = [pltpu.VMEM((TC, 16, TILE), bf16), pltpu.VMEM((TR, 16, TILE), f32)]
    column_acc = [pltpu.VMEM((TR, 16, TILE), bf16), pltpu.VMEM((TC, 16, TILE), f32)]
    blocks = [pltpu.VMEM((SLOTS, EXT, SB), bf16), pltpu.VMEM((SLOTS, EXT, PB), bf16)]
    piece_sems = pltpu.SemaphoreType.DMA((12,))
    r, m, n, g = call(
        first_kernel, [SMEM] * 3 + [ANY] * 12,
        [
            (VMEM, (TR, TILE), f32), (VMEM, (TR, TILE), f32), (VMEM, (TC, TILE), f32),
            (ANY, (TURNS, GROUP, TILE, TILE), bf16),
        ],
        blocks + [pltpu.VMEM((TR, TILE, F), bf16)] + row_acc + [tiles, piece_sems, tile_sems],
        *meta, *xs, *ys,
    )
    lists = meta[0:2]

    def columns(ra, rb):
        return call(
            column_kernel, [SMEM] * 2 + [VMEM] * 3 + [ANY], [(VMEM, (TC, TILE), f32)],
            column_acc + [tiles, tile_sems], *lists, ra, rb, m, g,
        )[0]

    ra, rb = in_vmem(sum_photo(r))
    ca, cb = in_vmem(sum_spec(columns(ra, rb)))
    (r,) = call(
        row_kernel, [SMEM] * 2 + [VMEM] * 3 + [ANY], [(VMEM, (TR, TILE), f32)],
        row_acc + [tiles, tile_sems], *lists, ca, cb, n, g,
    )
    ra, rb = in_vmem(sum_photo(r))
    ca, cb = in_vmem(sum_spec(columns(ra, rb)))
    *parts, share = call(
        grad_kernel, [SMEM] * 3 + [VMEM] * 6 + [ANY] * 13,
        [(ANY, (4, EXT, SB), bf16)] * 4 + [(ANY, (8, F, PB), bf16)] * 2 + [(VMEM, (4, 8, TILE), f32)],
        blocks
        + [
            pltpu.VMEM((TR, 8, TILE), f32),
            pltpu.VMEM((TC, 8, TILE), f32),
            pltpu.VMEM((TC, WROWS, TILE), bf16),
            pltpu.VMEM((TR, F, TILE), bf16),
            pltpu.VMEM((TR, WROWS, TILE), f32),
            pltpu.VMEM((TC, F, TILE), f32),
            pltpu.VMEM((SLOTS, EXT, SB), bf16),
            pltpu.VMEM((SLOTS, F, PB), bf16),
            tiles, piece_sems, tile_sems,
            pltpu.SemaphoreType.DMA((6,)),
        ],
        *meta, ra, rb, ca, cb, m, n, g, *xs, *ys,
    )
    share = share[:, 0, :].reshape(1, PB)

    spec_parts, photo_parts = (parts[0:4], parts[4:6])
    far = swap_core(photo_parts[1])
    y_parts = [shift_y(spec_parts[k], -k) for k in (1, 2, 3)]
    photo_sums = [
        photo_parts[0][2 * k : 2 * k + 2].astype(f32) + far[2 * k : 2 * k + 2].astype(f32) for k in range(4)
    ]
    x_parts = [shift_x(photo_sums[k].astype(bf16), -k) for k in (1, 2, 3)]
    y_parts, x_parts = lax.optimization_barrier((y_parts, x_parts))
    spec_sum, *z_parts = call(
        relay_kernel, [VMEM] * 4,
        [(VMEM, (EXT, SB), f32)] + [(VMEM, (EXT, SB), bf16)] * 3, [],
        spec_parts[0], *in_vmem(y_parts),
    )
    z_parts = [shift_z(part, -k) for k, part in zip((1, 2, 3), z_parts)]
    photo_sum = photo_sums[0]
    for part in x_parts:
        photo_sum = photo_sum + part.astype(f32)
    for part in z_parts:
        spec_sum = spec_sum + part.astype(f32)
    photo_sum = photo_sum[0] + swap_low(photo_sum[1].astype(bf16)).astype(f32)
    row_marginal = spec_sum[F : F + 1] + spec_sum[F + 1 : F + 2]
    grad_spec = 2.0 * (row_marginal * x_own.astype(f32) - spec_sum[0:F])
    grad_photo = 2.0 * (share * y_own.astype(f32) - photo_sum)
    return (grad_spec.T, grad_photo.T[None])


def solution(mesh):
    return jax.shard_map(
        per_device,
        mesh=mesh,
        in_specs=(
            P(("spec", "photo"), None),
            P("spec", "photo", None),
            P(("spec", "photo")),
            P("spec", "photo"),
            P("spec", "photo", None),
            P("spec", "photo"),
        ),
        out_specs=(P(("spec", "photo"), None), P("spec", "photo", None)),
        check_vma=False,
    )
```

```python
import math

import jax
import jax.numpy as jnp
from jax import lax
from jax.experimental import pallas as pl
from jax.experimental.pallas import tpu as pltpu
from jax.sharding import PartitionSpec as P


TILE = 256
TR = 32
TC = 64
F = 64
TMAX = 96
SB = 512
PB = 1024
EXT = 72
WROWS = 80
SLOTS = 16
GROUP = 8
TURNS = TMAX // GROUP
SCALE = 0.125 * math.log2(math.e)
f32 = jnp.float32
bf16 = jnp.bfloat16


def photo_perm(fy, fz):
    return [(y * 4 + z, fy(y) * 4 + fz(z)) for y in range(4) for z in range(4)]


def spec_perm(fl, fx, fc):
    return [
        (l * 8 + x * 2 + c, fl(l) * 8 + fx(x) * 2 + fc(c))
        for l in range(2)
        for x in range(4)
        for c in range(2)
    ]


def same(i):
    return i


def flip(i):
    return i ^ 1


def mirror(i):
    return 3 - i


def shift(k):
    return lambda i: (i + k) % 4


def shift_y(a, k):
    return lax.ppermute(a, "photo", photo_perm(shift(k), same))


def flip_z(a):
    return lax.ppermute(a, "photo", photo_perm(same, flip))


def mirror_z(a):
    return lax.ppermute(a, "photo", photo_perm(same, mirror))


def shift_x(a, k):
    return lax.ppermute(a, "spec", spec_perm(same, shift(k), same))


def swap_core(a):
    return lax.ppermute(a, "spec", spec_perm(same, same, flip))


def swap_low(a):
    return lax.ppermute(a, "spec", spec_perm(flip, same, same))


def sum_photo(a):
    parts = [lax.ppermute(a, "photo", photo_perm(fy, fz)) for fy, fz in ((flip, same), (same, flip), (flip, flip))]
    a = (a + parts[0]) + (parts[1] + parts[2])
    a = a + lax.ppermute(a, "photo", photo_perm(mirror, same))
    return (a, lax.ppermute(a, "photo", photo_perm(same, mirror)))


def sum_spec(a):
    a = a + swap_core(a)
    parts = [
        lax.ppermute(a, "spec", spec_perm(fl, fx, same)) for fl, fx in ((flip, same), (same, flip), (flip, flip))
    ]
    a = (a + parts[0]) + (parts[1] + parts[2])
    return (a, lax.ppermute(a, "spec", spec_perm(same, mirror, same)))


def spec_slot(q, photo_id):
    across = (photo_id ^ q) & 3
    return (((photo_id >> 2) - (q >> 2)) & 3) * 4 + (across ^ (across >> 1))


def photo_slot(q, spec_id):
    low = ((spec_id >> 3) - (q >> 3)) & 1
    across = ((spec_id >> 1) - (q >> 1)) & 3
    core = (spec_id - q) & 1
    return core * 8 + across * 2 + low


def entry_of(index_ref, t, last):
    entry = index_ref[jnp.minimum(t, last)]
    return ((entry >> 6) & 31, entry & 63)


def live(value, t, count_ref):
    return value * (t < count_ref[0]).astype(value.dtype)


def contract_last(a, b):
    return lax.dot_general(a, b, (((1,), (1,)), ((), ())), preferred_element_type=f32)


def high_low_rows(value):
    high = value.astype(bf16).astype(f32)
    sub = lax.broadcasted_iota(jnp.int32, value.shape, 0)
    return jnp.where(sub == 0, high, jnp.where(sub == 1, value - high, 0.0)).astype(bf16)


def high_low(value):
    return high_low_rows(jnp.broadcast_to(value, (16, value.shape[1])))


def turns_of(count_ref):
    return (count_ref[0] + GROUP - 1) // GROUP


def over_tiles(index_ref, count_ref, before, step, after):
    last = count_ref[0] - 1

    def turn(i, carry):
        before(i)
        for k in range(GROUP):
            row, column = entry_of(index_ref, i * GROUP + k, last)
            step(i, k, i * GROUP + k, row, column)
        after(i)
        return carry

    lax.fori_loop(0, turns_of(count_ref), turn, 0)


def start_tiles(count_ref, g_hbm, g_ref, sems):
    def turn(i, carry):
        pltpu.make_async_copy(g_hbm.at[i], g_ref.at[i], sems.at[i]).start()
        return carry

    lax.fori_loop(0, turns_of(count_ref), turn, 0)


def wait_tiles(g_hbm, g_ref, sems):
    return lambda i: pltpu.make_async_copy(g_hbm.at[i], g_ref.at[i], sems.at[i]).wait()


def nothing(i):
    pass


def store_pairs(acc_ref, out_ref):
    for i in range(out_ref.shape[0]):
        both = acc_ref[i]
        out_ref[i : i + 1, :] = both[0:1, :] + both[1:2, :]


def piece_copies(xs, ys, xt_ref, yt_ref, sems):
    copies = [pltpu.make_async_copy(xs[k], xt_ref.at[pl.ds(4 * k, 4)], sems.at[k]) for k in range(4)]
    return copies + [
        pltpu.make_async_copy(ys[k], yt_ref.at[pl.ds(2 * k, 2)], sems.at[4 + k]) for k in range(8)
    ]


def first_kernel(index_ref, count_ref, pos_ref, *refs):
    xs, ys = (refs[0:4], refs[4:12])
    out_ref, m_ref, n_ref, g_hbm = refs[12:16]
    xt_ref, yt_ref, xr_ref, w_ref, acc_ref, g_ref, sems, g_sems = refs[16:]
    copies = piece_copies(xs, ys, xt_ref, yt_ref, sems)
    for copy in copies:
        copy.start()
    acc_ref[...] = jnp.zeros_like(acc_ref)
    for copy in copies:
        copy.wait()

    def turn_slot(s, carry):
        for h in range(2):
            x = xt_ref[s, 0:F, h * TILE : (h + 1) * TILE].astype(f32)
            xr_ref[2 * s + h] = jnp.transpose(x).astype(bf16)
        return carry

    lax.fori_loop(0, SLOTS, turn_slot, 0)

    def weigh(q, carry):
        slot = photo_slot(q, pos_ref[1])
        for k in range(4):
            y = yt_ref[slot, 0:F, k * TILE : (k + 1) * TILE].astype(f32)
            norm = jnp.sum(y * y, axis=0, keepdims=True)
            w_ref[4 * q + k] = high_low(jnp.exp(norm * -0.0625))
        return carry

    lax.fori_loop(0, SLOTS, weigh, 0)
    for q in range(SLOTS):
        mass = xt_ref[spec_slot(q, pos_ref[0]), F:EXT, :].astype(f32)
        for k in range(2):
            m_ref[2 * q + k : 2 * q + k + 1, :] = mass[0:1, k * TILE : (k + 1) * TILE]
    for q in range(SLOTS):
        mass = yt_ref[photo_slot(q, pos_ref[1]), F:EXT, :].astype(f32)
        for k in range(4):
            n_ref[4 * q + k : 4 * q + k + 1, :] = mass[0:1, k * TILE : (k + 1) * TILE]

    def step(i, k, t, row, column):
        row_local = spec_slot(row >> 1, pos_ref[0]) * 2 + (row & 1)
        slot = photo_slot(column >> 2, pos_ref[1])
        lane = pl.multiple_of((column & 3) * TILE, TILE)
        y = yt_ref[slot, 0:F, pl.ds(lane, TILE)]
        cross = jnp.dot(xr_ref[row_local], y, preferred_element_type=f32)
        g = jnp.exp2(cross * SCALE).astype(bf16)
        g_ref[i, k] = g
        acc_ref[row] += contract_last(live(w_ref[column], t, count_ref), g)

    def send(i):
        pltpu.make_async_copy(g_ref.at[i], g_hbm.at[i], g_sems.at[i]).start()

    over_tiles(index_ref, count_ref, nothing, step, send)
    store_pairs(acc_ref, out_ref)

    def sent(i, carry):
        pltpu.make_async_copy(g_ref.at[i], g_hbm.at[i], g_sems.at[i]).wait()
        return carry

    lax.fori_loop(0, turns_of(count_ref), sent, 0)


def column_kernel(index_ref, count_ref, ra_ref, rb_ref, m_ref, g_hbm, out_ref, w_ref, acc_ref, g_ref, sems):
    start_tiles(count_ref, g_hbm, g_ref, sems)
    acc_ref[...] = jnp.zeros_like(acc_ref)
    u = m_ref[...] / (ra_ref[...] + rb_ref[...])
    for row in range(TR):
        w_ref[row] = high_low(u[row : row + 1, :])

    def step(i, k, t, row, column):
        acc_ref[column] += jnp.dot(live(w_ref[row], t, count_ref), g_ref[i, k], preferred_element_type=f32)

    over_tiles(index_ref, count_ref, wait_tiles(g_hbm, g_ref, sems), step, nothing)
    store_pairs(acc_ref, out_ref)


def row_kernel(index_ref, count_ref, ca_ref, cb_ref, n_ref, g_hbm, out_ref, w_ref, acc_ref, g_ref, sems):
    start_tiles(count_ref, g_hbm, g_ref, sems)
    acc_ref[...] = jnp.zeros_like(acc_ref)
    v = n_ref[...] / (ca_ref[...] + cb_ref[...])
    for column in range(TC):
        w_ref[column] = high_low(v[column : column + 1, :])

    def step(i, k, t, row, column):
        acc_ref[row] += contract_last(live(w_ref[column], t, count_ref), g_ref[i, k])

    over_tiles(index_ref, count_ref, wait_tiles(g_hbm, g_ref, sems), step, nothing)
    store_pairs(acc_ref, out_ref)


def grad_kernel(index_ref, count_ref, pos_ref, ra_ref, rb_ref, ca_ref, cb_ref, m_ref, n_ref, g_hbm, *refs):
    xs, ys = (refs[0:4], refs[4:12])
    spec_outs, photo_outs, share_ref = (refs[12:16], refs[16:18], refs[18])
    xt_ref, yt_ref, u_ref, v_ref, wy_ref, vx_ref, spec_acc, photo_acc = refs[19:27]
    spec_ref, photo_ref, g_ref, sems, g_sems, out_sems = refs[27:]
    copies = piece_copies(xs, ys, xt_ref, yt_ref, sems)
    for copy in copies:
        copy.start()
    start_tiles(count_ref, g_hbm, g_ref, g_sems)
    u_all = m_ref[...] / (ra_ref[...] + rb_ref[...])
    total = ca_ref[...] + cb_ref[...]
    v_all = n_ref[...] / total
    both_all = v_all * total
    for q in range(SLOTS):
        slot = spec_slot(q, pos_ref[0])
        for k in range(2):
            row = 2 * q + k
            u_ref[2 * slot + k] = jnp.broadcast_to(u_all[row : row + 1, :], (8, TILE))
    for q in range(SLOTS):
        slot = photo_slot(q, pos_ref[1])
        for k in range(4):
            column = 4 * q + k
            v_ref[4 * slot + k] = jnp.broadcast_to(v_all[column : column + 1, :], (8, TILE))

        @pl.when(slot == 0)
        def _():
            for k in range(4):
                share_ref[k] = jnp.broadcast_to(both_all[4 * q + k : 4 * q + k + 1, :], (8, TILE))

    spec_acc[...] = jnp.zeros_like(spec_acc)
    photo_acc[...] = jnp.zeros_like(photo_acc)
    for copy in copies:
        copy.wait()

    def ready_y(s, carry):
        for k in range(4):
            y = yt_ref[s, 0:F, k * TILE : (k + 1) * TILE].astype(f32)
            v = v_ref[4 * s + k][0:1, :]
            wy_ref[4 * s + k, 0:F, :] = (y * v).astype(bf16)
            wy_ref[4 * s + k, F:WROWS, :] = high_low(v)
        return carry

    def ready_x(s, carry):
        for k in range(2):
            x = xt_ref[s, 0:F, k * TILE : (k + 1) * TILE].astype(f32)
            vx_ref[2 * s + k] = (x * u_ref[2 * s + k][0:1, :]).astype(bf16)
        return carry

    lax.fori_loop(0, SLOTS, ready_y, 0)
    lax.fori_loop(0, SLOTS, ready_x, 0)

    def step(i, k, t, row, column):
        row_local = spec_slot(row >> 1, pos_ref[0]) * 2 + (row & 1)
        column_local = photo_slot(column >> 2, pos_ref[1]) * 4 + (column & 3)
        g = g_ref[i, k]
        spec_acc[row_local] += contract_last(live(wy_ref[column_local], t, count_ref), g)
        photo_acc[column_local] += jnp.dot(live(vx_ref[row_local], t, count_ref), g, preferred_element_type=f32)

    over_tiles(index_ref, count_ref, wait_tiles(g_hbm, g_ref, g_sems), step, nothing)

    def store_y(s, carry):
        for k in range(4):
            v = v_ref[4 * s + k][0:1, :]
            photo_ref[s, :, k * TILE : (k + 1) * TILE] = (photo_acc[4 * s + k] * v).astype(bf16)
        return carry

    def store_x(s, carry):
        for k in range(2):
            lanes = slice(k * TILE, (k + 1) * TILE)
            u = u_ref[2 * s + k][0:1, :]
            both = spec_acc[2 * s + k]
            spec_ref[s, 0:F, lanes] = (both[0:F, :] * u).astype(bf16)
            total = jnp.broadcast_to((both[F : F + 1, :] + both[F + 1 : F + 2, :]) * u, (8, TILE))
            spec_ref[s, F:EXT, lanes] = high_low_rows(total)
        return carry

    sends = []
    for h in (1, 0):
        lax.fori_loop(8 * h, 8 * h + 8, store_y, 0)
        sends.append(pltpu.make_async_copy(photo_ref.at[pl.ds(8 * h, 8)], photo_outs[h], out_sems.at[4 + h]))
        sends[-1].start()
    for h in range(4):
        lax.fori_loop(4 * h, 4 * h + 4, store_x, 0)
        sends.append(pltpu.make_async_copy(spec_ref.at[pl.ds(4 * h, 4)], spec_outs[h], out_sems.at[h]))
        sends[-1].start()
    for send in sends:
        send.wait()


def relay_kernel(*refs):
    *in_refs, own_ref, send_ref = refs
    half = own_ref.shape[0]
    for k in range(2 * half):
        part = in_refs[0][k].astype(f32)
        for ref in in_refs[1:]:
            part = part + ref[k].astype(f32)
        if k < half:
            own_ref[k] = part
            continue
        send_ref[k - half, 0:F, :] = part[0:F, :].astype(bf16)
        total = jnp.broadcast_to(part[F : F + 1, :] + part[F + 1 : F + 2, :], (8, SB))
        send_ref[k - half, F:EXT, :] = high_low_rows(total)


SMEM = pl.BlockSpec(memory_space=pltpu.SMEM)
VMEM = pl.BlockSpec(memory_space=pltpu.VMEM)
ANY = pl.BlockSpec(memory_space=pl.ANY)


def call(kernel, in_specs, outs, scratch, *args):
    return pl.pallas_call(
        kernel,
        in_specs=in_specs,
        out_specs=[spec for spec, _, _ in outs],
        out_shape=[jax.ShapeDtypeStruct(s, d) for _, s, d in outs],
        scratch_shapes=scratch,
    )(*args)


def in_vmem(arrays):
    return [pltpu.with_memory_space_constraint(a, pltpu.VMEM) for a in arrays]


def per_device(spec_feat, photo_feat, spec_mass, photo_mass, tile_index, tile_count):
    photo_id = lax.axis_index("photo")
    spec_id = lax.axis_index("spec")
    meta = (
        tile_index.reshape(TMAX),
        tile_count.reshape(1),
        jnp.stack([photo_id, spec_id]).astype(jnp.int32),
    )
    x_own = spec_feat.T
    y_own = photo_feat[0].T
    x_pad = jnp.zeros((EXT - F - 1, SB), bf16)
    y_pad = jnp.zeros((EXT - F - 1, PB), bf16)
    x0 = jnp.concatenate([x_own, spec_mass.reshape(1, SB), x_pad])[None]
    y0 = jnp.concatenate([y_own, photo_mass.reshape(1, PB), y_pad])[None]

    x_flip = flip_z(x0)
    y_low = swap_low(y0)
    x0 = jnp.concatenate([x0, x_flip])
    x_mirror = mirror_z(x0)
    y0 = jnp.concatenate([y0, y_low])
    x0 = jnp.concatenate([x0, x_mirror])
    ys = [y0] + [shift_x(y0, k) for k in (1, 2, 3)]
    xs = [x0] + [shift_y(x0, k) for k in (1, 2, 3)]
    ys = ys + [swap_core(y) for y in ys]

    tiles = pltpu.VMEM((TURNS, GROUP, TILE, TILE), bf16)
    tile_sems = pltpu.SemaphoreType.DMA((TURNS,))
    row_acc = [pltpu.VMEM((TC, 16, TILE), bf16), pltpu.VMEM((TR, 16, TILE), f32)]
    column_acc = [pltpu.VMEM((TR, 16, TILE), bf16), pltpu.VMEM((TC, 16, TILE), f32)]
    blocks = [pltpu.VMEM((SLOTS, EXT, SB), bf16), pltpu.VMEM((SLOTS, EXT, PB), bf16)]
    piece_sems = pltpu.SemaphoreType.DMA((12,))
    r, m, n, g = call(
        first_kernel, [SMEM] * 3 + [ANY] * 12,
        [
            (VMEM, (TR, TILE), f32), (VMEM, (TR, TILE), f32), (VMEM, (TC, TILE), f32),
            (ANY, (TURNS, GROUP, TILE, TILE), bf16),
        ],
        blocks + [pltpu.VMEM((TR, TILE, F), bf16)] + row_acc + [tiles, piece_sems, tile_sems],
        *meta, *xs, *ys,
    )
    lists = meta[0:2]

    def columns(ra, rb):
        return call(
            column_kernel, [SMEM] * 2 + [VMEM] * 3 + [ANY], [(VMEM, (TC, TILE), f32)],
            column_acc + [tiles, tile_sems], *lists, ra, rb, m, g,
        )[0]

    ra, rb = in_vmem(sum_photo(r))
    ca, cb = in_vmem(sum_spec(columns(ra, rb)))
    (r,) = call(
        row_kernel, [SMEM] * 2 + [VMEM] * 3 + [ANY], [(VMEM, (TR, TILE), f32)],
        row_acc + [tiles, tile_sems], *lists, ca, cb, n, g,
    )
    ra, rb = in_vmem(sum_photo(r))
    ca, cb = in_vmem(sum_spec(columns(ra, rb)))
    *parts, share = call(
        grad_kernel, [SMEM] * 3 + [VMEM] * 6 + [ANY] * 13,
        [(ANY, (4, EXT, SB), bf16)] * 4 + [(ANY, (8, F, PB), bf16)] * 2 + [(VMEM, (4, 8, TILE), f32)],
        blocks
        + [
            pltpu.VMEM((TR, 8, TILE), f32),
            pltpu.VMEM((TC, 8, TILE), f32),
            pltpu.VMEM((TC, WROWS, TILE), bf16),
            pltpu.VMEM((TR, F, TILE), bf16),
            pltpu.VMEM((TR, WROWS, TILE), f32),
            pltpu.VMEM((TC, F, TILE), f32),
            pltpu.VMEM((SLOTS, EXT, SB), bf16),
            pltpu.VMEM((SLOTS, F, PB), bf16),
            tiles, piece_sems, tile_sems,
            pltpu.SemaphoreType.DMA((6,)),
        ],
        *meta, ra, rb, ca, cb, m, n, g, *xs, *ys,
    )
    share = share[:, 0, :].reshape(1, PB)

    spec_parts, photo_parts = (parts[0:4], parts[4:6])
    far = swap_core(photo_parts[1])
    y_parts = [shift_y(spec_parts[k], -k) for k in (1, 2, 3)]
    photo_sums = [photo_parts[0][2 * k : 2 * k + 2].astype(f32) + far[2 * k : 2 * k + 2].astype(f32) for k in range(4)]
    x_parts = [total.astype(bf16) for total in photo_sums[1:]]
    x_parts = [shift_x(part, -k) for k, part in zip((1, 2, 3), x_parts)]

    def relay(half, first, rest):
        return call(
            relay_kernel, [VMEM] * (1 + len(rest)),
            [(VMEM, (half, EXT, SB), f32), (VMEM, (half, EXT, SB), bf16)], [], first, *in_vmem(rest),
        )

    spec_sum, send = relay(2, spec_parts[0], y_parts)
    mirrored = mirror_z(send)
    spec_sum, send = relay(1, spec_sum, [mirrored])
    flipped = flip_z(send)
    spec_sum = spec_sum[0] + flipped[0].astype(f32)
    photo_sum = photo_sums[0]
    for part in x_parts:
        photo_sum = photo_sum + part.astype(f32)
    photo_send = photo_sum[1].astype(bf16)
    lowered = swap_low(photo_send)
    photo_sum = photo_sum[0] + lowered.astype(f32)
    row_marginal = spec_sum[F : F + 1] + spec_sum[F + 1 : F + 2]
    grad_spec = 2.0 * (row_marginal * x_own.astype(f32) - spec_sum[0:F])
    grad_photo = 2.0 * (share * y_own.astype(f32) - photo_sum)
    return (grad_spec.T, grad_photo.T[None])


def solution(mesh):
    return jax.shard_map(
        per_device,
        mesh=mesh,
        in_specs=(
            P(("spec", "photo"), None),
            P("spec", "photo", None),
            P(("spec", "photo")),
            P("spec", "photo"),
            P("spec", "photo", None),
            P("spec", "photo"),
        ),
        out_specs=(P(("spec", "photo"), None), P("spec", "photo", None)),
        check_vma=False,
    )
```

```python
import math

import jax
import jax.numpy as jnp
from jax import lax
from jax.experimental import pallas as pl
from jax.experimental.pallas import tpu as pltpu
from jax.sharding import PartitionSpec as P


TILE = 256
TR = 32
TC = 64
F = 64
TMAX = 96
SB = 512
PB = 1024
EXT = 72
WROWS = 80
SLOTS = 16
GROUP = 8
TURNS = TMAX // GROUP
SCALE = 0.125 * math.log2(math.e)
f32 = jnp.float32
bf16 = jnp.bfloat16


def photo_perm(fy, fz):
    return [(y * 4 + z, fy(y) * 4 + fz(z)) for y in range(4) for z in range(4)]


def spec_perm(fl, fx, fc):
    return [
        (l * 8 + x * 2 + c, fl(l) * 8 + fx(x) * 2 + fc(c))
        for l in range(2)
        for x in range(4)
        for c in range(2)
    ]


def same(i):
    return i


def flip(i):
    return i ^ 1


def mirror(i):
    return 3 - i


def shift(k):
    return lambda i: (i + k) % 4


def shift_y(a, k):
    return lax.ppermute(a, "photo", photo_perm(shift(k), same))


def shift_z(a, k):
    return lax.ppermute(a, "photo", photo_perm(same, shift(k)))


def flip_z(a):
    return lax.ppermute(a, "photo", photo_perm(same, flip))


def across_z(a):
    return lax.ppermute(a, "photo", photo_perm(same, lambda i: i ^ 2))


def mirror_z(a):
    return lax.ppermute(a, "photo", photo_perm(same, mirror))


def shift_x(a, k):
    return lax.ppermute(a, "spec", spec_perm(same, shift(k), same))


def swap_core(a):
    return lax.ppermute(a, "spec", spec_perm(same, same, flip))


def swap_low(a):
    return lax.ppermute(a, "spec", spec_perm(flip, same, same))


def sum_photo(a):
    parts = [shift_y(a, k) for k in (1, 2, 3)]
    a = (a + parts[0]) + (parts[1] + parts[2])
    return [a] + [shift_z(a, k) for k in (1, 2, 3)]


def sum_spec(a):
    a = a + swap_core(a)
    parts = [
        lax.ppermute(a, "spec", spec_perm(fl, fx, same)) for fl, fx in ((flip, same), (same, flip), (flip, flip))
    ]
    a = (a + parts[0]) + (parts[1] + parts[2])
    return [a, lax.ppermute(a, "spec", spec_perm(same, mirror, same))]


def spec_slot(q, photo_id):
    across = (photo_id ^ q) & 3
    return (((photo_id >> 2) - (q >> 2)) & 3) * 4 + (across ^ (across >> 1))


def photo_slot(q, spec_id):
    low = ((spec_id >> 3) - (q >> 3)) & 1
    across = ((spec_id >> 1) - (q >> 1)) & 3
    core = (spec_id - q) & 1
    return core * 8 + across * 2 + low


def entry_of(index_ref, t, last):
    entry = index_ref[jnp.minimum(t, last)]
    return ((entry >> 6) & 31, entry & 63)


def live(value, t, count_ref):
    return value * (t < count_ref[0]).astype(value.dtype)


def contract_last(a, b):
    return lax.dot_general(a, b, (((1,), (1,)), ((), ())), preferred_element_type=f32)


def high_low_rows(value):
    high = value.astype(bf16).astype(f32)
    sub = lax.broadcasted_iota(jnp.int32, value.shape, 0)
    return jnp.where(sub == 0, high, jnp.where(sub == 1, value - high, 0.0)).astype(bf16)


def high_low(value):
    return high_low_rows(jnp.broadcast_to(value, (16, value.shape[1])))


def turns_of(count_ref):
    return (count_ref[0] + GROUP - 1) // GROUP


def over_tiles(index_ref, count_ref, before, step, after):
    last = count_ref[0] - 1

    def turn(i, carry):
        before(i)
        for k in range(GROUP):
            row, column = entry_of(index_ref, i * GROUP + k, last)
            step(i, k, i * GROUP + k, row, column)
        after(i)
        return carry

    lax.fori_loop(0, turns_of(count_ref), turn, 0)


def start_tiles(count_ref, g_hbm, g_ref, sems):
    def turn(i, carry):
        pltpu.make_async_copy(g_hbm.at[i], g_ref.at[i], sems.at[i]).start()
        return carry

    lax.fori_loop(0, turns_of(count_ref), turn, 0)


def wait_tiles(g_hbm, g_ref, sems):
    return lambda i: pltpu.make_async_copy(g_hbm.at[i], g_ref.at[i], sems.at[i]).wait()


def nothing(i):
    pass


def store_pairs(acc_ref, out_ref):
    for i in range(out_ref.shape[0]):
        both = acc_ref[i]
        out_ref[i : i + 1, :] = both[0:1, :] + both[1:2, :]


def piece_copies(xs, ys, xt_ref, yt_ref, sems):
    copies = [pltpu.make_async_copy(xs[k], xt_ref.at[pl.ds(4 * k, 4)], sems.at[k]) for k in range(4)]
    return copies + [
        pltpu.make_async_copy(ys[k], yt_ref.at[pl.ds(2 * k, 2)], sems.at[4 + k]) for k in range(8)
    ]


def column_start_kernel(pos_ref, *refs):
    ys = refs[0:8]
    n_ref, b_ref, yt_ref, sems = refs[8:]
    copies = [pltpu.make_async_copy(ys[k], yt_ref.at[pl.ds(2 * k, 2)], sems.at[k]) for k in range(8)]
    for copy in copies:
        copy.start()
    for copy in copies:
        copy.wait()
    for q in range(SLOTS):
        slot = photo_slot(q, pos_ref[0])
        mass = yt_ref[slot, F:EXT, :].astype(f32)
        y = yt_ref[slot, 0:F, :].astype(f32)
        weight = jnp.exp(jnp.sum(y * y, axis=0, keepdims=True) * -0.0625)
        for k in range(4):
            lanes = slice(k * TILE, (k + 1) * TILE)
            n_ref[4 * q + k : 4 * q + k + 1, :] = mass[0:1, lanes]
            b_ref[4 * q + k : 4 * q + k + 1, :] = weight[:, lanes]


def first_kernel(index_ref, count_ref, pos_ref, *refs):
    xs, ys, b_ref = (refs[0:4], refs[4:12], refs[12])
    out_ref, m_ref, g_hbm = refs[13:16]
    xt_ref, yt_ref, xr_ref, w_ref, acc_ref, g_ref, sems, g_sems = refs[16:]
    copies = piece_copies(xs, ys, xt_ref, yt_ref, sems)
    for copy in copies:
        copy.start()
    acc_ref[...] = jnp.zeros_like(acc_ref)
    for column in range(TC):
        w_ref[column] = high_low(b_ref[column : column + 1, :])
    for copy in copies:
        copy.wait()

    def turn_slot(s, carry):
        for h in range(2):
            x = xt_ref[s, 0:F, h * TILE : (h + 1) * TILE].astype(f32)
            xr_ref[2 * s + h] = jnp.transpose(x).astype(bf16)
        return carry

    lax.fori_loop(0, SLOTS, turn_slot, 0)

    for q in range(SLOTS):
        mass = xt_ref[spec_slot(q, pos_ref[0]), F:EXT, :].astype(f32)
        for k in range(2):
            m_ref[2 * q + k : 2 * q + k + 1, :] = mass[0:1, k * TILE : (k + 1) * TILE]

    def step(i, k, t, row, column):
        row_local = spec_slot(row >> 1, pos_ref[0]) * 2 + (row & 1)
        slot = photo_slot(column >> 2, pos_ref[1])
        lane = pl.multiple_of((column & 3) * TILE, TILE)
        y = yt_ref[slot, 0:F, pl.ds(lane, TILE)]
        cross = jnp.dot(xr_ref[row_local], y, preferred_element_type=f32)
        g = jnp.exp2(cross * SCALE).astype(bf16)
        g_ref[i, k] = g
        acc_ref[row] += contract_last(live(w_ref[column], t, count_ref), g)

    def send(i):
        pltpu.make_async_copy(g_ref.at[i], g_hbm.at[i], g_sems.at[i]).start()

    over_tiles(index_ref, count_ref, nothing, step, send)
    store_pairs(acc_ref, out_ref)

    def sent(i, carry):
        pltpu.make_async_copy(g_ref.at[i], g_hbm.at[i], g_sems.at[i]).wait()
        return carry

    lax.fori_loop(0, turns_of(count_ref), sent, 0)


def sum_of(refs):
    total = refs[0][...]
    for ref in refs[1:]:
        total = total + ref[...]
    return total


def column_kernel(index_ref, count_ref, *refs):
    r_refs = refs[0:4]
    m_ref, g_hbm, out_ref, w_ref, acc_ref, g_ref, sems = refs[4:]
    start_tiles(count_ref, g_hbm, g_ref, sems)
    acc_ref[...] = jnp.zeros_like(acc_ref)
    u = m_ref[...] / sum_of(r_refs)
    for row in range(TR):
        w_ref[row] = high_low(u[row : row + 1, :])

    def step(i, k, t, row, column):
        acc_ref[column] += jnp.dot(live(w_ref[row], t, count_ref), g_ref[i, k], preferred_element_type=f32)

    over_tiles(index_ref, count_ref, wait_tiles(g_hbm, g_ref, sems), step, nothing)
    store_pairs(acc_ref, out_ref)


def row_kernel(index_ref, count_ref, ca_ref, cb_ref, n_ref, g_hbm, out_ref, w_ref, acc_ref, g_ref, sems):
    start_tiles(count_ref, g_hbm, g_ref, sems)
    acc_ref[...] = jnp.zeros_like(acc_ref)
    v = n_ref[...] / (ca_ref[...] + cb_ref[...])
    for column in range(TC):
        w_ref[column] = high_low(v[column : column + 1, :])

    def step(i, k, t, row, column):
        acc_ref[row] += contract_last(live(w_ref[column], t, count_ref), g_ref[i, k])

    over_tiles(index_ref, count_ref, wait_tiles(g_hbm, g_ref, sems), step, nothing)
    store_pairs(acc_ref, out_ref)


def grad_kernel(index_ref, count_ref, pos_ref, *refs):
    r_refs, c_refs, m_ref, n_ref, g_hbm = (refs[0:4], refs[4:6], *refs[6:9])
    refs = refs[9:]
    xs, ys = (refs[0:4], refs[4:12])
    spec_outs, photo_outs, share_ref = (refs[12:16], refs[16:18], refs[18])
    xt_ref, yt_ref, u_ref, v_ref, wy_ref, vx_ref, spec_acc, photo_acc = refs[19:27]
    spec_ref, photo_ref, g_ref, sems, g_sems, out_sems = refs[27:]
    copies = piece_copies(xs, ys, xt_ref, yt_ref, sems)
    for copy in copies:
        copy.start()
    start_tiles(count_ref, g_hbm, g_ref, g_sems)
    u_all = m_ref[...] / sum_of(r_refs)
    total = sum_of(c_refs)
    v_all = n_ref[...] / total
    both_all = v_all * total
    for q in range(SLOTS):
        slot = spec_slot(q, pos_ref[0])
        for k in range(2):
            row = 2 * q + k
            u_ref[2 * slot + k] = jnp.broadcast_to(u_all[row : row + 1, :], (8, TILE))
    for q in range(SLOTS):
        slot = photo_slot(q, pos_ref[1])
        for k in range(4):
            column = 4 * q + k
            v_ref[4 * slot + k] = jnp.broadcast_to(v_all[column : column + 1, :], (8, TILE))

        @pl.when(slot == 0)
        def _():
            for k in range(4):
                share_ref[k] = jnp.broadcast_to(both_all[4 * q + k : 4 * q + k + 1, :], (8, TILE))

    spec_acc[...] = jnp.zeros_like(spec_acc)
    photo_acc[...] = jnp.zeros_like(photo_acc)
    for copy in copies:
        copy.wait()

    def ready_y(s, carry):
        for k in range(4):
            y = yt_ref[s, 0:F, k * TILE : (k + 1) * TILE].astype(f32)
            v = v_ref[4 * s + k][0:1, :]
            wy_ref[4 * s + k, 0:F, :] = (y * v).astype(bf16)
            wy_ref[4 * s + k, F:WROWS, :] = high_low(v)
        return carry

    def ready_x(s, carry):
        for k in range(2):
            x = xt_ref[s, 0:F, k * TILE : (k + 1) * TILE].astype(f32)
            vx_ref[2 * s + k] = (x * u_ref[2 * s + k][0:1, :]).astype(bf16)
        return carry

    lax.fori_loop(0, SLOTS, ready_y, 0)
    lax.fori_loop(0, SLOTS, ready_x, 0)

    def step(i, k, t, row, column):
        row_local = spec_slot(row >> 1, pos_ref[0]) * 2 + (row & 1)
        column_local = photo_slot(column >> 2, pos_ref[1]) * 4 + (column & 3)
        g = g_ref[i, k]
        spec_acc[row_local] += contract_last(live(wy_ref[column_local], t, count_ref), g)
        photo_acc[column_local] += jnp.dot(live(vx_ref[row_local], t, count_ref), g, preferred_element_type=f32)

    over_tiles(index_ref, count_ref, wait_tiles(g_hbm, g_ref, g_sems), step, nothing)

    def store_y(s, carry):
        for k in range(4):
            v = v_ref[4 * s + k][0:1, :]
            photo_ref[s, :, k * TILE : (k + 1) * TILE] = (photo_acc[4 * s + k] * v).astype(bf16)
        return carry

    def store_x(s, carry):
        for k in range(2):
            lanes = slice(k * TILE, (k + 1) * TILE)
            u = u_ref[2 * s + k][0:1, :]
            both = spec_acc[2 * s + k]
            spec_ref[s, 0:F, lanes] = (both[0:F, :] * u).astype(bf16)
            total = jnp.broadcast_to((both[F : F + 1, :] + both[F + 1 : F + 2, :]) * u, (8, TILE))
            spec_ref[s, F:EXT, lanes] = high_low_rows(total)
        return carry

    sends = []
    for h in (1, 0):
        lax.fori_loop(8 * h, 8 * h + 8, store_y, 0)
        sends.append(pltpu.make_async_copy(photo_ref.at[pl.ds(8 * h, 8)], photo_outs[h], out_sems.at[4 + h]))
        sends[-1].start()
    for h in range(4):
        lax.fori_loop(4 * h, 4 * h + 4, store_x, 0)
        sends.append(pltpu.make_async_copy(spec_ref.at[pl.ds(4 * h, 4)], spec_outs[h], out_sems.at[h]))
        sends[-1].start()
    for send in sends:
        send.wait()


def relay_kernel(a_ref, b_ref, c_ref, d_ref, own_ref, *send_refs):
    for k in range(4):
        parts = [ref[k].astype(f32) for ref in (a_ref, b_ref, c_ref, d_ref)]
        part = parts[0] + parts[1] + parts[2] + parts[3]
        if k == 0:
            own_ref[...] = part
            continue
        send_refs[k - 1][0:F, :] = part[0:F, :].astype(bf16)
        total = jnp.broadcast_to(part[F : F + 1, :] + part[F + 1 : F + 2, :], (8, SB))
        send_refs[k - 1][F:EXT, :] = high_low_rows(total)


SMEM = pl.BlockSpec(memory_space=pltpu.SMEM)
VMEM = pl.BlockSpec(memory_space=pltpu.VMEM)
ANY = pl.BlockSpec(memory_space=pl.ANY)


def call(kernel, in_specs, outs, scratch, *args):
    return pl.pallas_call(
        kernel,
        in_specs=in_specs,
        out_specs=[spec for spec, _, _ in outs],
        out_shape=[jax.ShapeDtypeStruct(s, d) for _, s, d in outs],
        scratch_shapes=scratch,
    )(*args)


def in_vmem(arrays):
    return [pltpu.with_memory_space_constraint(a, pltpu.VMEM) for a in arrays]


def per_device(spec_feat, photo_feat, spec_mass, photo_mass, tile_index, tile_count):
    photo_id = lax.axis_index("photo")
    spec_id = lax.axis_index("spec")
    meta = (
        tile_index.reshape(TMAX),
        tile_count.reshape(1),
        jnp.stack([photo_id, spec_id]).astype(jnp.int32),
    )
    x_own = spec_feat.T
    y_own = photo_feat[0].T
    x_pad = jnp.zeros((EXT - F - 1, SB), bf16)
    y_pad = jnp.zeros((EXT - F - 1, PB), bf16)
    x0 = jnp.concatenate([x_own, spec_mass.reshape(1, SB), x_pad])[None]
    y0 = jnp.concatenate([y_own, photo_mass.reshape(1, PB), y_pad])[None]

    x_flip = flip_z(x0)
    y_low = swap_low(y0)
    x0 = jnp.concatenate([x0, x_flip])
    x_mirror = mirror_z(x0)
    y0 = jnp.concatenate([y0, y_low])
    x0 = jnp.concatenate([x0, x_mirror])
    ys = [y0] + [shift_x(y0, k) for k in (1, 2, 3)]
    xs = [x0] + [shift_y(x0, k) for k in (1, 2, 3)]
    ys = ys + [swap_core(y) for y in ys]

    tiles = pltpu.VMEM((TURNS, GROUP, TILE, TILE), bf16)
    tile_sems = pltpu.SemaphoreType.DMA((TURNS,))
    row_acc = [pltpu.VMEM((TC, 16, TILE), bf16), pltpu.VMEM((TR, 16, TILE), f32)]
    column_acc = [pltpu.VMEM((TR, 16, TILE), bf16), pltpu.VMEM((TC, 16, TILE), f32)]
    blocks = [pltpu.VMEM((SLOTS, EXT, SB), bf16), pltpu.VMEM((SLOTS, EXT, PB), bf16)]
    piece_sems = pltpu.SemaphoreType.DMA((12,))
    n, b = call(
        column_start_kernel, [SMEM] + [ANY] * 8, [(VMEM, (TC, TILE), f32)] * 2,
        [pltpu.VMEM((SLOTS, EXT, PB), bf16), pltpu.SemaphoreType.DMA((8,))], meta[2][1:], *ys,
    )
    r, m, g = call(
        first_kernel, [SMEM] * 3 + [ANY] * 12 + [VMEM],
        [
            (VMEM, (TR, TILE), f32), (VMEM, (TR, TILE), f32),
            (ANY, (TURNS, GROUP, TILE, TILE), bf16),
        ],
        blocks + [pltpu.VMEM((TR, TILE, F), bf16)] + row_acc + [tiles, piece_sems, tile_sems],
        *meta, *xs, *ys, b,
    )
    lists = meta[0:2]

    def columns(rs):
        return call(
            column_kernel, [SMEM] * 2 + [VMEM] * 5 + [ANY], [(VMEM, (TC, TILE), f32)],
            column_acc + [tiles, tile_sems], *lists, *rs, m, g,
        )[0]

    rs = in_vmem(sum_photo(r))
    cs = in_vmem(sum_spec(columns(rs)))
    (r,) = call(
        row_kernel, [SMEM] * 2 + [VMEM] * 3 + [ANY], [(VMEM, (TR, TILE), f32)],
        row_acc + [tiles, tile_sems], *lists, *cs, n, g,
    )
    rs = in_vmem(sum_photo(r))
    cs = in_vmem(sum_spec(columns(rs)))
    *parts, share = call(
        grad_kernel, [SMEM] * 3 + [VMEM] * 8 + [ANY] * 13,
        [(ANY, (4, EXT, SB), bf16)] * 4 + [(ANY, (8, F, PB), bf16)] * 2 + [(VMEM, (4, 8, TILE), f32)],
        blocks
        + [
            pltpu.VMEM((TR, 8, TILE), f32),
            pltpu.VMEM((TC, 8, TILE), f32),
            pltpu.VMEM((TC, WROWS, TILE), bf16),
            pltpu.VMEM((TR, F, TILE), bf16),
            pltpu.VMEM((TR, WROWS, TILE), f32),
            pltpu.VMEM((TC, F, TILE), f32),
            pltpu.VMEM((SLOTS, EXT, SB), bf16),
            pltpu.VMEM((SLOTS, F, PB), bf16),
            tiles, piece_sems, tile_sems,
            pltpu.SemaphoreType.DMA((6,)),
        ],
        *meta, *rs, *cs, m, n, g, *xs, *ys,
    )
    share = share[:, 0, :].reshape(1, PB)

    spec_parts, photo_parts = (parts[0:4], parts[4:6])
    far = swap_core(photo_parts[1])
    y_parts = [shift_y(spec_parts[k], -k) for k in (1, 2, 3)]
    photo_sums = [photo_parts[0][2 * k : 2 * k + 2].astype(f32) + far[2 * k : 2 * k + 2].astype(f32) for k in range(4)]
    x_parts = [total.astype(bf16) for total in photo_sums[1:]]
    x_parts = [shift_x(part, -k) for k, part in zip((1, 2, 3), x_parts)]

    spec_sum, *z_parts = call(
        relay_kernel, [VMEM] * 4, [(VMEM, (EXT, SB), f32)] + [(VMEM, (EXT, SB), bf16)] * 3, [],
        spec_parts[0], *in_vmem(y_parts),
    )
    z_parts = [move(part) for move, part in zip((flip_z, mirror_z, across_z), z_parts)]
    for part in z_parts:
        spec_sum = spec_sum + part.astype(f32)
    photo_sum = photo_sums[0]
    for part in x_parts:
        photo_sum = photo_sum + part.astype(f32)
    photo_send = photo_sum[1].astype(bf16)
    lowered = swap_low(photo_send)
    photo_sum = photo_sum[0] + lowered.astype(f32)
    grad_photo = (2.0 * (share * y_own.astype(f32) - photo_sum)).T[None]
    row_marginal = spec_sum[F : F + 1] + spec_sum[F + 1 : F + 2]
    grad_spec = 2.0 * (row_marginal * x_own.astype(f32) - spec_sum[0:F])
    return (grad_spec.T, grad_photo)


def solution(mesh):
    return jax.shard_map(
        per_device,
        mesh=mesh,
        in_specs=(
            P(("spec", "photo"), None),
            P("spec", "photo", None),
            P(("spec", "photo")),
            P("spec", "photo"),
            P("spec", "photo", None),
            P("spec", "photo"),
        ),
        out_specs=(P(("spec", "photo"), None), P("spec", "photo", None)),
        check_vma=False,
    )
```

```python
import math

import jax
import jax.numpy as jnp
from jax import lax
from jax.experimental import pallas as pl
from jax.experimental.pallas import tpu as pltpu
from jax.sharding import PartitionSpec as P


TILE = 256
TR = 32
TC = 64
F = 64
TMAX = 96
SB = 512
PB = 1024
EXT = 72
WROWS = 80
SLOTS = 16
GROUP = 8
TURNS = TMAX // GROUP
SCALE = 0.125 * math.log2(math.e)
f32 = jnp.float32
bf16 = jnp.bfloat16


def photo_perm(fy, fz):
    return [(y * 4 + z, fy(y) * 4 + fz(z)) for y in range(4) for z in range(4)]


def spec_perm(fl, fx, fc):
    return [
        (l * 8 + x * 2 + c, fl(l) * 8 + fx(x) * 2 + fc(c))
        for l in range(2)
        for x in range(4)
        for c in range(2)
    ]


def same(i):
    return i


def flip(i):
    return i ^ 1


def mirror(i):
    return 3 - i


def shift(k):
    return lambda i: (i + k) % 4


def shift_y(a, k):
    return lax.ppermute(a, "photo", photo_perm(shift(k), same))


def shift_z(a, k):
    return lax.ppermute(a, "photo", photo_perm(same, shift(k)))


def flip_z(a):
    return lax.ppermute(a, "photo", photo_perm(same, flip))


def across_z(a):
    return lax.ppermute(a, "photo", photo_perm(same, lambda i: i ^ 2))


def mirror_z(a):
    return lax.ppermute(a, "photo", photo_perm(same, mirror))


def shift_x(a, k):
    return lax.ppermute(a, "spec", spec_perm(same, shift(k), same))


def swap_core(a):
    return lax.ppermute(a, "spec", spec_perm(same, same, flip))


def swap_low(a):
    return lax.ppermute(a, "spec", spec_perm(flip, same, same))


def sum_photo(a):
    parts = [shift_y(a, k) for k in (1, 2, 3)]
    a = (a + parts[0]) + (parts[1] + parts[2])
    return [a] + [shift_z(a, k) for k in (1, 2, 3)]


def sum_spec(a):
    a = a + swap_core(a)
    parts = [
        lax.ppermute(a, "spec", spec_perm(fl, fx, same)) for fl, fx in ((flip, same), (same, flip), (flip, flip))
    ]
    a = (a + parts[0]) + (parts[1] + parts[2])
    return [a, lax.ppermute(a, "spec", spec_perm(same, mirror, same))]


def spec_slot(q, photo_id):
    across = (photo_id ^ q) & 3
    return (((photo_id >> 2) - (q >> 2)) & 3) * 4 + (across ^ (across >> 1))


def photo_slot(q, spec_id):
    low = ((spec_id >> 3) - (q >> 3)) & 1
    across = ((spec_id >> 1) - (q >> 1)) & 3
    core = (spec_id - q) & 1
    return core * 8 + across * 2 + low


def entry_of(index_ref, t, last):
    entry = index_ref[jnp.minimum(t, last)]
    return ((entry >> 6) & 31, entry & 63)


def live(value, t, count_ref):
    return value * (t < count_ref[0]).astype(value.dtype)


def contract_last(a, b):
    return lax.dot_general(a, b, (((1,), (1,)), ((), ())), preferred_element_type=f32)


def high_low_rows(value):
    high = value.astype(bf16).astype(f32)
    sub = lax.broadcasted_iota(jnp.int32, value.shape, 0)
    return jnp.where(sub == 0, high, jnp.where(sub == 1, value - high, 0.0)).astype(bf16)


def high_low(value):
    return high_low_rows(jnp.broadcast_to(value, (16, value.shape[1])))


def turns_of(count_ref):
    return (count_ref[0] + GROUP - 1) // GROUP


def over_tiles(index_ref, count_ref, before, step, after):
    last = count_ref[0] - 1

    def turn(i, carry):
        before(i)
        for k in range(GROUP):
            row, column = entry_of(index_ref, i * GROUP + k, last)
            step(i, k, i * GROUP + k, row, column)
        after(i)
        return carry

    lax.fori_loop(0, turns_of(count_ref), turn, 0)


def start_tiles(count_ref, g_hbm, g_ref, sems):
    def turn(i, carry):
        pltpu.make_async_copy(g_hbm.at[i], g_ref.at[i], sems.at[i]).start()
        return carry

    lax.fori_loop(0, turns_of(count_ref), turn, 0)


def wait_tiles(g_hbm, g_ref, sems):
    return lambda i: pltpu.make_async_copy(g_hbm.at[i], g_ref.at[i], sems.at[i]).wait()


def nothing(i):
    pass


def store_pairs(acc_ref, out_ref):
    for i in range(out_ref.shape[0]):
        both = acc_ref[i]
        out_ref[i : i + 1, :] = both[0:1, :] + both[1:2, :]


def piece_copies(xs, ys, xt_ref, yt_ref, sems):
    copies = [pltpu.make_async_copy(xs[k], xt_ref.at[pl.ds(4 * k, 4)], sems.at[k]) for k in range(4)]
    return copies + [
        pltpu.make_async_copy(ys[k], yt_ref.at[pl.ds(2 * k, 2)], sems.at[4 + k]) for k in range(8)
    ]


def pack_kernel(x_ref, y_ref, x_mass_ref, y_mass_ref, x_out, y_out):
    def rows(values):
        sub = lax.broadcasted_iota(jnp.int32, (8, values[0].shape[1]), 0)
        block = jnp.zeros(sub.shape, f32)
        for i, value in enumerate(values):
            block = jnp.where(sub == i, value, block)
        return block.astype(bf16)

    x_out[0, 0:F, :] = x_ref[...]
    x_out[0, F:EXT, :] = rows([x_mass_ref[...].astype(f32)])
    y = y_ref[...].astype(f32)
    weight = jnp.exp(jnp.sum(y * y, axis=0, keepdims=True) * -0.0625)
    high = weight.astype(bf16).astype(f32)
    y_out[0, 0:F, :] = y_ref[...]
    y_out[0, F:EXT, :] = rows([y_mass_ref[...].astype(f32), high, weight - high])


def first_kernel(index_ref, count_ref, pos_ref, *refs):
    xs, ys = (refs[0:4], refs[4:12])
    out_ref, m_ref, n_ref, g_hbm = refs[12:16]
    xt_ref, yt_ref, xr_ref, w_ref, acc_ref, g_ref, sems, g_sems = refs[16:]
    copies = piece_copies(xs, ys, xt_ref, yt_ref, sems)
    for copy in copies:
        copy.start()
    acc_ref[...] = jnp.zeros_like(acc_ref)
    for copy in copies:
        copy.wait()
    for q in range(SLOTS):
        rows = yt_ref[photo_slot(q, pos_ref[1]), F:EXT, :].astype(f32)
        for k in range(4):
            lanes = slice(k * TILE, (k + 1) * TILE)
            n_ref[4 * q + k : 4 * q + k + 1, :] = rows[0:1, lanes]
            sub = lax.broadcasted_iota(jnp.int32, (16, TILE), 0)
            pair = jnp.where(sub == 0, rows[1:2, lanes], jnp.where(sub == 1, rows[2:3, lanes], 0.0))
            w_ref[4 * q + k] = pair.astype(bf16)

    def turn_slot(s, carry):
        for h in range(2):
            xr_ref[2 * s + h] = jnp.transpose(xt_ref[s, 0:F, h * TILE : (h + 1) * TILE])
        return carry

    lax.fori_loop(0, SLOTS, turn_slot, 0)

    for q in range(SLOTS):
        mass = xt_ref[spec_slot(q, pos_ref[0]), F:EXT, :].astype(f32)
        for k in range(2):
            m_ref[2 * q + k : 2 * q + k + 1, :] = mass[0:1, k * TILE : (k + 1) * TILE]

    def step(i, k, t, row, column):
        row_local = spec_slot(row >> 1, pos_ref[0]) * 2 + (row & 1)
        slot = photo_slot(column >> 2, pos_ref[1])
        lane = pl.multiple_of((column & 3) * TILE, TILE)
        y = yt_ref[slot, 0:F, pl.ds(lane, TILE)]
        cross = jnp.dot(xr_ref[row_local], y, preferred_element_type=f32)
        g = jnp.exp2(cross * SCALE).astype(bf16)
        g_ref[i, k] = g
        acc_ref[row] += contract_last(live(w_ref[column], t, count_ref), g)

    def send(i):
        pltpu.make_async_copy(g_ref.at[i], g_hbm.at[i], g_sems.at[i]).start()

    over_tiles(index_ref, count_ref, nothing, step, send)
    store_pairs(acc_ref, out_ref)

    def sent(i, carry):
        pltpu.make_async_copy(g_ref.at[i], g_hbm.at[i], g_sems.at[i]).wait()
        return carry

    lax.fori_loop(0, turns_of(count_ref), sent, 0)


def sum_of(refs):
    total = refs[0][...]
    for ref in refs[1:]:
        total = total + ref[...]
    return total


def column_kernel(index_ref, count_ref, *refs):
    r_refs = refs[0:4]
    m_ref, g_hbm, out_ref, w_ref, acc_ref, g_ref, sems = refs[4:]
    start_tiles(count_ref, g_hbm, g_ref, sems)
    acc_ref[...] = jnp.zeros_like(acc_ref)
    u = m_ref[...] / sum_of(r_refs)
    for row in range(TR):
        w_ref[row] = high_low(u[row : row + 1, :])

    def step(i, k, t, row, column):
        acc_ref[column] += jnp.dot(live(w_ref[row], t, count_ref), g_ref[i, k], preferred_element_type=f32)

    over_tiles(index_ref, count_ref, wait_tiles(g_hbm, g_ref, sems), step, nothing)
    store_pairs(acc_ref, out_ref)


def row_kernel(index_ref, count_ref, ca_ref, cb_ref, n_ref, g_hbm, out_ref, w_ref, acc_ref, g_ref, sems):
    start_tiles(count_ref, g_hbm, g_ref, sems)
    acc_ref[...] = jnp.zeros_like(acc_ref)
    v = n_ref[...] / (ca_ref[...] + cb_ref[...])
    for column in range(TC):
        w_ref[column] = high_low(v[column : column + 1, :])

    def step(i, k, t, row, column):
        acc_ref[row] += contract_last(live(w_ref[column], t, count_ref), g_ref[i, k])

    over_tiles(index_ref, count_ref, wait_tiles(g_hbm, g_ref, sems), step, nothing)
    store_pairs(acc_ref, out_ref)


def grad_kernel(index_ref, count_ref, pos_ref, *refs):
    r_refs, c_refs, m_ref, n_ref, g_hbm = (refs[0:4], refs[4:6], *refs[6:9])
    refs = refs[9:]
    xs, ys = (refs[0:4], refs[4:12])
    spec_outs, photo_outs, share_ref = (refs[12:16], refs[16:18], refs[18])
    xt_ref, yt_ref, u_ref, v_ref, wy_ref, vx_ref, spec_acc, photo_acc = refs[19:27]
    spec_ref, photo_ref, g_ref, sems, g_sems, out_sems = refs[27:]
    copies = piece_copies(xs, ys, xt_ref, yt_ref, sems)
    for copy in copies:
        copy.start()
    start_tiles(count_ref, g_hbm, g_ref, g_sems)
    u_all = m_ref[...] / sum_of(r_refs)
    total = sum_of(c_refs)
    v_all = n_ref[...] / total
    both_all = v_all * total
    for q in range(SLOTS):
        slot = spec_slot(q, pos_ref[0])
        for k in range(2):
            row = 2 * q + k
            u_ref[2 * slot + k] = jnp.broadcast_to(u_all[row : row + 1, :], (8, TILE))
    for q in range(SLOTS):
        slot = photo_slot(q, pos_ref[1])
        for k in range(4):
            column = 4 * q + k
            v_ref[4 * slot + k] = jnp.broadcast_to(v_all[column : column + 1, :], (8, TILE))

        @pl.when(slot == 0)
        def _():
            for k in range(4):
                share_ref[k] = jnp.broadcast_to(both_all[4 * q + k : 4 * q + k + 1, :], (8, TILE))

    spec_acc[...] = jnp.zeros_like(spec_acc)
    photo_acc[...] = jnp.zeros_like(photo_acc)
    for copy in copies:
        copy.wait()

    def ready_y(s, carry):
        for k in range(4):
            y = yt_ref[s, 0:F, k * TILE : (k + 1) * TILE].astype(f32)
            v = v_ref[4 * s + k][0:1, :]
            wy_ref[4 * s + k, 0:F, :] = (y * v).astype(bf16)
            wy_ref[4 * s + k, F:WROWS, :] = high_low(v)
        return carry

    def ready_x(s, carry):
        for k in range(2):
            x = xt_ref[s, 0:F, k * TILE : (k + 1) * TILE].astype(f32)
            vx_ref[2 * s + k] = (x * u_ref[2 * s + k][0:1, :]).astype(bf16)
        return carry

    lax.fori_loop(0, SLOTS, ready_y, 0)
    lax.fori_loop(0, SLOTS, ready_x, 0)

    def step(i, k, t, row, column):
        row_local = spec_slot(row >> 1, pos_ref[0]) * 2 + (row & 1)
        column_local = photo_slot(column >> 2, pos_ref[1]) * 4 + (column & 3)
        g = g_ref[i, k]
        spec_acc[row_local] += contract_last(live(wy_ref[column_local], t, count_ref), g)
        photo_acc[column_local] += jnp.dot(live(vx_ref[row_local], t, count_ref), g, preferred_element_type=f32)

    over_tiles(index_ref, count_ref, wait_tiles(g_hbm, g_ref, g_sems), step, nothing)

    def store_y(s, carry):
        for k in range(4):
            v = v_ref[4 * s + k][0:1, :]
            photo_ref[s, :, k * TILE : (k + 1) * TILE] = (photo_acc[4 * s + k] * v).astype(bf16)
        return carry

    def store_x(s, carry):
        for k in range(2):
            lanes = slice(k * TILE, (k + 1) * TILE)
            u = u_ref[2 * s + k][0:1, :]
            both = spec_acc[2 * s + k]
            spec_ref[s, 0:F, lanes] = (both[0:F, :] * u).astype(bf16)
            total = jnp.broadcast_to((both[F : F + 1, :] + both[F + 1 : F + 2, :]) * u, (8, TILE))
            spec_ref[s, F:EXT, lanes] = high_low_rows(total)
        return carry

    sends = []
    for h in (1, 0):
        lax.fori_loop(8 * h, 8 * h + 8, store_y, 0)
        sends.append(pltpu.make_async_copy(photo_ref.at[pl.ds(8 * h, 8)], photo_outs[h], out_sems.at[4 + h]))
        sends[-1].start()
    for h in range(4):
        lax.fori_loop(4 * h, 4 * h + 4, store_x, 0)
        sends.append(pltpu.make_async_copy(spec_ref.at[pl.ds(4 * h, 4)], spec_outs[h], out_sems.at[h]))
        sends[-1].start()
    for send in sends:
        send.wait()


def relay_kernel(a_ref, b_ref, c_ref, d_ref, own_ref, *send_refs):
    for k in range(4):
        parts = [ref[k].astype(f32) for ref in (a_ref, b_ref, c_ref, d_ref)]
        part = parts[0] + parts[1] + parts[2] + parts[3]
        if k == 0:
            own_ref[...] = part
            continue
        send_refs[k - 1][0:F, :] = part[0:F, :].astype(bf16)
        total = jnp.broadcast_to(part[F : F + 1, :] + part[F + 1 : F + 2, :], (8, SB))
        send_refs[k - 1][F:EXT, :] = high_low_rows(total)


SMEM = pl.BlockSpec(memory_space=pltpu.SMEM)
VMEM = pl.BlockSpec(memory_space=pltpu.VMEM)
ANY = pl.BlockSpec(memory_space=pl.ANY)


def call(kernel, in_specs, outs, scratch, *args):
    return pl.pallas_call(
        kernel,
        in_specs=in_specs,
        out_specs=[spec for spec, _, _ in outs],
        out_shape=[jax.ShapeDtypeStruct(s, d) for _, s, d in outs],
        scratch_shapes=scratch,
    )(*args)


def in_vmem(arrays):
    return [pltpu.with_memory_space_constraint(a, pltpu.VMEM) for a in arrays]


def per_device(spec_feat, photo_feat, spec_mass, photo_mass, tile_index, tile_count):
    photo_id = lax.axis_index("photo")
    spec_id = lax.axis_index("spec")
    meta = (
        tile_index.reshape(TMAX),
        tile_count.reshape(1),
        jnp.stack([photo_id, spec_id]).astype(jnp.int32),
    )
    x_own = spec_feat.T
    y_own = photo_feat[0].T
    x0, y0 = call(
        pack_kernel, [VMEM] * 4, [(VMEM, (1, EXT, SB), bf16), (VMEM, (1, EXT, PB), bf16)], [],
        x_own, y_own, spec_mass.reshape(1, SB), photo_mass.reshape(1, PB),
    )
    x_flip = flip_z(x0)
    y_low = swap_low(y0)
    x0 = jnp.concatenate([x0, x_flip])
    x_mirror = mirror_z(x0)
    y0 = jnp.concatenate([y0, y_low])
    x0 = jnp.concatenate([x0, x_mirror])
    ys = [y0] + [shift_x(y0, k) for k in (1, 2, 3)]
    xs = [x0] + [shift_y(x0, k) for k in (1, 2, 3)]
    ys = ys + [swap_core(y) for y in ys]

    tiles = pltpu.VMEM((TURNS, GROUP, TILE, TILE), bf16)
    tile_sems = pltpu.SemaphoreType.DMA((TURNS,))
    row_acc = [pltpu.VMEM((TC, 16, TILE), bf16), pltpu.VMEM((TR, 16, TILE), f32)]
    column_acc = [pltpu.VMEM((TR, 16, TILE), bf16), pltpu.VMEM((TC, 16, TILE), f32)]
    blocks = [pltpu.VMEM((SLOTS, EXT, SB), bf16), pltpu.VMEM((SLOTS, EXT, PB), bf16)]
    piece_sems = pltpu.SemaphoreType.DMA((12,))
    r, m, n, g = call(
        first_kernel, [SMEM] * 3 + [ANY] * 12,
        [
            (VMEM, (TR, TILE), f32), (VMEM, (TR, TILE), f32), (VMEM, (TC, TILE), f32),
            (ANY, (TURNS, GROUP, TILE, TILE), bf16),
        ],
        blocks + [pltpu.VMEM((TR, TILE, F), bf16)] + row_acc + [tiles, piece_sems, tile_sems],
        *meta, *xs, *ys,
    )
    lists = meta[0:2]

    def columns(rs):
        return call(
            column_kernel, [SMEM] * 2 + [VMEM] * 5 + [ANY], [(VMEM, (TC, TILE), f32)],
            column_acc + [tiles, tile_sems], *lists, *rs, m, g,
        )[0]

    rs = in_vmem(sum_photo(r))
    cs = in_vmem(sum_spec(columns(rs)))
    (r,) = call(
        row_kernel, [SMEM] * 2 + [VMEM] * 3 + [ANY], [(VMEM, (TR, TILE), f32)],
        row_acc + [tiles, tile_sems], *lists, *cs, n, g,
    )
    rs = in_vmem(sum_photo(r))
    cs = in_vmem(sum_spec(columns(rs)))
    *parts, share = call(
        grad_kernel, [SMEM] * 3 + [VMEM] * 8 + [ANY] * 13,
        [(ANY, (4, EXT, SB), bf16)] * 4 + [(ANY, (8, F, PB), bf16)] * 2 + [(VMEM, (4, 8, TILE), f32)],
        blocks
        + [
            pltpu.VMEM((TR, 8, TILE), f32),
            pltpu.VMEM((TC, 8, TILE), f32),
            pltpu.VMEM((TC, WROWS, TILE), bf16),
            pltpu.VMEM((TR, F, TILE), bf16),
            pltpu.VMEM((TR, WROWS, TILE), f32),
            pltpu.VMEM((TC, F, TILE), f32),
            pltpu.VMEM((SLOTS, EXT, SB), bf16),
            pltpu.VMEM((SLOTS, F, PB), bf16),
            tiles, piece_sems, tile_sems,
            pltpu.SemaphoreType.DMA((6,)),
        ],
        *meta, *rs, *cs, m, n, g, *xs, *ys,
    )
    share = share[:, 0, :].reshape(1, PB)

    spec_parts, photo_parts = (parts[0:4], parts[4:6])
    far = swap_core(photo_parts[1])
    y_parts = [shift_y(spec_parts[k], -k) for k in (1, 2, 3)]
    photo_sums = [photo_parts[0][2 * k : 2 * k + 2].astype(f32) + far[2 * k : 2 * k + 2].astype(f32) for k in range(4)]
    x_parts = [total.astype(bf16) for total in photo_sums[1:]]
    x_parts = [shift_x(part, -k) for k, part in zip((1, 2, 3), x_parts)]

    spec_sum, *z_parts = call(
        relay_kernel, [VMEM] * 4, [(VMEM, (EXT, SB), f32)] + [(VMEM, (EXT, SB), bf16)] * 3, [],
        spec_parts[0], *in_vmem(y_parts),
    )
    z_parts = [move(part) for move, part in zip((flip_z, mirror_z, across_z), z_parts)]
    for part in z_parts:
        spec_sum = spec_sum + part.astype(f32)
    photo_sum = photo_sums[0]
    for part in x_parts:
        photo_sum = photo_sum + part.astype(f32)
    photo_send = photo_sum[1].astype(bf16)
    lowered = swap_low(photo_send)
    photo_sum = photo_sum[0] + lowered.astype(f32)
    grad_photo = (2.0 * (share * y_own.astype(f32) - photo_sum)).T[None]
    row_marginal = spec_sum[F : F + 1] + spec_sum[F + 1 : F + 2]
    grad_spec = 2.0 * (row_marginal * x_own.astype(f32) - spec_sum[0:F])
    return (grad_spec.T, grad_photo)


def solution(mesh):
    return jax.shard_map(
        per_device,
        mesh=mesh,
        in_specs=(
            P(("spec", "photo"), None),
            P("spec", "photo", None),
            P(("spec", "photo")),
            P("spec", "photo"),
            P("spec", "photo", None),
            P("spec", "photo"),
        ),
        out_specs=(P(("spec", "photo"), None), P("spec", "photo", None)),
        check_vma=False,
    )
```

```python
import math

import jax
import jax.numpy as jnp
from jax import lax
from jax.experimental import pallas as pl
from jax.experimental.pallas import tpu as pltpu
from jax.sharding import PartitionSpec as P


TILE = 256
TR = 32
TC = 64
F = 64
TMAX = 96
SB = 512
PB = 1024
EXT = 72
WROWS = 80
SLOTS = 16
GROUP = 8
TURNS = TMAX // GROUP
SCALE = 0.125 * math.log2(math.e)
f32 = jnp.float32
bf16 = jnp.bfloat16


def photo_perm(fy, fz):
    return [(y * 4 + z, fy(y) * 4 + fz(z)) for y in range(4) for z in range(4)]


def spec_perm(fl, fx, fc):
    return [
        (l * 8 + x * 2 + c, fl(l) * 8 + fx(x) * 2 + fc(c))
        for l in range(2)
        for x in range(4)
        for c in range(2)
    ]


def same(i):
    return i


def flip(i):
    return i ^ 1


def mirror(i):
    return 3 - i


def shift(k):
    return lambda i: (i + k) % 4


def shift_y(a, k):
    return lax.ppermute(a, "photo", photo_perm(shift(k), same))


def shift_z(a, k):
    return lax.ppermute(a, "photo", photo_perm(same, shift(k)))


def flip_z(a):
    return lax.ppermute(a, "photo", photo_perm(same, flip))


def across_z(a):
    return lax.ppermute(a, "photo", photo_perm(same, lambda i: i ^ 2))


def mirror_z(a):
    return lax.ppermute(a, "photo", photo_perm(same, mirror))


def shift_x(a, k):
    return lax.ppermute(a, "spec", spec_perm(same, shift(k), same))


def swap_core(a):
    return lax.ppermute(a, "spec", spec_perm(same, same, flip))


def swap_low(a):
    return lax.ppermute(a, "spec", spec_perm(flip, same, same))


def sum_photo(a):
    parts = [shift_y(a, k) for k in (1, 2, 3)]
    a = (a + parts[0]) + (parts[1] + parts[2])
    return [a] + [shift_z(a, k) for k in (1, 2, 3)]


def sum_spec(a):
    a = a + swap_core(a)
    parts = [
        lax.ppermute(a, "spec", spec_perm(fl, fx, same)) for fl, fx in ((flip, same), (same, flip), (flip, flip))
    ]
    a = (a + parts[0]) + (parts[1] + parts[2])
    return [a, lax.ppermute(a, "spec", spec_perm(same, mirror, same))]


def spec_slot(q, photo_id):
    across = (photo_id ^ q) & 3
    return (((photo_id >> 2) - (q >> 2)) & 3) * 4 + (across ^ (across >> 1))


def photo_slot(q, spec_id):
    low = ((spec_id >> 3) - (q >> 3)) & 1
    across = ((spec_id >> 1) - (q >> 1)) & 3
    core = (spec_id - q) & 1
    return core * 8 + across * 2 + low


def entry_of(index_ref, t, last):
    entry = index_ref[jnp.minimum(t, last)]
    return ((entry >> 6) & 31, entry & 63)


def live(value, t, count_ref):
    return value * (t < count_ref[0]).astype(value.dtype)


def contract_last(a, b):
    return lax.dot_general(a, b, (((1,), (1,)), ((), ())), preferred_element_type=f32)


def high_low_rows(value):
    high = value.astype(bf16).astype(f32)
    sub = lax.broadcasted_iota(jnp.int32, value.shape, 0)
    return jnp.where(sub == 0, high, jnp.where(sub == 1, value - high, 0.0)).astype(bf16)


def high_low(value):
    return high_low_rows(jnp.broadcast_to(value, (16, value.shape[1])))


def turns_of(count_ref):
    return (count_ref[0] + GROUP - 1) // GROUP


def over_tiles(index_ref, count_ref, before, step, after):
    last = count_ref[0] - 1

    def turn(i, carry):
        before(i)
        for k in range(GROUP):
            row, column = entry_of(index_ref, i * GROUP + k, last)
            step(i, k, i * GROUP + k, row, column)
        after(i)
        return carry

    lax.fori_loop(0, turns_of(count_ref), turn, 0)


def start_tiles(count_ref, g_hbm, g_ref, sems):
    def turn(i, carry):
        pltpu.make_async_copy(g_hbm.at[i], g_ref.at[i], sems.at[i]).start()
        return carry

    lax.fori_loop(0, turns_of(count_ref), turn, 0)


def wait_tiles(g_hbm, g_ref, sems):
    return lambda i: pltpu.make_async_copy(g_hbm.at[i], g_ref.at[i], sems.at[i]).wait()


def nothing(i):
    pass


def store_pairs(acc_ref, out_ref):
    for i in range(out_ref.shape[0]):
        both = acc_ref[i]
        out_ref[i : i + 1, :] = both[0:1, :] + both[1:2, :]


def piece_copies(xs, ys, xt_ref, yt_ref, sems):
    copies = [pltpu.make_async_copy(xs[k], xt_ref.at[pl.ds(4 * k, 4)], sems.at[k]) for k in range(4)]
    return copies + [
        pltpu.make_async_copy(ys[k], yt_ref.at[pl.ds(2 * k, 2)], sems.at[4 + k]) for k in range(8)
    ]


def pack_kernel(y_ref, mass_ref, out_ref):
    y = y_ref[...].astype(f32)
    weight = jnp.exp(jnp.sum(y * y, axis=0, keepdims=True) * -0.0625)
    high = weight.astype(bf16).astype(f32)
    sub = lax.broadcasted_iota(jnp.int32, (8, PB), 0)
    block = jnp.where(sub == 0, mass_ref[...].astype(f32), 0.0)
    block = jnp.where(sub == 1, high, jnp.where(sub == 2, weight - high, block))
    out_ref[0, 0:F, :] = y_ref[...]
    out_ref[0, F:EXT, :] = block.astype(bf16)


def first_kernel(index_ref, count_ref, pos_ref, *refs):
    xs, ys = (refs[0:4], refs[4:12])
    out_ref, m_ref, n_ref, g_hbm = refs[12:16]
    xt_ref, yt_ref, xr_ref, w_ref, acc_ref, g_ref, sems, g_sems = refs[16:]
    copies = piece_copies(xs, ys, xt_ref, yt_ref, sems)
    for copy in copies:
        copy.start()
    acc_ref[...] = jnp.zeros_like(acc_ref)
    for copy in copies:
        copy.wait()
    for q in range(SLOTS):
        rows = yt_ref[photo_slot(q, pos_ref[1]), F:EXT, :].astype(f32)
        for k in range(4):
            lanes = slice(k * TILE, (k + 1) * TILE)
            n_ref[4 * q + k : 4 * q + k + 1, :] = rows[0:1, lanes]
            sub = lax.broadcasted_iota(jnp.int32, (16, TILE), 0)
            pair = jnp.where(sub == 0, rows[1:2, lanes], jnp.where(sub == 1, rows[2:3, lanes], 0.0))
            w_ref[4 * q + k] = pair.astype(bf16)

    def turn_slot(s, carry):
        for h in range(2):
            xr_ref[2 * s + h] = jnp.transpose(xt_ref[s, 0:F, h * TILE : (h + 1) * TILE])
        return carry

    lax.fori_loop(0, SLOTS, turn_slot, 0)

    for q in range(SLOTS):
        mass = xt_ref[spec_slot(q, pos_ref[0]), F:EXT, :].astype(f32)
        for k in range(2):
            m_ref[2 * q + k : 2 * q + k + 1, :] = mass[0:1, k * TILE : (k + 1) * TILE]

    def step(i, k, t, row, column):
        row_local = spec_slot(row >> 1, pos_ref[0]) * 2 + (row & 1)
        slot = photo_slot(column >> 2, pos_ref[1])
        lane = pl.multiple_of((column & 3) * TILE, TILE)
        y = yt_ref[slot, 0:F, pl.ds(lane, TILE)]
        cross = jnp.dot(xr_ref[row_local], y, preferred_element_type=f32)
        g = jnp.exp2(cross * SCALE).astype(bf16)
        g_ref[i, k] = g
        acc_ref[row] += contract_last(live(w_ref[column], t, count_ref), g)

    def send(i):
        pltpu.make_async_copy(g_ref.at[i], g_hbm.at[i], g_sems.at[i]).start()

    over_tiles(index_ref, count_ref, nothing, step, send)
    store_pairs(acc_ref, out_ref)

    def sent(i, carry):
        pltpu.make_async_copy(g_ref.at[i], g_hbm.at[i], g_sems.at[i]).wait()
        return carry

    lax.fori_loop(0, turns_of(count_ref), sent, 0)


def sum_of(refs):
    total = refs[0][...]
    for ref in refs[1:]:
        total = total + ref[...]
    return total


def column_kernel(index_ref, count_ref, *refs):
    r_refs = refs[0:4]
    m_ref, g_hbm, out_ref, w_ref, acc_ref, g_ref, sems = refs[4:]
    start_tiles(count_ref, g_hbm, g_ref, sems)
    acc_ref[...] = jnp.zeros_like(acc_ref)
    u = m_ref[...] / sum_of(r_refs)
    for row in range(TR):
        w_ref[row] = high_low(u[row : row + 1, :])

    def step(i, k, t, row, column):
        acc_ref[column] += jnp.dot(live(w_ref[row], t, count_ref), g_ref[i, k], preferred_element_type=f32)

    over_tiles(index_ref, count_ref, wait_tiles(g_hbm, g_ref, sems), step, nothing)
    store_pairs(acc_ref, out_ref)


def row_kernel(index_ref, count_ref, ca_ref, cb_ref, n_ref, g_hbm, out_ref, w_ref, acc_ref, g_ref, sems):
    start_tiles(count_ref, g_hbm, g_ref, sems)
    acc_ref[...] = jnp.zeros_like(acc_ref)
    v = n_ref[...] / (ca_ref[...] + cb_ref[...])
    for column in range(TC):
        w_ref[column] = high_low(v[column : column + 1, :])

    def step(i, k, t, row, column):
        acc_ref[row] += contract_last(live(w_ref[column], t, count_ref), g_ref[i, k])

    over_tiles(index_ref, count_ref, wait_tiles(g_hbm, g_ref, sems), step, nothing)
    store_pairs(acc_ref, out_ref)


def grad_kernel(index_ref, count_ref, pos_ref, *refs):
    r_refs, c_refs, m_ref, n_ref, g_hbm = (refs[0:4], refs[4:6], *refs[6:9])
    refs = refs[9:]
    xs, ys = (refs[0:4], refs[4:12])
    spec_outs, photo_outs, share_ref = (refs[12:16], refs[16:18], refs[18])
    xt_ref, yt_ref, u_ref, v_ref, wy_ref, vx_ref, spec_acc, photo_acc = refs[19:27]
    spec_ref, photo_ref, g_ref, sems, g_sems, out_sems = refs[27:]
    copies = piece_copies(xs, ys, xt_ref, yt_ref, sems)
    for copy in copies:
        copy.start()
    start_tiles(count_ref, g_hbm, g_ref, g_sems)
    u_all = m_ref[...] / sum_of(r_refs)
    total = sum_of(c_refs)
    v_all = n_ref[...] / total
    both_all = v_all * total
    for q in range(SLOTS):
        slot = spec_slot(q, pos_ref[0])
        for k in range(2):
            row = 2 * q + k
            u_ref[2 * slot + k] = jnp.broadcast_to(u_all[row : row + 1, :], (8, TILE))
    for q in range(SLOTS):
        slot = photo_slot(q, pos_ref[1])
        for k in range(4):
            column = 4 * q + k
            v_ref[4 * slot + k] = jnp.broadcast_to(v_all[column : column + 1, :], (8, TILE))

        @pl.when(slot == 0)
        def _():
            for k in range(4):
                share_ref[k] = jnp.broadcast_to(both_all[4 * q + k : 4 * q + k + 1, :], (8, TILE))

    spec_acc[...] = jnp.zeros_like(spec_acc)
    photo_acc[...] = jnp.zeros_like(photo_acc)
    for copy in copies:
        copy.wait()

    def ready_y(s, carry):
        for k in range(4):
            y = yt_ref[s, 0:F, k * TILE : (k + 1) * TILE].astype(f32)
            v = v_ref[4 * s + k][0:1, :]
            wy_ref[4 * s + k, 0:F, :] = (y * v).astype(bf16)
            wy_ref[4 * s + k, F:WROWS, :] = high_low(v)
        return carry

    def ready_x(s, carry):
        for k in range(2):
            x = xt_ref[s, 0:F, k * TILE : (k + 1) * TILE].astype(f32)
            vx_ref[2 * s + k] = (x * u_ref[2 * s + k][0:1, :]).astype(bf16)
        return carry

    lax.fori_loop(0, SLOTS, ready_y, 0)
    lax.fori_loop(0, SLOTS, ready_x, 0)

    def step(i, k, t, row, column):
        row_local = spec_slot(row >> 1, pos_ref[0]) * 2 + (row & 1)
        column_local = photo_slot(column >> 2, pos_ref[1]) * 4 + (column & 3)
        g = g_ref[i, k]
        spec_acc[row_local] += contract_last(live(wy_ref[column_local], t, count_ref), g)
        photo_acc[column_local] += jnp.dot(live(vx_ref[row_local], t, count_ref), g, preferred_element_type=f32)

    over_tiles(index_ref, count_ref, wait_tiles(g_hbm, g_ref, g_sems), step, nothing)

    def store_y(s, carry):
        for k in range(4):
            v = v_ref[4 * s + k][0:1, :]
            photo_ref[s, :, k * TILE : (k + 1) * TILE] = (photo_acc[4 * s + k] * v).astype(bf16)
        return carry

    def store_x(s, carry):
        for k in range(2):
            lanes = slice(k * TILE, (k + 1) * TILE)
            u = u_ref[2 * s + k][0:1, :]
            both = spec_acc[2 * s + k]
            spec_ref[s, 0:F, lanes] = (both[0:F, :] * u).astype(bf16)
            total = jnp.broadcast_to((both[F : F + 1, :] + both[F + 1 : F + 2, :]) * u, (8, TILE))
            spec_ref[s, F:EXT, lanes] = high_low_rows(total)
        return carry

    sends = []
    for h in (1, 0):
        lax.fori_loop(8 * h, 8 * h + 8, store_y, 0)
        sends.append(pltpu.make_async_copy(photo_ref.at[pl.ds(8 * h, 8)], photo_outs[h], out_sems.at[4 + h]))
        sends[-1].start()
    for h in range(4):
        lax.fori_loop(4 * h, 4 * h + 4, store_x, 0)
        sends.append(pltpu.make_async_copy(spec_ref.at[pl.ds(4 * h, 4)], spec_outs[h], out_sems.at[h]))
        sends[-1].start()
    for send in sends:
        send.wait()


def relay_kernel(a_ref, b_ref, c_ref, d_ref, own_ref, *send_refs):
    for k in range(4):
        parts = [ref[k].astype(f32) for ref in (a_ref, b_ref, c_ref, d_ref)]
        part = parts[0] + parts[1] + parts[2] + parts[3]
        if k == 0:
            own_ref[...] = part
            continue
        send_refs[k - 1][0:F, :] = part[0:F, :].astype(bf16)
        total = jnp.broadcast_to(part[F : F + 1, :] + part[F + 1 : F + 2, :], (8, SB))
        send_refs[k - 1][F:EXT, :] = high_low_rows(total)


SMEM = pl.BlockSpec(memory_space=pltpu.SMEM)
VMEM = pl.BlockSpec(memory_space=pltpu.VMEM)
ANY = pl.BlockSpec(memory_space=pl.ANY)


def call(kernel, in_specs, outs, scratch, *args):
    return pl.pallas_call(
        kernel,
        in_specs=in_specs,
        out_specs=[spec for spec, _, _ in outs],
        out_shape=[jax.ShapeDtypeStruct(s, d) for _, s, d in outs],
        scratch_shapes=scratch,
    )(*args)


def in_vmem(arrays):
    return [pltpu.with_memory_space_constraint(a, pltpu.VMEM) for a in arrays]


def per_device(spec_feat, photo_feat, spec_mass, photo_mass, tile_index, tile_count):
    photo_id = lax.axis_index("photo")
    spec_id = lax.axis_index("spec")
    meta = (
        tile_index.reshape(TMAX),
        tile_count.reshape(1),
        jnp.stack([photo_id, spec_id]).astype(jnp.int32),
    )
    x_own = spec_feat.T
    y_own = photo_feat[0].T
    x_pad = jnp.zeros((EXT - F - 1, SB), bf16)
    x0 = jnp.concatenate([x_own, spec_mass.reshape(1, SB), x_pad])[None]
    (y0,) = call(
        pack_kernel, [VMEM] * 2, [(VMEM, (1, EXT, PB), bf16)], [],
        y_own, photo_mass.reshape(1, PB),
    )
    x_parts = [move(x0) for move in (flip_z, mirror_z, across_z)]
    y_low = swap_low(y0)
    x0 = jnp.concatenate([x0] + x_parts)
    y0 = jnp.concatenate([y0, y_low])
    ys = [y0] + [shift_x(y0, k) for k in (1, 2, 3)]
    xs = [x0] + [shift_y(x0, k) for k in (1, 2, 3)]
    ys = ys + [swap_core(y) for y in ys]

    tiles = pltpu.VMEM((TURNS, GROUP, TILE, TILE), bf16)
    tile_sems = pltpu.SemaphoreType.DMA((TURNS,))
    row_acc = [pltpu.VMEM((TC, 16, TILE), bf16), pltpu.VMEM((TR, 16, TILE), f32)]
    column_acc = [pltpu.VMEM((TR, 16, TILE), bf16), pltpu.VMEM((TC, 16, TILE), f32)]
    blocks = [pltpu.VMEM((SLOTS, EXT, SB), bf16), pltpu.VMEM((SLOTS, EXT, PB), bf16)]
    piece_sems = pltpu.SemaphoreType.DMA((12,))
    r, m, n, g = call(
        first_kernel, [SMEM] * 3 + [ANY] * 12,
        [
            (VMEM, (TR, TILE), f32), (VMEM, (TR, TILE), f32), (VMEM, (TC, TILE), f32),
            (ANY, (TURNS, GROUP, TILE, TILE), bf16),
        ],
        blocks + [pltpu.VMEM((TR, TILE, F), bf16)] + row_acc + [tiles, piece_sems, tile_sems],
        *meta, *xs, *ys,
    )
    lists = meta[0:2]

    def columns(rs):
        return call(
            column_kernel, [SMEM] * 2 + [VMEM] * 5 + [ANY], [(VMEM, (TC, TILE), f32)],
            column_acc + [tiles, tile_sems], *lists, *rs, m, g,
        )[0]

    rs = in_vmem(sum_photo(r))
    cs = in_vmem(sum_spec(columns(rs)))
    (r,) = call(
        row_kernel, [SMEM] * 2 + [VMEM] * 3 + [ANY], [(VMEM, (TR, TILE), f32)],
        row_acc + [tiles, tile_sems], *lists, *cs, n, g,
    )
    rs = in_vmem(sum_photo(r))
    cs = in_vmem(sum_spec(columns(rs)))
    *parts, share = call(
        grad_kernel, [SMEM] * 3 + [VMEM] * 8 + [ANY] * 13,
        [(ANY, (4, EXT, SB), bf16)] * 4 + [(ANY, (8, F, PB), bf16)] * 2 + [(VMEM, (4, 8, TILE), f32)],
        blocks
        + [
            pltpu.VMEM((TR, 8, TILE), f32),
            pltpu.VMEM((TC, 8, TILE), f32),
            pltpu.VMEM((TC, WROWS, TILE), bf16),
            pltpu.VMEM((TR, F, TILE), bf16),
            pltpu.VMEM((TR, WROWS, TILE), f32),
            pltpu.VMEM((TC, F, TILE), f32),
            pltpu.VMEM((SLOTS, EXT, SB), bf16),
            pltpu.VMEM((SLOTS, F, PB), bf16),
            tiles, piece_sems, tile_sems,
            pltpu.SemaphoreType.DMA((6,)),
        ],
        *meta, *rs, *cs, m, n, g, *xs, *ys,
    )
    share = share[:, 0, :].reshape(1, PB)

    spec_parts, photo_parts = (parts[0:4], parts[4:6])
    far = swap_core(photo_parts[1])
    y_parts = [shift_y(spec_parts[k], -k) for k in (1, 2, 3)]
    photo_sums = [photo_parts[0][2 * k : 2 * k + 2].astype(f32) + far[2 * k : 2 * k + 2].astype(f32) for k in range(4)]
    x_parts = [total.astype(bf16) for total in photo_sums[1:]]
    x_parts = [shift_x(part, -k) for k, part in zip((1, 2, 3), x_parts)]

    spec_sum, *z_parts = call(
        relay_kernel, [VMEM] * 4, [(VMEM, (EXT, SB), f32)] + [(VMEM, (EXT, SB), bf16)] * 3, [],
        spec_parts[0], *in_vmem(y_parts),
    )
    z_parts = [move(part) for move, part in zip((flip_z, mirror_z, across_z), z_parts)]
    for part in z_parts:
        spec_sum = spec_sum + part.astype(f32)
    photo_sum = photo_sums[0]
    for part in x_parts:
        photo_sum = photo_sum + part.astype(f32)
    photo_send = photo_sum[1].astype(bf16)
    lowered = swap_low(photo_send)
    photo_sum = photo_sum[0] + lowered.astype(f32)
    grad_photo = (2.0 * (share * y_own.astype(f32) - photo_sum)).T[None]
    row_marginal = spec_sum[F : F + 1] + spec_sum[F + 1 : F + 2]
    grad_spec = 2.0 * (row_marginal * x_own.astype(f32) - spec_sum[0:F])
    return (grad_spec.T, grad_photo)


def solution(mesh):
    return jax.shard_map(
        per_device,
        mesh=mesh,
        in_specs=(
            P(("spec", "photo"), None),
            P("spec", "photo", None),
            P(("spec", "photo")),
            P("spec", "photo"),
            P("spec", "photo", None),
            P("spec", "photo"),
        ),
        out_specs=(P(("spec", "photo"), None), P("spec", "photo", None)),
        check_vma=False,
    )
```

```python
import math

import jax
import jax.numpy as jnp
from jax import lax
from jax.experimental import pallas as pl
from jax.experimental.pallas import tpu as pltpu
from jax.sharding import PartitionSpec as P


TILE = 256
TR = 32
TC = 64
F = 64
TMAX = 96
SB = 512
PB = 1024
EXT = 72
WROWS = 80
SLOTS = 16
GROUP = 8
TURNS = TMAX // GROUP
SCALE = 0.125 * math.log2(math.e)
f32 = jnp.float32
bf16 = jnp.bfloat16


def photo_perm(fy, fz):
    return [(y * 4 + z, fy(y) * 4 + fz(z)) for y in range(4) for z in range(4)]


def spec_perm(fl, fx, fc):
    return [
        (l * 8 + x * 2 + c, fl(l) * 8 + fx(x) * 2 + fc(c))
        for l in range(2)
        for x in range(4)
        for c in range(2)
    ]


def same(i):
    return i


def flip(i):
    return i ^ 1


def mirror(i):
    return 3 - i


def shift(k):
    return lambda i: (i + k) % 4


def shift_y(a, k):
    return lax.ppermute(a, "photo", photo_perm(shift(k), same))


def shift_z(a, k):
    return lax.ppermute(a, "photo", photo_perm(same, shift(k)))


def flip_z(a):
    return lax.ppermute(a, "photo", photo_perm(same, flip))


def across_z(a):
    return lax.ppermute(a, "photo", photo_perm(same, lambda i: i ^ 2))


def mirror_z(a):
    return lax.ppermute(a, "photo", photo_perm(same, mirror))


def shift_x(a, k):
    return lax.ppermute(a, "spec", spec_perm(same, shift(k), same))


def swap_core(a):
    return lax.ppermute(a, "spec", spec_perm(same, same, flip))


def swap_low(a):
    return lax.ppermute(a, "spec", spec_perm(flip, same, same))


def sum_photo(a):
    parts = [shift_y(a, k) for k in (1, 2, 3)]
    a = (a + parts[0]) + (parts[1] + parts[2])
    return [a] + [shift_z(a, k) for k in (1, 2, 3)]


def sum_spec(a):
    a = a + swap_core(a)
    parts = [
        lax.ppermute(a, "spec", spec_perm(fl, fx, same)) for fl, fx in ((flip, same), (same, flip), (flip, flip))
    ]
    a = (a + parts[0]) + (parts[1] + parts[2])
    return [a, lax.ppermute(a, "spec", spec_perm(same, mirror, same))]


def spec_slot(q, photo_id):
    across = (photo_id ^ q) & 3
    return (((photo_id >> 2) - (q >> 2)) & 3) * 4 + (across ^ (across >> 1))


def photo_slot(q, spec_id):
    low = ((spec_id >> 3) - (q >> 3)) & 1
    across = ((spec_id >> 1) - (q >> 1)) & 3
    core = (spec_id - q) & 1
    return core * 8 + across * 2 + low


def entry_of(index_ref, t, last):
    entry = index_ref[jnp.minimum(t, last)]
    return ((entry >> 6) & 31, entry & 63)


def live(value, t, count_ref):
    return value * (t < count_ref[0]).astype(value.dtype)


def contract_last(a, b):
    return lax.dot_general(a, b, (((1,), (1,)), ((), ())), preferred_element_type=f32)


def high_low_rows(value):
    high = value.astype(bf16).astype(f32)
    sub = lax.broadcasted_iota(jnp.int32, value.shape, 0)
    return jnp.where(sub == 0, high, jnp.where(sub == 1, value - high, 0.0)).astype(bf16)


def high_low(value):
    return high_low_rows(jnp.broadcast_to(value, (16, value.shape[1])))


def turns_of(count_ref):
    return (count_ref[0] + GROUP - 1) // GROUP


def over_tiles(index_ref, count_ref, before, step, after):
    last = count_ref[0] - 1

    def turn(i, carry):
        before(i)
        for k in range(GROUP):
            row, column = entry_of(index_ref, i * GROUP + k, last)
            step(i, k, i * GROUP + k, row, column)
        after(i)
        return carry

    lax.fori_loop(0, turns_of(count_ref), turn, 0)


def start_tiles(count_ref, g_hbm, g_ref, sems):
    def turn(i, carry):
        pltpu.make_async_copy(g_hbm.at[i], g_ref.at[i], sems.at[i]).start()
        return carry

    lax.fori_loop(0, turns_of(count_ref), turn, 0)


def wait_tiles(g_hbm, g_ref, sems):
    return lambda i: pltpu.make_async_copy(g_hbm.at[i], g_ref.at[i], sems.at[i]).wait()


def nothing(i):
    pass


def store_pairs(acc_ref, out_ref):
    for i in range(out_ref.shape[0]):
        both = acc_ref[i]
        out_ref[i : i + 1, :] = both[0:1, :] + both[1:2, :]


def piece_copies(xs, ys, xt_ref, yt_ref, sems):
    copies = [pltpu.make_async_copy(xs[k], xt_ref.at[pl.ds(4 * k, 4)], sems.at[k]) for k in range(4)]
    return copies + [
        pltpu.make_async_copy(ys[k], yt_ref.at[pl.ds(2 * k, 2)], sems.at[4 + k]) for k in range(8)
    ]


def pack_kernel(y_ref, mass_ref, out_ref):
    y = y_ref[...].astype(f32)
    weight = jnp.exp(jnp.sum(y * y, axis=0, keepdims=True) * -0.0625)
    high = weight.astype(bf16).astype(f32)
    sub = lax.broadcasted_iota(jnp.int32, (8, PB), 0)
    block = jnp.where(sub == 0, mass_ref[...].astype(f32), 0.0)
    block = jnp.where(sub == 1, high, jnp.where(sub == 2, weight - high, block))
    out_ref[0, 0:F, :] = y_ref[...]
    out_ref[0, F:EXT, :] = block.astype(bf16)


def first_kernel(index_ref, count_ref, pos_ref, *refs):
    xs, ys = (refs[0:4], refs[4:12])
    out_ref, m_ref, n_ref, g_hbm = refs[12:16]
    xt_ref, yt_ref, xr_ref, w_ref, acc_ref, g_ref, sems, g_sems = refs[16:]
    copies = piece_copies(xs, ys, xt_ref, yt_ref, sems)
    for copy in copies:
        copy.start()
    acc_ref[...] = jnp.zeros_like(acc_ref)
    for copy in copies:
        copy.wait()
    for q in range(SLOTS):
        rows = yt_ref[photo_slot(q, pos_ref[1]), F:EXT, :].astype(f32)
        for k in range(4):
            lanes = slice(k * TILE, (k + 1) * TILE)
            n_ref[4 * q + k : 4 * q + k + 1, :] = rows[0:1, lanes]
            sub = lax.broadcasted_iota(jnp.int32, (16, TILE), 0)
            pair = jnp.where(sub == 0, rows[1:2, lanes], jnp.where(sub == 1, rows[2:3, lanes], 0.0))
            w_ref[4 * q + k] = pair.astype(bf16)

    def turn_slot(s, carry):
        for h in range(2):
            xr_ref[2 * s + h] = jnp.transpose(xt_ref[s, 0:F, h * TILE : (h + 1) * TILE])
        return carry

    lax.fori_loop(0, SLOTS, turn_slot, 0)

    for q in range(SLOTS):
        mass = xt_ref[spec_slot(q, pos_ref[0]), F:EXT, :].astype(f32)
        for k in range(2):
            m_ref[2 * q + k : 2 * q + k + 1, :] = mass[0:1, k * TILE : (k + 1) * TILE]

    def step(i, k, t, row, column):
        row_local = spec_slot(row >> 1, pos_ref[0]) * 2 + (row & 1)
        slot = photo_slot(column >> 2, pos_ref[1])
        lane = pl.multiple_of((column & 3) * TILE, TILE)
        y = yt_ref[slot, 0:F, pl.ds(lane, TILE)]
        cross = jnp.dot(xr_ref[row_local], y, preferred_element_type=f32)
        g = jnp.exp2(cross * SCALE).astype(bf16)
        g_ref[i, k] = g
        acc_ref[row] += contract_last(live(w_ref[column], t, count_ref), g)

    def send(i):
        pltpu.make_async_copy(g_ref.at[i], g_hbm.at[i], g_sems.at[i]).start()

    over_tiles(index_ref, count_ref, nothing, step, send)
    store_pairs(acc_ref, out_ref)

    def sent(i, carry):
        pltpu.make_async_copy(g_ref.at[i], g_hbm.at[i], g_sems.at[i]).wait()
        return carry

    lax.fori_loop(0, turns_of(count_ref), sent, 0)


def sum_of(refs):
    total = refs[0][...]
    for ref in refs[1:]:
        total = total + ref[...]
    return total


def column_kernel(index_ref, count_ref, *refs):
    r_refs = refs[0:4]
    m_ref, g_hbm, out_ref, w_ref, acc_ref, g_ref, sems = refs[4:]
    start_tiles(count_ref, g_hbm, g_ref, sems)
    acc_ref[...] = jnp.zeros_like(acc_ref)
    u = m_ref[...] / sum_of(r_refs)
    for row in range(TR):
        w_ref[row] = high_low(u[row : row + 1, :])

    def step(i, k, t, row, column):
        acc_ref[column] += jnp.dot(live(w_ref[row], t, count_ref), g_ref[i, k], preferred_element_type=f32)

    over_tiles(index_ref, count_ref, wait_tiles(g_hbm, g_ref, sems), step, nothing)
    store_pairs(acc_ref, out_ref)


def row_kernel(index_ref, count_ref, ca_ref, cb_ref, n_ref, g_hbm, out_ref, w_ref, acc_ref, g_ref, sems):
    start_tiles(count_ref, g_hbm, g_ref, sems)
    acc_ref[...] = jnp.zeros_like(acc_ref)
    v = n_ref[...] / (ca_ref[...] + cb_ref[...])
    for column in range(TC):
        w_ref[column] = high_low(v[column : column + 1, :])

    def step(i, k, t, row, column):
        acc_ref[row] += contract_last(live(w_ref[column], t, count_ref), g_ref[i, k])

    over_tiles(index_ref, count_ref, wait_tiles(g_hbm, g_ref, sems), step, nothing)
    store_pairs(acc_ref, out_ref)


def grad_kernel(index_ref, count_ref, pos_ref, *refs):
    r_refs, c_refs, m_ref, n_ref, g_hbm = (refs[0:4], refs[4:6], *refs[6:9])
    refs = refs[9:]
    xs, ys = (refs[0:4], refs[4:12])
    spec_outs, photo_outs, share_ref = (refs[12:16], refs[16:18], refs[18])
    xt_ref, yt_ref, u_ref, v_ref, wy_ref, vx_ref, spec_acc, photo_acc = refs[19:27]
    spec_ref, photo_ref, g_ref, sems, g_sems, out_sems = refs[27:]
    copies = piece_copies(xs, ys, xt_ref, yt_ref, sems)
    for copy in copies:
        copy.start()
    start_tiles(count_ref, g_hbm, g_ref, g_sems)
    u_all = m_ref[...] / sum_of(r_refs)
    total = sum_of(c_refs)
    v_all = n_ref[...] / total
    both_all = v_all * total
    for q in range(SLOTS):
        slot = spec_slot(q, pos_ref[0])
        for k in range(2):
            row = 2 * q + k
            u_ref[2 * slot + k] = jnp.broadcast_to(u_all[row : row + 1, :], (8, TILE))
    for q in range(SLOTS):
        slot = photo_slot(q, pos_ref[1])
        for k in range(4):
            column = 4 * q + k
            v_ref[4 * slot + k] = jnp.broadcast_to(v_all[column : column + 1, :], (8, TILE))

        @pl.when(slot == 0)
        def _():
            for k in range(4):
                share_ref[k] = jnp.broadcast_to(both_all[4 * q + k : 4 * q + k + 1, :], (8, TILE))

    spec_acc[...] = jnp.zeros_like(spec_acc)
    photo_acc[...] = jnp.zeros_like(photo_acc)
    for copy in copies:
        copy.wait()

    def ready_y(s, carry):
        for k in range(4):
            y = yt_ref[s, 0:F, k * TILE : (k + 1) * TILE].astype(f32)
            v = v_ref[4 * s + k][0:1, :]
            wy_ref[4 * s + k, 0:F, :] = (y * v).astype(bf16)
            wy_ref[4 * s + k, F:WROWS, :] = high_low(v)
        return carry

    def ready_x(s, carry):
        for k in range(2):
            x = xt_ref[s, 0:F, k * TILE : (k + 1) * TILE].astype(f32)
            vx_ref[2 * s + k] = (x * u_ref[2 * s + k][0:1, :]).astype(bf16)
        return carry

    lax.fori_loop(0, SLOTS, ready_y, 0)
    lax.fori_loop(0, SLOTS, ready_x, 0)

    def step(i, k, t, row, column):
        row_local = spec_slot(row >> 1, pos_ref[0]) * 2 + (row & 1)
        column_local = photo_slot(column >> 2, pos_ref[1]) * 4 + (column & 3)
        g = g_ref[i, k]
        spec_acc[row_local] += contract_last(live(wy_ref[column_local], t, count_ref), g)
        photo_acc[column_local] += jnp.dot(live(vx_ref[row_local], t, count_ref), g, preferred_element_type=f32)

    over_tiles(index_ref, count_ref, wait_tiles(g_hbm, g_ref, g_sems), step, nothing)

    def store_y(s, carry):
        for k in range(4):
            v = v_ref[4 * s + k][0:1, :]
            photo_ref[s, :, k * TILE : (k + 1) * TILE] = (photo_acc[4 * s + k] * v).astype(bf16)
        return carry

    def store_x(s, carry):
        for k in range(2):
            lanes = slice(k * TILE, (k + 1) * TILE)
            u = u_ref[2 * s + k][0:1, :]
            both = spec_acc[2 * s + k]
            spec_ref[s, 0:F, lanes] = (both[0:F, :] * u).astype(bf16)
            total = jnp.broadcast_to((both[F : F + 1, :] + both[F + 1 : F + 2, :]) * u, (8, TILE))
            spec_ref[s, F:EXT, lanes] = high_low_rows(total)
        return carry

    sends = []
    for h in (1, 0):
        lax.fori_loop(8 * h, 8 * h + 8, store_y, 0)
        sends.append(pltpu.make_async_copy(photo_ref.at[pl.ds(8 * h, 8)], photo_outs[h], out_sems.at[4 + h]))
        sends[-1].start()
    for h in range(4):
        lax.fori_loop(4 * h, 4 * h + 4, store_x, 0)
        sends.append(pltpu.make_async_copy(spec_ref.at[pl.ds(4 * h, 4)], spec_outs[h], out_sems.at[h]))
        sends[-1].start()
    for send in sends:
        send.wait()


def relay_kernel(a_ref, b_ref, c_ref, d_ref, own_ref, *send_refs):
    for k in range(4):
        parts = [ref[k].astype(f32) for ref in (a_ref, b_ref, c_ref, d_ref)]
        part = parts[0] + parts[1] + parts[2] + parts[3]
        if k == 0:
            own_ref[...] = part
            continue
        send_refs[k - 1][0:F, :] = part[0:F, :].astype(bf16)
        total = jnp.broadcast_to(part[F : F + 1, :] + part[F + 1 : F + 2, :], (8, SB))
        send_refs[k - 1][F:EXT, :] = high_low_rows(total)


SMEM = pl.BlockSpec(memory_space=pltpu.SMEM)
VMEM = pl.BlockSpec(memory_space=pltpu.VMEM)
ANY = pl.BlockSpec(memory_space=pl.ANY)
KEPT = pl.BlockSpec(memory_space=pltpu.VMEM)


def kept(shape, dtype):
    return pltpu.VMEM(shape, dtype)


def call(kernel, in_specs, outs, scratch, *args):
    return pl.pallas_call(
        kernel,
        in_specs=in_specs,
        out_specs=[spec for spec, _, _ in outs],
        out_shape=[kept(s, d) if spec is KEPT else jax.ShapeDtypeStruct(s, d) for spec, s, d in outs],
        scratch_shapes=scratch,
    )(*args)


def in_vmem(arrays):
    return [pltpu.with_memory_space_constraint(a, pltpu.VMEM) for a in arrays]


def per_device(spec_feat, photo_feat, spec_mass, photo_mass, tile_index, tile_count):
    photo_id = lax.axis_index("photo")
    spec_id = lax.axis_index("spec")
    meta = (
        tile_index.reshape(TMAX),
        tile_count.reshape(1),
        jnp.stack([photo_id, spec_id]).astype(jnp.int32),
    )
    x_own = spec_feat.T
    y_own = photo_feat[0].T
    x_pad = jnp.zeros((EXT - F - 1, SB), bf16)
    x0 = jnp.concatenate([x_own, spec_mass.reshape(1, SB), x_pad])[None]
    (y0,) = call(
        pack_kernel, [VMEM] * 2, [(VMEM, (1, EXT, PB), bf16)], [],
        y_own, photo_mass.reshape(1, PB),
    )
    x_flip = flip_z(x0)
    y_low = swap_low(y0)
    x0 = jnp.concatenate([x0, x_flip])
    x_mirror = mirror_z(x0)
    y0 = jnp.concatenate([y0, y_low])
    x0 = jnp.concatenate([x0, x_mirror])
    ys = [y0] + [shift_x(y0, k) for k in (1, 2, 3)]
    xs = [x0] + [shift_y(x0, k) for k in (1, 2, 3)]
    ys = ys + [swap_core(y) for y in ys]

    tiles = pltpu.VMEM((TURNS, GROUP, TILE, TILE), bf16)
    tile_sems = pltpu.SemaphoreType.DMA((TURNS,))
    row_acc = [pltpu.VMEM((TC, 16, TILE), bf16), pltpu.VMEM((TR, 16, TILE), f32)]
    column_acc = [pltpu.VMEM((TR, 16, TILE), bf16), pltpu.VMEM((TC, 16, TILE), f32)]
    blocks = [pltpu.VMEM((SLOTS, EXT, SB), bf16), pltpu.VMEM((SLOTS, EXT, PB), bf16)]
    piece_sems = pltpu.SemaphoreType.DMA((12,))
    r, m, n, g = call(
        first_kernel, [SMEM] * 3 + [ANY] * 12,
        [
            (KEPT, (TR, TILE), f32), (KEPT, (TR, TILE), f32), (KEPT, (TC, TILE), f32),
            (ANY, (TURNS, GROUP, TILE, TILE), bf16),
        ],
        blocks + [pltpu.VMEM((TR, TILE, F), bf16)] + row_acc + [tiles, piece_sems, tile_sems],
        *meta, *xs, *ys,
    )
    m, n = in_vmem([m, n])
    lists = meta[0:2]

    def columns(rs):
        return call(
            column_kernel, [SMEM] * 2 + [VMEM] * 5 + [ANY], [(KEPT, (TC, TILE), f32)],
            column_acc + [tiles, tile_sems], *lists, *rs, m, g,
        )[0]

    rs = in_vmem(sum_photo(r))
    cs = in_vmem(sum_spec(columns(rs)))
    (r,) = call(
        row_kernel, [SMEM] * 2 + [VMEM] * 3 + [ANY], [(KEPT, (TR, TILE), f32)],
        row_acc + [tiles, tile_sems], *lists, *cs, n, g,
    )
    rs = in_vmem(sum_photo(r))
    cs = in_vmem(sum_spec(columns(rs)))
    *parts, share = call(
        grad_kernel, [SMEM] * 3 + [VMEM] * 8 + [ANY] * 13,
        [(ANY, (4, EXT, SB), bf16)] * 4 + [(ANY, (8, F, PB), bf16)] * 2 + [(VMEM, (4, 8, TILE), f32)],
        blocks
        + [
            pltpu.VMEM((TR, 8, TILE), f32),
            pltpu.VMEM((TC, 8, TILE), f32),
            pltpu.VMEM((TC, WROWS, TILE), bf16),
            pltpu.VMEM((TR, F, TILE), bf16),
            pltpu.VMEM((TR, WROWS, TILE), f32),
            pltpu.VMEM((TC, F, TILE), f32),
            pltpu.VMEM((SLOTS, EXT, SB), bf16),
            pltpu.VMEM((SLOTS, F, PB), bf16),
            tiles, piece_sems, tile_sems,
            pltpu.SemaphoreType.DMA((6,)),
        ],
        *meta, *rs, *cs, m, n, g, *xs, *ys,
    )
    share = share[:, 0, :].reshape(1, PB)

    spec_parts, photo_parts = (parts[0:4], parts[4:6])
    far = swap_core(photo_parts[1])
    y_parts = [shift_y(spec_parts[k], -k) for k in (1, 2, 3)]
    photo_sums = [photo_parts[0][2 * k : 2 * k + 2].astype(f32) + far[2 * k : 2 * k + 2].astype(f32) for k in range(4)]
    x_parts = [total.astype(bf16) for total in photo_sums[1:]]
    x_parts = [shift_x(part, -k) for k, part in zip((1, 2, 3), x_parts)]

    spec_sum, *z_parts = call(
        relay_kernel, [VMEM] * 4, [(VMEM, (EXT, SB), f32)] + [(VMEM, (EXT, SB), bf16)] * 3, [],
        spec_parts[0], *in_vmem(y_parts),
    )
    z_parts = [move(part) for move, part in zip((flip_z, mirror_z, across_z), z_parts)]
    photo_sum = photo_sums[0]
    for part in x_parts:
        photo_sum = photo_sum + part.astype(f32)
    photo_send = photo_sum[1].astype(bf16)
    lowered = swap_low(photo_send)
    photo_sum = photo_sum[0] + lowered.astype(f32)
    grad_photo = (2.0 * (share * y_own.astype(f32) - photo_sum)).T[None]
    for part in z_parts:
        spec_sum = spec_sum + part.astype(f32)
    row_marginal = spec_sum[F : F + 1] + spec_sum[F + 1 : F + 2]
    grad_spec = (2.0 * (row_marginal * x_own.astype(f32) - spec_sum[0:F])).T
    return (grad_spec, grad_photo)


def solution(mesh):
    return jax.shard_map(
        per_device,
        mesh=mesh,
        in_specs=(
            P(("spec", "photo"), None),
            P("spec", "photo", None),
            P(("spec", "photo")),
            P("spec", "photo"),
            P("spec", "photo", None),
            P("spec", "photo"),
        ),
        out_specs=(P(("spec", "photo"), None), P("spec", "photo", None)),
        check_vma=False,
    )
```

```python
import math

import jax
import jax.numpy as jnp
from jax import lax
from jax.experimental import pallas as pl
from jax.experimental.pallas import tpu as pltpu
from jax.sharding import PartitionSpec as P


TILE = 256
TR = 32
TC = 64
F = 64
TMAX = 96
SB = 512
PB = 1024
EXT = 72
WROWS = 80
SLOTS = 16
GROUP = 8
TURNS = TMAX // GROUP
SCALE = 0.125 * math.log2(math.e)
f32 = jnp.float32
bf16 = jnp.bfloat16


def photo_perm(fy, fz):
    return [(y * 4 + z, fy(y) * 4 + fz(z)) for y in range(4) for z in range(4)]


def spec_perm(fl, fx, fc):
    return [
        (l * 8 + x * 2 + c, fl(l) * 8 + fx(x) * 2 + fc(c))
        for l in range(2)
        for x in range(4)
        for c in range(2)
    ]


def same(i):
    return i


def flip(i):
    return i ^ 1


def mirror(i):
    return 3 - i


def shift(k):
    return lambda i: (i + k) % 4


def shift_y(a, k):
    return lax.ppermute(a, "photo", photo_perm(shift(k), same))


def shift_z(a, k):
    return lax.ppermute(a, "photo", photo_perm(same, shift(k)))


def flip_z(a):
    return lax.ppermute(a, "photo", photo_perm(same, flip))


def across_z(a):
    return lax.ppermute(a, "photo", photo_perm(same, lambda i: i ^ 2))


def mirror_z(a):
    return lax.ppermute(a, "photo", photo_perm(same, mirror))


def shift_x(a, k):
    return lax.ppermute(a, "spec", spec_perm(same, shift(k), same))


def swap_core(a):
    return lax.ppermute(a, "spec", spec_perm(same, same, flip))


def swap_low(a):
    return lax.ppermute(a, "spec", spec_perm(flip, same, same))


def sum_photo(a):
    parts = [shift_y(a, k) for k in (1, 2, 3)]
    a = (a + parts[0]) + (parts[1] + parts[2])
    return [a] + [shift_z(a, k) for k in (1, 2, 3)]


def sum_spec(a):
    a = a + swap_core(a)
    parts = [
        lax.ppermute(a, "spec", spec_perm(fl, fx, same)) for fl, fx in ((flip, same), (same, flip), (flip, flip))
    ]
    a = (a + parts[0]) + (parts[1] + parts[2])
    return [a, lax.ppermute(a, "spec", spec_perm(same, mirror, same))]


def spec_slot(q, photo_id):
    across = (photo_id ^ q) & 3
    return (((photo_id >> 2) - (q >> 2)) & 3) * 4 + (across ^ (across >> 1))


def photo_slot(q, spec_id):
    low = ((spec_id >> 3) - (q >> 3)) & 1
    across = ((spec_id >> 1) - (q >> 1)) & 3
    core = (spec_id - q) & 1
    return core * 8 + across * 2 + low


def entry_of(index_ref, t, last):
    entry = index_ref[jnp.minimum(t, last)]
    return ((entry >> 6) & 31, entry & 63)


def live(value, t, count_ref):
    return value * (t < count_ref[0]).astype(value.dtype)


def contract_last(a, b):
    return lax.dot_general(a, b, (((1,), (1,)), ((), ())), preferred_element_type=f32)


def high_low_rows(value):
    high = value.astype(bf16).astype(f32)
    sub = lax.broadcasted_iota(jnp.int32, value.shape, 0)
    return jnp.where(sub == 0, high, jnp.where(sub == 1, value - high, 0.0)).astype(bf16)


def high_low(value):
    return high_low_rows(jnp.broadcast_to(value, (16, value.shape[1])))


def turns_of(count_ref):
    return (count_ref[0] + GROUP - 1) // GROUP


def over_tiles(index_ref, count_ref, before, step, after):
    last = count_ref[0] - 1

    def turn(i, carry):
        before(i)
        for k in range(GROUP):
            row, column = entry_of(index_ref, i * GROUP + k, last)
            step(i, k, i * GROUP + k, row, column)
        after(i)
        return carry

    lax.fori_loop(0, turns_of(count_ref), turn, 0)


def start_tiles(count_ref, g_hbm, g_ref, sems):
    def turn(i, carry):
        pltpu.make_async_copy(g_hbm.at[i], g_ref.at[i], sems.at[i]).start()
        return carry

    lax.fori_loop(0, turns_of(count_ref), turn, 0)


def wait_tiles(g_hbm, g_ref, sems):
    return lambda i: pltpu.make_async_copy(g_hbm.at[i], g_ref.at[i], sems.at[i]).wait()


def nothing(i):
    pass


def store_pairs(acc_ref, out_ref):
    for i in range(out_ref.shape[0]):
        both = acc_ref[i]
        out_ref[i : i + 1, :] = both[0:1, :] + both[1:2, :]


def piece_copies(xs, ys, xt_ref, yt_ref, sems):
    copies = [pltpu.make_async_copy(xs[k], xt_ref.at[pl.ds(4 * k, 4)], sems.at[k]) for k in range(4)]
    return copies + [
        pltpu.make_async_copy(ys[k], yt_ref.at[pl.ds(2 * k, 2)], sems.at[4 + k]) for k in range(8)
    ]


def pack_kernel(y_ref, mass_ref, out_ref):
    y = y_ref[...].astype(f32)
    weight = jnp.exp(jnp.sum(y * y, axis=0, keepdims=True) * -0.0625)
    high = weight.astype(bf16).astype(f32)
    sub = lax.broadcasted_iota(jnp.int32, (8, PB), 0)
    block = jnp.where(sub == 0, mass_ref[...].astype(f32), 0.0)
    block = jnp.where(sub == 1, high, jnp.where(sub == 2, weight - high, block))
    out_ref[0, 0:F, :] = y_ref[...]
    out_ref[0, F:EXT, :] = block.astype(bf16)


def first_kernel(index_ref, count_ref, pos_ref, *refs):
    xs, ys = (refs[0:4], refs[4:12])
    out_ref, m_ref, n_ref, g_hbm = refs[12:16]
    xt_ref, yt_ref, xr_ref, w_ref, acc_ref, g_ref, sems, g_sems = refs[16:]
    copies = piece_copies(xs, ys, xt_ref, yt_ref, sems)
    for copy in copies:
        copy.start()
    acc_ref[...] = jnp.zeros_like(acc_ref)
    for copy in copies:
        copy.wait()
    for q in range(SLOTS):
        rows = yt_ref[photo_slot(q, pos_ref[1]), F:EXT, :].astype(f32)
        for k in range(4):
            lanes = slice(k * TILE, (k + 1) * TILE)
            n_ref[4 * q + k : 4 * q + k + 1, :] = rows[0:1, lanes]
            sub = lax.broadcasted_iota(jnp.int32, (16, TILE), 0)
            pair = jnp.where(sub == 0, rows[1:2, lanes], jnp.where(sub == 1, rows[2:3, lanes], 0.0))
            w_ref[4 * q + k] = pair.astype(bf16)

    def turn_slot(s, carry):
        for h in range(2):
            xr_ref[2 * s + h] = jnp.transpose(xt_ref[s, 0:F, h * TILE : (h + 1) * TILE])
        return carry

    lax.fori_loop(0, SLOTS, turn_slot, 0)

    for q in range(SLOTS):
        mass = xt_ref[spec_slot(q, pos_ref[0]), F:EXT, :].astype(f32)
        for k in range(2):
            m_ref[2 * q + k : 2 * q + k + 1, :] = mass[0:1, k * TILE : (k + 1) * TILE]

    def step(i, k, t, row, column):
        row_local = spec_slot(row >> 1, pos_ref[0]) * 2 + (row & 1)
        slot = photo_slot(column >> 2, pos_ref[1])
        lane = pl.multiple_of((column & 3) * TILE, TILE)
        y = yt_ref[slot, 0:F, pl.ds(lane, TILE)]
        cross = jnp.dot(xr_ref[row_local], y, preferred_element_type=f32)
        g = jnp.exp2(cross * SCALE).astype(bf16)
        g_ref[i, k] = g
        acc_ref[row] += contract_last(live(w_ref[column], t, count_ref), g)

    def send(i):
        pltpu.make_async_copy(g_ref.at[i], g_hbm.at[i], g_sems.at[i]).start()

    over_tiles(index_ref, count_ref, nothing, step, send)
    store_pairs(acc_ref, out_ref)

    def sent(i, carry):
        pltpu.make_async_copy(g_ref.at[i], g_hbm.at[i], g_sems.at[i]).wait()
        return carry

    lax.fori_loop(0, turns_of(count_ref), sent, 0)


def sum_of(refs):
    total = refs[0][...]
    for ref in refs[1:]:
        total = total + ref[...]
    return total


def column_kernel(index_ref, count_ref, *refs):
    r_refs = refs[0:4]
    m_ref, g_hbm, out_ref, w_ref, acc_ref, g_ref, sems = refs[4:]
    start_tiles(count_ref, g_hbm, g_ref, sems)
    acc_ref[...] = jnp.zeros_like(acc_ref)
    u = m_ref[...] / sum_of(r_refs)
    for row in range(TR):
        w_ref[row] = high_low(u[row : row + 1, :])

    def step(i, k, t, row, column):
        acc_ref[column] += jnp.dot(live(w_ref[row], t, count_ref), g_ref[i, k], preferred_element_type=f32)

    over_tiles(index_ref, count_ref, wait_tiles(g_hbm, g_ref, sems), step, nothing)
    store_pairs(acc_ref, out_ref)


def row_kernel(index_ref, count_ref, ca_ref, cb_ref, n_ref, g_hbm, out_ref, w_ref, acc_ref, g_ref, sems):
    start_tiles(count_ref, g_hbm, g_ref, sems)
    acc_ref[...] = jnp.zeros_like(acc_ref)
    v = n_ref[...] / (ca_ref[...] + cb_ref[...])
    for column in range(TC):
        w_ref[column] = high_low(v[column : column + 1, :])

    def step(i, k, t, row, column):
        acc_ref[row] += contract_last(live(w_ref[column], t, count_ref), g_ref[i, k])

    over_tiles(index_ref, count_ref, wait_tiles(g_hbm, g_ref, sems), step, nothing)
    store_pairs(acc_ref, out_ref)


def grad_kernel(index_ref, count_ref, pos_ref, *refs):
    r_refs, c_refs, m_ref, n_ref, g_hbm = (refs[0:4], refs[4:6], *refs[6:9])
    refs = refs[9:]
    xs, ys = (refs[0:4], refs[4:12])
    spec_outs, photo_outs, share_ref = (refs[12:16], refs[16:18], refs[18])
    xt_ref, yt_ref, u_ref, v_ref, wy_ref, vx_ref, spec_acc, photo_acc = refs[19:27]
    g_ref, sems, g_sems = refs[27:]
    copies = piece_copies(xs, ys, xt_ref, yt_ref, sems)
    for copy in copies:
        copy.start()
    start_tiles(count_ref, g_hbm, g_ref, g_sems)
    u_all = m_ref[...] / sum_of(r_refs)
    total = sum_of(c_refs)
    v_all = n_ref[...] / total
    both_all = v_all * total
    for q in range(SLOTS):
        slot = spec_slot(q, pos_ref[0])
        for k in range(2):
            row = 2 * q + k
            u_ref[2 * slot + k] = jnp.broadcast_to(u_all[row : row + 1, :], (8, TILE))
    for q in range(SLOTS):
        slot = photo_slot(q, pos_ref[1])
        for k in range(4):
            column = 4 * q + k
            v_ref[4 * slot + k] = jnp.broadcast_to(v_all[column : column + 1, :], (8, TILE))

        @pl.when(slot == 0)
        def _():
            for k in range(4):
                share_ref[k] = jnp.broadcast_to(both_all[4 * q + k : 4 * q + k + 1, :], (8, TILE))

    spec_acc[...] = jnp.zeros_like(spec_acc)
    photo_acc[...] = jnp.zeros_like(photo_acc)
    for copy in copies:
        copy.wait()

    def ready_y(s, carry):
        for k in range(4):
            y = yt_ref[s, 0:F, k * TILE : (k + 1) * TILE].astype(f32)
            v = v_ref[4 * s + k][0:1, :]
            wy_ref[4 * s + k, 0:F, :] = (y * v).astype(bf16)
            wy_ref[4 * s + k, F:WROWS, :] = high_low(v)
        return carry

    def ready_x(s, carry):
        for k in range(2):
            x = xt_ref[s, 0:F, k * TILE : (k + 1) * TILE].astype(f32)
            vx_ref[2 * s + k] = (x * u_ref[2 * s + k][0:1, :]).astype(bf16)
        return carry

    lax.fori_loop(0, SLOTS, ready_y, 0)
    lax.fori_loop(0, SLOTS, ready_x, 0)

    def step(i, k, t, row, column):
        row_local = spec_slot(row >> 1, pos_ref[0]) * 2 + (row & 1)
        column_local = photo_slot(column >> 2, pos_ref[1]) * 4 + (column & 3)
        g = g_ref[i, k]
        spec_acc[row_local] += contract_last(live(wy_ref[column_local], t, count_ref), g)
        photo_acc[column_local] += jnp.dot(live(vx_ref[row_local], t, count_ref), g, preferred_element_type=f32)

    over_tiles(index_ref, count_ref, wait_tiles(g_hbm, g_ref, g_sems), step, nothing)

    def store_y(h):
        def store(j, carry):
            for k in range(4):
                tile = 32 * h + 4 * j + k
                v = v_ref[tile][0:1, :]
                photo_outs[h][j, :, k * TILE : (k + 1) * TILE] = (photo_acc[tile] * v).astype(bf16)
            return carry

        lax.fori_loop(0, 8, store, 0)

    def store_x(h):
        def store(j, carry):
            for k in range(2):
                lanes = slice(k * TILE, (k + 1) * TILE)
                tile = 8 * h + 2 * j + k
                u = u_ref[tile][0:1, :]
                both = spec_acc[tile]
                spec_outs[h][j, 0:F, lanes] = (both[0:F, :] * u).astype(bf16)
                total = jnp.broadcast_to((both[F : F + 1, :] + both[F + 1 : F + 2, :]) * u, (8, TILE))
                spec_outs[h][j, F:EXT, lanes] = high_low_rows(total)
            return carry

        lax.fori_loop(0, 4, store, 0)

    for h in range(2):
        store_y(h)
    for h in range(4):
        store_x(h)


def relay_kernel(a_ref, b_ref, c_ref, d_ref, own_ref, *send_refs):
    for k in range(4):
        parts = [ref[k].astype(f32) for ref in (a_ref, b_ref, c_ref, d_ref)]
        part = parts[0] + parts[1] + parts[2] + parts[3]
        if k == 0:
            own_ref[...] = part
            continue
        send_refs[k - 1][0:F, :] = part[0:F, :].astype(bf16)
        total = jnp.broadcast_to(part[F : F + 1, :] + part[F + 1 : F + 2, :], (8, SB))
        send_refs[k - 1][F:EXT, :] = high_low_rows(total)


SMEM = pl.BlockSpec(memory_space=pltpu.SMEM)
VMEM = pl.BlockSpec(memory_space=pltpu.VMEM)
ANY = pl.BlockSpec(memory_space=pl.ANY)
KEPT = pl.BlockSpec(memory_space=pltpu.VMEM)


def kept(shape, dtype):
    return pltpu.VMEM(shape, dtype)


def call(kernel, in_specs, outs, scratch, *args):
    return pl.pallas_call(
        kernel,
        in_specs=in_specs,
        out_specs=[spec for spec, _, _ in outs],
        out_shape=[kept(s, d) if spec is KEPT else jax.ShapeDtypeStruct(s, d) for spec, s, d in outs],
        scratch_shapes=scratch,
        compiler_params=pltpu.CompilerParams(vmem_limit_bytes=40 << 20),
    )(*args)


def in_vmem(arrays):
    return [pltpu.with_memory_space_constraint(a, pltpu.VMEM) for a in arrays]


def per_device(spec_feat, photo_feat, spec_mass, photo_mass, tile_index, tile_count):
    photo_id = lax.axis_index("photo")
    spec_id = lax.axis_index("spec")
    meta = (
        tile_index.reshape(TMAX),
        tile_count.reshape(1),
        jnp.stack([photo_id, spec_id]).astype(jnp.int32),
    )
    x_own = spec_feat.T
    y_own = photo_feat[0].T
    x_pad = jnp.zeros((EXT - F - 1, SB), bf16)
    x0 = jnp.concatenate([x_own, spec_mass.reshape(1, SB), x_pad])[None]
    (y0,) = call(
        pack_kernel, [VMEM] * 2, [(KEPT, (1, EXT, PB), bf16)], [],
        y_own, photo_mass.reshape(1, PB),
    )
    x_flip = flip_z(x0)
    y_low = swap_low(y0)
    x0 = jnp.concatenate([x0, x_flip])
    x_mirror = mirror_z(x0)
    y0 = jnp.concatenate([y0, y_low])
    x0 = jnp.concatenate([x0, x_mirror])
    ys = [y0] + [shift_x(y0, k) for k in (1, 2, 3)]
    xs = [x0] + [shift_y(x0, k) for k in (1, 2, 3)]
    ys = ys + [swap_core(y) for y in ys]

    tiles = pltpu.VMEM((TURNS, GROUP, TILE, TILE), bf16)
    tile_sems = pltpu.SemaphoreType.DMA((TURNS,))
    row_acc = [pltpu.VMEM((TC, 16, TILE), bf16), pltpu.VMEM((TR, 16, TILE), f32)]
    column_acc = [pltpu.VMEM((TR, 16, TILE), bf16), pltpu.VMEM((TC, 16, TILE), f32)]
    blocks = [pltpu.VMEM((SLOTS, EXT, SB), bf16), pltpu.VMEM((SLOTS, EXT, PB), bf16)]
    piece_sems = pltpu.SemaphoreType.DMA((12,))
    r, m, n, g = call(
        first_kernel, [SMEM] * 3 + [ANY] * 12,
        [
            (KEPT, (TR, TILE), f32), (KEPT, (TR, TILE), f32), (KEPT, (TC, TILE), f32),
            (ANY, (TURNS, GROUP, TILE, TILE), bf16),
        ],
        blocks + [pltpu.VMEM((TR, TILE, F), bf16)] + row_acc + [tiles, piece_sems, tile_sems],
        *meta, *xs, *ys,
    )
    m, n = in_vmem([m, n])
    lists = meta[0:2]

    def columns(rs):
        return call(
            column_kernel, [SMEM] * 2 + [VMEM] * 5 + [ANY], [(KEPT, (TC, TILE), f32)],
            column_acc + [tiles, tile_sems], *lists, *rs, m, g,
        )[0]

    rs = in_vmem(sum_photo(r))
    cs = in_vmem(sum_spec(columns(rs)))
    (r,) = call(
        row_kernel, [SMEM] * 2 + [VMEM] * 3 + [ANY], [(KEPT, (TR, TILE), f32)],
        row_acc + [tiles, tile_sems], *lists, *cs, n, g,
    )
    rs = in_vmem(sum_photo(r))
    cs = in_vmem(sum_spec(columns(rs)))
    *parts, share = call(
        grad_kernel, [SMEM] * 3 + [VMEM] * 8 + [ANY] * 13,
        [(KEPT, (4, EXT, SB), bf16)] * 4 + [(KEPT, (8, F, PB), bf16)] * 2 + [(KEPT, (4, 8, TILE), f32)],
        blocks
        + [
            pltpu.VMEM((TR, 8, TILE), f32),
            pltpu.VMEM((TC, 8, TILE), f32),
            pltpu.VMEM((TC, WROWS, TILE), bf16),
            pltpu.VMEM((TR, F, TILE), bf16),
            pltpu.VMEM((TR, WROWS, TILE), f32),
            pltpu.VMEM((TC, F, TILE), f32),
            tiles, piece_sems, tile_sems,
        ],
        *meta, *rs, *cs, m, n, g, *xs, *ys,
    )
    share = share[:, 0, :].reshape(1, PB)

    spec_parts, photo_parts = (parts[0:4], parts[4:6])
    far = swap_core(photo_parts[1])
    y_parts = [shift_y(spec_parts[k], -k) for k in (1, 2, 3)]
    photo_sums = [photo_parts[0][2 * k : 2 * k + 2].astype(f32) + far[2 * k : 2 * k + 2].astype(f32) for k in range(4)]
    x_parts = [total.astype(bf16) for total in photo_sums[1:]]
    x_parts = [shift_x(part, -k) for k, part in zip((1, 2, 3), x_parts)]

    spec_sum, *z_parts = call(
        relay_kernel, [VMEM] * 4, [(KEPT, (EXT, SB), f32)] + [(KEPT, (EXT, SB), bf16)] * 3, [],
        spec_parts[0], *in_vmem(y_parts),
    )
    z_parts = [move(part) for move, part in zip((flip_z, mirror_z, across_z), z_parts)]
    photo_sum = photo_sums[0]
    for part in x_parts:
        photo_sum = photo_sum + part.astype(f32)
    photo_send = photo_sum[1].astype(bf16)
    lowered = swap_low(photo_send)
    photo_sum = photo_sum[0] + lowered.astype(f32)
    grad_photo = (2.0 * (share * y_own.astype(f32) - photo_sum)).T[None]
    for part in z_parts:
        spec_sum = spec_sum + part.astype(f32)
    row_marginal = spec_sum[F : F + 1] + spec_sum[F + 1 : F + 2]
    grad_spec = (2.0 * (row_marginal * x_own.astype(f32) - spec_sum[0:F])).T
    return (grad_spec, grad_photo)


def solution(mesh):
    return jax.shard_map(
        per_device,
        mesh=mesh,
        in_specs=(
            P(("spec", "photo"), None),
            P("spec", "photo", None),
            P(("spec", "photo")),
            P("spec", "photo"),
            P("spec", "photo", None),
            P("spec", "photo"),
        ),
        out_specs=(P(("spec", "photo"), None), P("spec", "photo", None)),
        check_vma=False,
    )
```

```python
import math

import jax
import jax.numpy as jnp
from jax import lax
from jax.experimental import pallas as pl
from jax.experimental.pallas import tpu as pltpu
from jax.sharding import PartitionSpec as P


TILE = 256
TR = 32
TC = 64
F = 64
TMAX = 96
SB = 512
PB = 1024
EXT = 72
WROWS = 80
SLOTS = 16
GROUP = 8
TURNS = TMAX // GROUP
SCALE = 0.125 * math.log2(math.e)
f32 = jnp.float32
bf16 = jnp.bfloat16


def photo_perm(fy, fz):
    return [(y * 4 + z, fy(y) * 4 + fz(z)) for y in range(4) for z in range(4)]


def spec_perm(fl, fx, fc):
    return [
        (l * 8 + x * 2 + c, fl(l) * 8 + fx(x) * 2 + fc(c))
        for l in range(2)
        for x in range(4)
        for c in range(2)
    ]


def same(i):
    return i


def flip(i):
    return i ^ 1


def mirror(i):
    return 3 - i


def shift(k):
    return lambda i: (i + k) % 4


def shift_y(a, k):
    return lax.ppermute(a, "photo", photo_perm(shift(k), same))


def shift_z(a, k):
    return lax.ppermute(a, "photo", photo_perm(same, shift(k)))


def flip_z(a):
    return lax.ppermute(a, "photo", photo_perm(same, flip))


def across_z(a):
    return lax.ppermute(a, "photo", photo_perm(same, lambda i: i ^ 2))


def mirror_z(a):
    return lax.ppermute(a, "photo", photo_perm(same, mirror))


def shift_x(a, k):
    return lax.ppermute(a, "spec", spec_perm(same, shift(k), same))


def swap_core(a):
    return lax.ppermute(a, "spec", spec_perm(same, same, flip))


def swap_low(a):
    return lax.ppermute(a, "spec", spec_perm(flip, same, same))


def sum_photo(a):
    parts = [shift_y(a, k) for k in (1, 2, 3)]
    a = (a + parts[0]) + (parts[1] + parts[2])
    return [a] + [shift_z(a, k) for k in (1, 2, 3)]


def sum_spec(a):
    a = a + swap_core(a)
    parts = [
        lax.ppermute(a, "spec", spec_perm(fl, fx, same)) for fl, fx in ((flip, same), (same, flip), (flip, flip))
    ]
    a = (a + parts[0]) + (parts[1] + parts[2])
    return [a, lax.ppermute(a, "spec", spec_perm(same, mirror, same))]


def spec_slot(q, photo_id):
    across = (photo_id ^ q) & 3
    return (((photo_id >> 2) - (q >> 2)) & 3) * 4 + (across ^ (across >> 1))


def photo_slot(q, spec_id):
    low = ((spec_id >> 3) - (q >> 3)) & 1
    across = ((spec_id >> 1) - (q >> 1)) & 3
    core = (spec_id - q) & 1
    return core * 8 + across * 2 + low


def entry_of(index_ref, t, last):
    entry = index_ref[jnp.minimum(t, last)]
    return ((entry >> 6) & 31, entry & 63)


def live(value, t, count_ref):
    return value * (t < count_ref[0]).astype(value.dtype)


def contract_last(a, b):
    return lax.dot_general(a, b, (((1,), (1,)), ((), ())), preferred_element_type=f32)


def high_low_rows(value):
    high = value.astype(bf16).astype(f32)
    sub = lax.broadcasted_iota(jnp.int32, value.shape, 0)
    return jnp.where(sub == 0, high, jnp.where(sub == 1, value - high, 0.0)).astype(bf16)


def high_low(value):
    return high_low_rows(jnp.broadcast_to(value, (16, value.shape[1])))


def turns_of(count_ref):
    return (count_ref[0] + GROUP - 1) // GROUP


def over_tiles(index_ref, count_ref, step):
    last = count_ref[0] - 1

    def turn(i, carry):
        for k in range(GROUP):
            row, column = entry_of(index_ref, i * GROUP + k, last)
            step(i, k, i * GROUP + k, row, column)
        return carry

    lax.fori_loop(0, turns_of(count_ref), turn, 0)


def store_pairs(acc_ref, out_ref):
    for i in range(out_ref.shape[0]):
        both = acc_ref[i]
        out_ref[i : i + 1, :] = both[0:1, :] + both[1:2, :]


def piece_copies(xs, ys, xt_ref, yt_ref, sems):
    copies = [pltpu.make_async_copy(xs[k], xt_ref.at[pl.ds(4 * k, 4)], sems.at[k]) for k in range(4)]
    return copies + [
        pltpu.make_async_copy(ys[k], yt_ref.at[pl.ds(2 * k, 2)], sems.at[4 + k]) for k in range(8)
    ]


def pack_kernel(y_ref, mass_ref, out_ref):
    y = y_ref[...].astype(f32)
    weight = jnp.exp(jnp.sum(y * y, axis=0, keepdims=True) * -0.0625)
    high = weight.astype(bf16).astype(f32)
    sub = lax.broadcasted_iota(jnp.int32, (8, PB), 0)
    block = jnp.where(sub == 0, mass_ref[...].astype(f32), 0.0)
    block = jnp.where(sub == 1, high, jnp.where(sub == 2, weight - high, block))
    out_ref[0, 0:F, :] = y_ref[...]
    out_ref[0, F:EXT, :] = block.astype(bf16)


def first_kernel(index_ref, count_ref, pos_ref, *refs):
    xs, ys = (refs[0:4], refs[4:12])
    out_ref, m_ref, n_ref, g_ref = refs[12:16]
    xt_ref, yt_ref, xr_ref, w_ref, acc_ref, sems = refs[16:]
    copies = piece_copies(xs, ys, xt_ref, yt_ref, sems)
    for copy in copies:
        copy.start()
    acc_ref[...] = jnp.zeros_like(acc_ref)
    for copy in copies:
        copy.wait()
    for q in range(SLOTS):
        rows = yt_ref[photo_slot(q, pos_ref[1]), F:EXT, :].astype(f32)
        for k in range(4):
            lanes = slice(k * TILE, (k + 1) * TILE)
            n_ref[4 * q + k : 4 * q + k + 1, :] = rows[0:1, lanes]
            sub = lax.broadcasted_iota(jnp.int32, (16, TILE), 0)
            pair = jnp.where(sub == 0, rows[1:2, lanes], jnp.where(sub == 1, rows[2:3, lanes], 0.0))
            w_ref[4 * q + k] = pair.astype(bf16)

    def turn_slot(s, carry):
        for h in range(2):
            xr_ref[2 * s + h] = jnp.transpose(xt_ref[s, 0:F, h * TILE : (h + 1) * TILE])
        return carry

    lax.fori_loop(0, SLOTS, turn_slot, 0)

    for q in range(SLOTS):
        mass = xt_ref[spec_slot(q, pos_ref[0]), F:EXT, :].astype(f32)
        for k in range(2):
            m_ref[2 * q + k : 2 * q + k + 1, :] = mass[0:1, k * TILE : (k + 1) * TILE]

    def step(i, k, t, row, column):
        row_local = spec_slot(row >> 1, pos_ref[0]) * 2 + (row & 1)
        slot = photo_slot(column >> 2, pos_ref[1])
        lane = pl.multiple_of((column & 3) * TILE, TILE)
        y = yt_ref[slot, 0:F, pl.ds(lane, TILE)]
        cross = jnp.dot(xr_ref[row_local], y, preferred_element_type=f32)
        g = jnp.exp2(cross * SCALE).astype(bf16)
        g_ref[i, k] = g
        acc_ref[row] += contract_last(live(w_ref[column], t, count_ref), g)

    over_tiles(index_ref, count_ref, step)
    store_pairs(acc_ref, out_ref)


def sum_of(refs):
    total = refs[0][...]
    for ref in refs[1:]:
        total = total + ref[...]
    return total


def column_kernel(index_ref, count_ref, *refs):
    r_refs = refs[0:4]
    m_ref, g_ref, out_ref, w_ref, acc_ref = refs[4:]
    acc_ref[...] = jnp.zeros_like(acc_ref)
    u = m_ref[...] / sum_of(r_refs)
    for row in range(TR):
        w_ref[row] = high_low(u[row : row + 1, :])

    def step(i, k, t, row, column):
        acc_ref[column] += jnp.dot(live(w_ref[row], t, count_ref), g_ref[i, k], preferred_element_type=f32)

    over_tiles(index_ref, count_ref, step)
    store_pairs(acc_ref, out_ref)


def row_kernel(index_ref, count_ref, ca_ref, cb_ref, n_ref, g_ref, out_ref, w_ref, acc_ref):
    acc_ref[...] = jnp.zeros_like(acc_ref)
    v = n_ref[...] / (ca_ref[...] + cb_ref[...])
    for column in range(TC):
        w_ref[column] = high_low(v[column : column + 1, :])

    def step(i, k, t, row, column):
        acc_ref[row] += contract_last(live(w_ref[column], t, count_ref), g_ref[i, k])

    over_tiles(index_ref, count_ref, step)
    store_pairs(acc_ref, out_ref)


def grad_kernel(index_ref, count_ref, pos_ref, *refs):
    r_refs, c_refs, m_ref, n_ref, g_ref = (refs[0:4], refs[4:6], *refs[6:9])
    refs = refs[9:]
    xs, ys = (refs[0:4], refs[4:12])
    spec_outs, photo_outs, share_ref = (refs[12:16], refs[16:18], refs[18])
    xt_ref, yt_ref, u_ref, v_ref, wy_ref, vx_ref, spec_acc, photo_acc = refs[19:27]
    (sems,) = refs[27:]
    copies = piece_copies(xs, ys, xt_ref, yt_ref, sems)
    for copy in copies:
        copy.start()
    u_all = m_ref[...] / sum_of(r_refs)
    total = sum_of(c_refs)
    v_all = n_ref[...] / total
    both_all = v_all * total
    for q in range(SLOTS):
        slot = spec_slot(q, pos_ref[0])
        for k in range(2):
            row = 2 * q + k
            u_ref[2 * slot + k] = jnp.broadcast_to(u_all[row : row + 1, :], (8, TILE))
    for q in range(SLOTS):
        slot = photo_slot(q, pos_ref[1])
        for k in range(4):
            column = 4 * q + k
            v_ref[4 * slot + k] = jnp.broadcast_to(v_all[column : column + 1, :], (8, TILE))

        @pl.when(slot == 0)
        def _():
            for k in range(4):
                share_ref[k] = jnp.broadcast_to(both_all[4 * q + k : 4 * q + k + 1, :], (8, TILE))

    spec_acc[...] = jnp.zeros_like(spec_acc)
    photo_acc[...] = jnp.zeros_like(photo_acc)
    for copy in copies:
        copy.wait()

    def ready_y(s, carry):
        for k in range(4):
            y = yt_ref[s, 0:F, k * TILE : (k + 1) * TILE].astype(f32)
            v = v_ref[4 * s + k][0:1, :]
            wy_ref[4 * s + k, 0:F, :] = (y * v).astype(bf16)
            wy_ref[4 * s + k, F:WROWS, :] = high_low(v)
        return carry

    def ready_x(s, carry):
        for k in range(2):
            x = xt_ref[s, 0:F, k * TILE : (k + 1) * TILE].astype(f32)
            vx_ref[2 * s + k] = (x * u_ref[2 * s + k][0:1, :]).astype(bf16)
        return carry

    lax.fori_loop(0, SLOTS, ready_y, 0)
    lax.fori_loop(0, SLOTS, ready_x, 0)

    def step(i, k, t, row, column):
        row_local = spec_slot(row >> 1, pos_ref[0]) * 2 + (row & 1)
        column_local = photo_slot(column >> 2, pos_ref[1]) * 4 + (column & 3)
        g = g_ref[i, k]
        spec_acc[row_local] += contract_last(live(wy_ref[column_local], t, count_ref), g)
        photo_acc[column_local] += jnp.dot(live(vx_ref[row_local], t, count_ref), g, preferred_element_type=f32)

    over_tiles(index_ref, count_ref, step)

    def store_y(h):
        def store(j, carry):
            for k in range(4):
                tile = 32 * h + 4 * j + k
                v = v_ref[tile][0:1, :]
                photo_outs[h][j, :, k * TILE : (k + 1) * TILE] = (photo_acc[tile] * v).astype(bf16)
            return carry

        lax.fori_loop(0, 8, store, 0)

    def store_x(h):
        def store(j, carry):
            for k in range(2):
                lanes = slice(k * TILE, (k + 1) * TILE)
                tile = 8 * h + 2 * j + k
                u = u_ref[tile][0:1, :]
                both = spec_acc[tile]
                spec_outs[h][j, 0:F, lanes] = (both[0:F, :] * u).astype(bf16)
                total = jnp.broadcast_to((both[F : F + 1, :] + both[F + 1 : F + 2, :]) * u, (8, TILE))
                spec_outs[h][j, F:EXT, lanes] = high_low_rows(total)
            return carry

        lax.fori_loop(0, 4, store, 0)

    for h in range(2):
        store_y(h)
    for h in range(4):
        store_x(h)


def relay_kernel(a_ref, b_ref, c_ref, d_ref, own_ref, *send_refs):
    for k in range(4):
        parts = [ref[k].astype(f32) for ref in (a_ref, b_ref, c_ref, d_ref)]
        part = parts[0] + parts[1] + parts[2] + parts[3]
        if k == 0:
            own_ref[...] = part
            continue
        send_refs[k - 1][0:F, :] = part[0:F, :].astype(bf16)
        total = jnp.broadcast_to(part[F : F + 1, :] + part[F + 1 : F + 2, :], (8, SB))
        send_refs[k - 1][F:EXT, :] = high_low_rows(total)


SMEM = pl.BlockSpec(memory_space=pltpu.SMEM)
VMEM = pl.BlockSpec(memory_space=pltpu.VMEM)
ANY = pl.BlockSpec(memory_space=pl.ANY)
KEPT = pl.BlockSpec(memory_space=pltpu.VMEM)


def kept(shape, dtype):
    return pltpu.VMEM(shape, dtype)


def call(kernel, in_specs, outs, scratch, *args):
    return pl.pallas_call(
        kernel,
        in_specs=in_specs,
        out_specs=[spec for spec, _, _ in outs],
        out_shape=[kept(s, d) if spec is KEPT else jax.ShapeDtypeStruct(s, d) for spec, s, d in outs],
        scratch_shapes=scratch,
        compiler_params=pltpu.CompilerParams(vmem_limit_bytes=18 << 20),
    )(*args)


def in_vmem(arrays):
    return [pltpu.with_memory_space_constraint(a, pltpu.VMEM) for a in arrays]


def per_device(spec_feat, photo_feat, spec_mass, photo_mass, tile_index, tile_count):
    photo_id = lax.axis_index("photo")
    spec_id = lax.axis_index("spec")
    meta = (
        tile_index.reshape(TMAX),
        tile_count.reshape(1),
        jnp.stack([photo_id, spec_id]).astype(jnp.int32),
    )
    x_own = spec_feat.T
    y_own = photo_feat[0].T
    x_pad = jnp.zeros((EXT - F - 1, SB), bf16)
    x0 = jnp.concatenate([x_own, spec_mass.reshape(1, SB), x_pad])[None]
    (y0,) = call(
        pack_kernel, [VMEM] * 2, [(KEPT, (1, EXT, PB), bf16)], [],
        y_own, photo_mass.reshape(1, PB),
    )
    x_flip = flip_z(x0)
    y_low = swap_low(y0)
    x0 = jnp.concatenate([x0, x_flip])
    x_mirror = mirror_z(x0)
    y0 = jnp.concatenate([y0, y_low])
    x0 = jnp.concatenate([x0, x_mirror])
    ys = [y0] + [shift_x(y0, k) for k in (1, 2, 3)]
    xs = [x0] + [shift_y(x0, k) for k in (1, 2, 3)]
    ys = ys + [swap_core(y) for y in ys]

    row_acc = [pltpu.VMEM((TC, 16, TILE), bf16), pltpu.VMEM((TR, 16, TILE), f32)]
    column_acc = [pltpu.VMEM((TR, 16, TILE), bf16), pltpu.VMEM((TC, 16, TILE), f32)]
    blocks = [pltpu.VMEM((SLOTS, EXT, SB), bf16), pltpu.VMEM((SLOTS, EXT, PB), bf16)]
    piece_sems = pltpu.SemaphoreType.DMA((12,))
    r, m, n, g = call(
        first_kernel, [SMEM] * 3 + [ANY] * 12,
        [
            (KEPT, (TR, TILE), f32), (KEPT, (TR, TILE), f32), (KEPT, (TC, TILE), f32),
            (KEPT, (TURNS, GROUP, TILE, TILE), bf16),
        ],
        blocks + [pltpu.VMEM((TR, TILE, F), bf16)] + row_acc + [piece_sems],
        *meta, *xs, *ys,
    )
    m, n, g = in_vmem([m, n, g])
    lists = meta[0:2]

    def columns(rs):
        return call(
            column_kernel, [SMEM] * 2 + [VMEM] * 6, [(KEPT, (TC, TILE), f32)],
            column_acc, *lists, *rs, m, g,
        )[0]

    rs = in_vmem(sum_photo(r))
    cs = in_vmem(sum_spec(columns(rs)))
    (r,) = call(
        row_kernel, [SMEM] * 2 + [VMEM] * 4, [(KEPT, (TR, TILE), f32)],
        row_acc, *lists, *cs, n, g,
    )
    rs = in_vmem(sum_photo(r))
    cs = in_vmem(sum_spec(columns(rs)))
    *parts, share = call(
        grad_kernel, [SMEM] * 3 + [VMEM] * 9 + [ANY] * 12,
        [(KEPT, (4, EXT, SB), bf16)] * 4 + [(KEPT, (8, F, PB), bf16)] * 2 + [(KEPT, (4, 8, TILE), f32)],
        blocks
        + [
            pltpu.VMEM((TR, 8, TILE), f32),
            pltpu.VMEM((TC, 8, TILE), f32),
            pltpu.VMEM((TC, WROWS, TILE), bf16),
            pltpu.VMEM((TR, F, TILE), bf16),
            pltpu.VMEM((TR, WROWS, TILE), f32),
            pltpu.VMEM((TC, F, TILE), f32),
            piece_sems,
        ],
        *meta, *rs, *cs, m, n, g, *xs, *ys,
    )
    share = share[:, 0, :].reshape(1, PB)

    spec_parts, photo_parts = (parts[0:4], parts[4:6])
    far = swap_core(photo_parts[1])
    y_parts = [shift_y(spec_parts[k], -k) for k in (1, 2, 3)]
    photo_sums = [photo_parts[0][2 * k : 2 * k + 2].astype(f32) + far[2 * k : 2 * k + 2].astype(f32) for k in range(4)]
    x_parts = [total.astype(bf16) for total in photo_sums[1:]]
    x_parts = [shift_x(part, -k) for k, part in zip((1, 2, 3), x_parts)]

    spec_sum, *z_parts = call(
        relay_kernel, [VMEM] * 4, [(KEPT, (EXT, SB), f32)] + [(KEPT, (EXT, SB), bf16)] * 3, [],
        spec_parts[0], *in_vmem(y_parts),
    )
    z_parts = [move(part) for move, part in zip((flip_z, mirror_z, across_z), z_parts)]
    photo_sum = photo_sums[0]
    for part in x_parts:
        photo_sum = photo_sum + part.astype(f32)
    photo_send = photo_sum[1].astype(bf16)
    lowered = swap_low(photo_send)
    photo_sum = photo_sum[0] + lowered.astype(f32)
    grad_photo = (2.0 * (share * y_own.astype(f32) - photo_sum)).T[None]
    for part in z_parts:
        spec_sum = spec_sum + part.astype(f32)
    row_marginal = spec_sum[F : F + 1] + spec_sum[F + 1 : F + 2]
    grad_spec = (2.0 * (row_marginal * x_own.astype(f32) - spec_sum[0:F])).T
    return (grad_spec, grad_photo)


def solution(mesh):
    return jax.shard_map(
        per_device,
        mesh=mesh,
        in_specs=(
            P(("spec", "photo"), None),
            P("spec", "photo", None),
            P(("spec", "photo")),
            P("spec", "photo"),
            P("spec", "photo", None),
            P("spec", "photo"),
        ),
        out_specs=(P(("spec", "photo"), None), P("spec", "photo", None)),
        check_vma=False,
    )
```
